512 devices in a mesh: src: 128 (over y, z, core), seg: 4 (over x).
Axes of the slice: x: 4, y: 4, z: 16, core: 2. Of those that a mesh axis runs over, the one named last changes fastest.
Arguments:
- residual: float32 [8388608], P(('src', 'seg')), may hold values from -24 to 24
- obs_weight: float32 [8388608], P(('src', 'seg')), may hold values from 0.25 to 4
- time_frac: float32 [8388608], P(('src', 'seg')), may hold values from 0 to 0.99
- src_partials: float32 [5, 8388608], P(None, ('src', 'seg')), may hold values from -6 to 6
- att_dir: float32 [3, 8388608], P(None, ('src', 'seg')), may hold values from -6 to 6
- src_prior: float32 [5, 262144], P(None, 'src'), may hold values from 4 to 40
- att_prior: float32 [3, 32768], P(None, ('src', 'seg')), may hold values from 16 to 128
- obs_source: int32 [8388608], P(('src', 'seg')), may hold values from 0 to 2047, as said below
- obs_interval: int32 [8388608], P(('src', 'seg')), may hold values from 0 to 32767, as said below
- obs_count: int32 [512, 128], P(('src', 'seg')), may hold values from 16 to 128, as said below
Outputs:
- src_update: float32 [5, 262144], P(None, 'src')
- att_update: float32 [3, 32768], P(None, ('src', 'seg'))
- residual_out: float32 [8388608], P(('src', 'seg'))
The draws below stay inside these ranges and needn't reach their ends.
Inputs may be any that keep to these rules, and one draw needn't show every extreme that they name: obs_source of a slot on row r of obs_count (slot i with r = i // 16384) is the index of its source within the src block r // 4. A slot of row r in block b has an interval owned by knot block t = b * 4 + (r mod 4): obs_interval lies in t * 64 to (t + 1) * 64 - 1. `obs_count`: row r counts the live slots, from the start, of the 128 blocks of device r; for every seg index one block index is full (128) on every row of that seg index.
All inputs are finite; a program needn't handle non-finite values.
Results may differ from the reference program's by a relative error of at most 0.0003.
Values sent between devices are 32-bit elements; how exact they have to be, the bound alone decides.
No kernel may reach another device: no remote copies, remote signals or barrier semaphores. Data moves between devices by JAX's collectives and lax.ppermute only.
A program may use at most 128 MiB of HBM per device.

```python
import math
import jax
import jax.numpy as jnp
from jax import lax

SRC_DEV = 2048
OBS_DEV = 16384
KD = 64
ITERS_ATT = 6
CAP = 128
S = 262144
NK = 32768
NOBS = 8388608
N_SRC = 128
N_SEG = 4


def draw_obs_count(key, part):
    first_key, second_key = jax.random.split(jax.random.fold_in(key, 11))
    rows_total = N_SRC * N_SEG
    base_counts = jax.random.randint(first_key, (rows_total, N_SRC), CAP // 8, 3 * CAP // 4 + 1)
    busiest = jax.random.randint(second_key, (N_SEG,), 0, N_SRC)
    column_at = jnp.arange(rows_total, dtype=jnp.int32) % N_SEG
    destination_slot = jnp.take(busiest, column_at)
    full_block = jnp.arange(N_SRC, dtype=jnp.int32)[None, :] == destination_slot[:, None]
    return jnp.where(full_block, CAP, base_counts).astype(jnp.int32)


def draw_obs_source(key, part):
    picked = jax.random.randint(jax.random.fold_in(key, 23), (NOBS,), 0, SRC_DEV)
    return picked.astype(jnp.int32)


def draw_obs_interval(key, part):
    position = jnp.arange(NOBS, dtype=jnp.int32)
    seg_place = position // OBS_DEV % N_SEG
    dest_block = position % OBS_DEV // CAP
    owner = dest_block * N_SEG + seg_place
    picked = jax.random.randint(jax.random.fold_in(key, 37), (NOBS,), 0, KD)
    return (owner * KD + picked).astype(jnp.int32)


def levels(stream_key, dims, cuts, smallest, largest):
    def one(dim, shards_of):
        draws = jax.random.uniform(jax.random.fold_in(jax.random.fold_in(stream_key, 6), dim), (shards_of,), jnp.float32, smallest / len(cuts), largest / len(cuts))
        return jnp.repeat(jnp.exp(draws), dims[dim] // shards_of).reshape((-1,) + (1,) * (len(dims) - dim - 1))

    loudness = one(*cuts[0])
    for cut in cuts[1:]:
        loudness = loudness * one(*cut)
    return loudness


def normal_values(stream_key, extent, width, most, cuts=(), kind=jnp.bfloat16):
    drawn = width * jax.random.normal(stream_key, extent, jnp.float32)
    if cuts:
        drawn = drawn * levels(stream_key, extent, cuts, -0.22, 0.18)
    return jnp.clip(drawn, -most, most).astype(kind)


def setup_inputs(seed: int = 0) -> dict:
    keys = jax.random.split(jax.random.key(seed), 11)
    residual = normal_values(keys[0], (NOBS,), 4.0, 24.0, ((0, 512),), jnp.float32)
    obs_weight = jnp.clip(jnp.exp(math.log(4.0) - 2.7725887 * jax.random.uniform(keys[1], (NOBS,), jnp.float32) ** levels(keys[1], (NOBS,), ((0, 512),), -0.2, 0.2)), 0.25, 4.0)
    time_frac = jnp.clip(0.99 * jax.random.uniform(keys[2], (NOBS,), jnp.float32) ** levels(keys[2], (NOBS,), ((0, 512),), -0.2, 0.2), 0.0, 0.99)
    src_partials = normal_values(keys[3], (5, NOBS), 1.0, 6.0, ((1, 512),), jnp.float32)
    att_dir = normal_values(keys[4], (3, NOBS), 1.0, 6.0, ((1, 512),), jnp.float32)
    src_prior = jnp.clip(jnp.exp(math.log(40.0) - 2.3025851 * jax.random.uniform(keys[5], (5, S), jnp.float32) ** levels(keys[5], (5, S), ((1, 128),), -0.2, 0.2)), 4.0, 40.0)
    att_prior = jnp.clip(jnp.exp(math.log(128.0) - 2.0794415 * jax.random.uniform(keys[6], (3, NK), jnp.float32) ** levels(keys[6], (3, NK), ((1, 512),), -0.2, 0.2)), 16.0, 128.0)
    obs_source = draw_obs_source(jax.random.fold_in(keys[10], 71), 0)
    obs_interval = draw_obs_interval(jax.random.fold_in(keys[10], 71), 0)
    obs_count = draw_obs_count(jax.random.fold_in(keys[10], 71), 0)
    return {"residual": residual, "obs_weight": obs_weight, "time_frac": time_frac, "src_partials": src_partials, "att_dir": att_dir, "src_prior": src_prior, "att_prior": att_prior, "obs_source": obs_source, "obs_interval": obs_interval, "obs_count": obs_count}


param_pairs = [(0, 0), (0, 1), (0, 2), (0, 3), (0, 4), (1, 1), (1, 2), (1, 3), (1, 4), (2, 2), (2, 3), (2, 4), (3, 3), (3, 4), (4, 4)]
sym_pairs = [(0, 0), (0, 1), (0, 2), (1, 1), (1, 2), (2, 2)]
damping = 0.5

def cholesky_solve5(normal, rhs_terms, prior_diag):
    matrix = {}
    for number, pair_at in enumerate(param_pairs):
        matrix[pair_at] = normal[number]
        matrix[pair_at[1], pair_at[0]] = normal[number]
    for number in range(5):
        matrix[number, number] = matrix[number, number] + prior_diag[number]
    factor = {}
    for row_at in range(5):
        for col_at in range(row_at + 1):
            running = matrix[row_at, col_at]
            for inner_k in range(col_at):
                running = running - factor[row_at, inner_k] * factor[col_at, inner_k]
            if row_at == col_at:
                factor[row_at, row_at] = jnp.sqrt(running)
            else:
                factor[row_at, col_at] = running / factor[col_at, col_at]
    forward = []
    for row_at in range(5):
        running = rhs_terms[row_at]
        for inner_k in range(row_at):
            running = running - factor[row_at, inner_k] * forward[inner_k]
        forward.append(running / factor[row_at, row_at])
    backward = [None] * 5
    for row_at in reversed(range(5)):
        running = forward[row_at]
        for inner_k in range(row_at + 1, 5):
            running = running - factor[inner_k, row_at] * backward[inner_k]
        backward[row_at] = running / factor[row_at, row_at]
    return jnp.stack(backward)

def spline_basis(local_time):
    floor_part = jnp.floor(local_time)
    frac_part = local_time - floor_part
    square = frac_part * frac_part
    cube_term = square * frac_part
    rest = 1.0 - frac_part
    splines = [rest * rest * rest / 6.0, (3.0 * cube_term - 6.0 * square + 4.0) / 6.0, (-3.0 * cube_term + 3.0 * square + 3.0 * frac_part + 1.0) / 6.0, cube_term / 6.0]
    return (floor_part.astype(jnp.int32), splines)

def knot_term(weight, first_pass, splines, direction, spline_at, stack_axis):
    outer_terms = []
    for left_at, right_at in sym_pairs:
        outer_terms.append(weight * direction[left_at] * direction[right_at])
    rows_out = []
    for offset in range(4):
        if spline_at + offset <= 3:
            coeff_pair = splines[spline_at] * splines[spline_at + offset]
            for entry_term in outer_terms:
                rows_out.append(coeff_pair * entry_term)
        else:
            for entry_term in outer_terms:
                rows_out.append(jnp.zeros_like(entry_term))
    scaled = weight * splines[spline_at] * first_pass
    for axis_at in range(3):
        rows_out.append(scaled * direction[axis_at])
    return jnp.stack(rows_out, stack_axis)

def sym_apply(entries, vector):
    first_row = entries[0] * vector[0] + entries[1] * vector[1] + entries[2] * vector[2]
    middle_row_entries = entries[1] * vector[0] + entries[3] * vector[1] + entries[4] * vector[2]
    third_row = entries[2] * vector[0] + entries[4] * vector[1] + entries[5] * vector[2]
    return jnp.stack([first_row, middle_row_entries, third_row])

def symmetric_inverse(entries):
    cof_00 = entries[3] * entries[5] - entries[4] * entries[4]
    cof_01 = entries[2] * entries[4] - entries[1] * entries[5]
    cof_02 = entries[1] * entries[4] - entries[2] * entries[3]
    cof_11 = entries[0] * entries[5] - entries[2] * entries[2]
    cof_12 = entries[1] * entries[2] - entries[0] * entries[4]
    cof_22 = entries[0] * entries[3] - entries[1] * entries[1]
    determinant = entries[0] * cof_00 + entries[1] * cof_01 + entries[2] * cof_02
    return jnp.stack([cof_00, cof_01, cof_02, cof_11, cof_12, cof_22]) / determinant

def add_prior(diag_sums, prior_diag):
    return jnp.stack([diag_sums[0] + prior_diag[0], diag_sums[1], diag_sums[2], diag_sums[3] + prior_diag[1], diag_sums[4], diag_sums[5] + prior_diag[2]])

def apply_operator(diag_block, upper_triangle_filled, vector_padded, knot_count):
    applied = sym_apply(diag_block, vector_padded[:, 3:3 + knot_count])
    for offset in range(1, 4):
        upper_here = upper_triangle_filled[6 * (offset - 1):6 * offset, 3:3 + knot_count]
        upper_left = upper_triangle_filled[6 * (offset - 1):6 * offset, 3 - offset:3 - offset + knot_count]
        applied = applied + sym_apply(upper_here, vector_padded[:, 3 + offset:3 + offset + knot_count])
        applied = applied + sym_apply(upper_left, vector_padded[:, 3 - offset:3 - offset + knot_count])
    return applied

def table_correction(full_table, interval, splines, direction):
    padded = jnp.pad(full_table, ((0, 0), (1, 2)))
    correction = jnp.zeros(interval.shape, jnp.float32)
    for spline_at in range(4):
        looked = jnp.take(padded, interval + spline_at, axis=1)
        correction = correction + splines[spline_at] * lax.optimization_barrier(jnp.sum(direction * looked, 0))
    return correction

def reference(residual, obs_weight, time_frac, src_partials, att_dir, src_prior, att_prior, obs_source, obs_interval, obs_count):
    total_obs = residual.shape[0]
    position = jnp.arange(total_obs, dtype=jnp.int32)
    device_at = position // OBS_DEV
    block_at = position % OBS_DEV // CAP
    slot_at = position % CAP
    live_mask = (slot_at < obs_count[device_at, block_at]).astype(jnp.float32)
    weight = obs_weight * live_mask
    global_source = (device_at // N_SEG * SRC_DEV + obs_source).astype(jnp.int32)
    features = []
    for left_at, right_at in param_pairs:
        features.append(weight * src_partials[left_at] * src_partials[right_at])
    for axis_at in range(5):
        features.append(weight * src_partials[axis_at] * residual)
    src_sums = jax.ops.segment_sum(jnp.stack(features, 1), global_source, num_segments=S).T
    src_update = cholesky_solve5(src_sums[:15], src_sums[15:], src_prior)
    src_corr = lax.optimization_barrier(jnp.sum(src_partials * jnp.take(src_update, global_source, axis=1), 0))
    first_pass = residual - src_corr
    local_time = (obs_interval % KD).astype(jnp.float32) + time_frac
    floor_at, splines = spline_basis(local_time)
    knot_sums = jnp.zeros((NK + 3, 27), jnp.float32)
    for spline_at in range(4):
        term = knot_term(weight, first_pass, splines, att_dir, spline_at, 1)
        knot_sums = knot_sums + jax.ops.segment_sum(term, obs_interval + spline_at, num_segments=NK + 3)
    own_sums = knot_sums[1:NK + 1].T
    diag_block = add_prior(own_sums[:6], att_prior)
    inverse = symmetric_inverse(diag_block)
    upper_triangle_filled = jnp.pad(own_sums[6:24], ((0, 0), (3, 0)))
    att_rhs = own_sums[24:27]
    att_update = jnp.zeros((3, NK), jnp.float32)
    for sweep_at in range(ITERS_ATT):
        vector_padded = jnp.pad(att_update, ((0, 0), (3, 3)))
        att_update = att_update + damping * sym_apply(inverse, att_rhs - apply_operator(diag_block, upper_triangle_filled, vector_padded, NK))
    att_corr = table_correction(att_update, obs_interval, splines, att_dir)
    residual_out = residual - live_mask * (src_corr + att_corr)
    return (src_update, att_update, residual_out)
```

```python
import functools

import jax
import jax.numpy as jnp
from jax import lax
from jax.experimental import pallas as pl
from jax.experimental.pallas import tpu as pltpu
from jax.sharding import PartitionSpec as P

ITERS_ATT = 6
DAMPING = 0.5
LEFT = 20

param_pairs = [(i, j) for i in range(5) for j in range(i, 5)]
sym_pairs = [(0, 0), (0, 1), (0, 2), (1, 1), (1, 2), (2, 2)]
spline_pairs = [(m, m + d) for d in range(4) for m in range(4 - d)]

VMEM_SPEC = pl.BlockSpec(memory_space=pltpu.VMEM)
SMEM_SPEC = pl.BlockSpec(memory_space=pltpu.SMEM)
NT = (((1,), (1,)), ((), ()))


def split_parts(values):
    high = values.astype(jnp.bfloat16)
    low = (values - high.astype(jnp.float32)).astype(jnp.bfloat16)
    return high, low


def spline_weights(local_time):
    floor_part = jnp.floor(local_time)
    frac = local_time - floor_part
    square = frac * frac
    cube = square * frac
    rest = 1.0 - frac
    sixth = 1.0 / 6.0
    splines = [
        rest * rest * rest * sixth,
        (3.0 * cube - 6.0 * square + 4.0) * sixth,
        (-3.0 * cube + 3.0 * square + 3.0 * frac + 1.0) * sixth,
        cube * sixth,
    ]
    return floor_part.astype(jnp.int32), splines


def source_sums_kernel(count_ref, res_ref, weight_ref, part_ref, src_ref, out_ref, live_ref, a_ref, l_ref, acc_ref):
    acc_ref[...] = jnp.zeros_like(acc_ref)
    lane = lax.broadcasted_iota(jnp.int32, (1, 128), 1)
    high_id = lax.broadcasted_iota(jnp.int32, (8, 128), 0)
    low_id = lax.broadcasted_iota(jnp.int32, (256, 128), 0)

    def group(g, carry):
        first = pl.multiple_of(g * 8, 8)
        res8 = res_ref[pl.ds(first, 8), :]
        weight8 = weight_ref[pl.ds(first, 8), :]
        src8 = src_ref[pl.ds(first, 8), :]
        live_rows = []
        for k in range(8):
            at = pl.multiple_of((g * 8 + k) * 128, 128)
            live = lane < count_ref[0, g * 8 + k]
            weight = jnp.where(live, weight8[k : k + 1], 0.0)
            live_rows.append(weight)
            part = part_ref[:, pl.ds(at, 128)]
            both = jnp.concatenate([part, res8[k : k + 1]], 0)
            weighted = weight * part
            src = src8[k : k + 1]
            high_mask = jnp.broadcast_to(src >> 8, (8, 128)) == high_id
            tiles = []
            products = [jnp.broadcast_to(weighted[i : i + 1], (6, 128)) * both for i in range(5)]
            for i, j in param_pairs:
                tiles.append(products[i][j : j + 1])
            for i in range(5):
                tiles.append(products[i][5:6])
            rows = [jnp.where(high_mask, jnp.broadcast_to(t, (8, 128)), 0.0) for t in tiles]
            high, low = split_parts(jnp.concatenate(rows, 0))
            a_ref[0:160, k * 128 : (k + 1) * 128] = high
            a_ref[160:320, k * 128 : (k + 1) * 128] = low
            hot = jnp.broadcast_to(src & 255, (256, 128)) == low_id
            l_ref[:, k * 128 : (k + 1) * 128] = jnp.where(hot, 1.0, 0.0).astype(jnp.bfloat16)
        live_ref[pl.ds(first, 8), :] = jnp.concatenate(live_rows, 0)
        acc_ref[...] += lax.dot_general(a_ref[...], l_ref[...], NT, preferred_element_type=jnp.float32)
        return carry

    lax.fori_loop(0, 16, group, 0)
    for f in range(20):
        for h in range(2):
            total = acc_ref[f * 8 : f * 8 + 8, h * 128 : (h + 1) * 128] + acc_ref[160 + f * 8 : 168 + f * 8, h * 128 : (h + 1) * 128]
            for q in range(4):
                out_ref[q, (h * 20 + f) * 8 : (h * 20 + f) * 8 + 8, :] = total


def cholesky_solve5(normal, rhs_terms):
    matrix = {}
    for number, (i, j) in enumerate(param_pairs):
        matrix[i, j] = normal[number]
        matrix[j, i] = normal[number]
    factor = {}
    inverse_diag = []
    for row_at in range(5):
        for col_at in range(row_at + 1):
            running = matrix[row_at, col_at]
            for inner_k in range(col_at):
                running = running - factor[row_at, inner_k] * factor[col_at, inner_k]
            if row_at == col_at:
                factor[row_at, row_at] = jnp.sqrt(running)
                inverse_diag.append(1.0 / factor[row_at, row_at])
            else:
                factor[row_at, col_at] = running * inverse_diag[col_at]
    forward = []
    for row_at in range(5):
        running = rhs_terms[row_at]
        for inner_k in range(row_at):
            running = running - factor[row_at, inner_k] * forward[inner_k]
        forward.append(running * inverse_diag[row_at])
    backward = [None] * 5
    for row_at in reversed(range(5)):
        running = forward[row_at]
        for inner_k in range(row_at + 1, 5):
            running = running - factor[inner_k, row_at] * backward[inner_k]
        backward[row_at] = running * inverse_diag[row_at]
    return backward


def source_solve_kernel(
    sums_ref, prior_ref, res_ref, live_ref, part_ref, src_ref, frac_ref, interval_ref, dir_ref,
    update_ref, pack_ref, base_ref, scale_ref, table_ref, root_ref, corr_ref,
):
    table_ref[...] = jnp.zeros_like(table_ref)
    for h in range(2):
        terms = []
        for f in range(20):
            at = (h * 20 + f) * 8
            terms.append(
                (sums_ref[0, at : at + 8, :] + sums_ref[1, at : at + 8, :])
                + (sums_ref[2, at : at + 8, :] + sums_ref[3, at : at + 8, :])
            )
        for number, (i, j) in enumerate(param_pairs):
            if i == j:
                prior = [prior_ref[i : i + 1, (2 * r + h) * 128 : (2 * r + h + 1) * 128] for r in range(8)]
                terms[number] = terms[number] + jnp.concatenate(prior, 0)
        solved = cholesky_solve5(terms[:15], terms[15:])
        for p in range(5):
            for r in range(8):
                table_ref[p : p + 1, (2 * r + h) * 128 : (2 * r + h + 1) * 128] = solved[p][r : r + 1]
    update_ref[...] = table_ref[0:5, :]
    root_ref[...] = jnp.sqrt(live_ref[...])

    def group(g, carry):
        first = pl.multiple_of(g * 8, 8)
        res8 = res_ref[pl.ds(first, 8), :]
        src8 = src_ref[pl.ds(first, 8), :]
        root8 = root_ref[pl.ds(first, 8), :]
        time8 = (interval_ref[pl.ds(first, 8), :] & 63).astype(jnp.float32) + frac_ref[pl.ds(first, 8), :]
        low8 = src8 & 127
        high8 = src8 >> 7
        pack = pack_ref.at[pl.ds(pl.multiple_of(g * 40, 8), 40), :]
        corr_rows = []
        for k in range(8):
            at = pl.multiple_of((g * 8 + k) * 128, 128)
            low = jnp.broadcast_to(low8[k : k + 1], (8, 128))
            high = jnp.broadcast_to(high8[k : k + 1], (8, 128))
            found = jnp.zeros((8, 128), jnp.float32)
            for c in range(16):
                taken = jnp.take_along_axis(table_ref[:, c * 128 : (c + 1) * 128], low, axis=1, mode="promise_in_bounds")
                found = jnp.where(high == c, taken, found)
            corr = jnp.sum(part_ref[:, pl.ds(at, 128)] * found[0:5], 0, keepdims=True)
            corr_rows.append(corr)
            root = root8[k : k + 1]
            first_pass = root * (res8[k : k + 1] - corr)
            pack[k * 5 : k * 5 + 5, :] = jnp.concatenate([time8[k : k + 1], root * dir_ref[:, pl.ds(at, 128)], first_pass], 0)
        corr_ref[pl.ds(first, 8), :] = jnp.concatenate(corr_rows, 0)
        return carry

    lax.fori_loop(0, 16, group, 0)
    live = root_ref[...] > 0.0
    base_ref[...] = res_ref[...] - jnp.where(live, corr_ref[...], 0.0)
    scale_ref[...] = jnp.where(live, 1.0 / jnp.where(live, root_ref[...], 1.0), 0.0)


def band_sums_kernel(slots_ref, prior_ref, frame_ref, feat_ref, a_ref, o_ref, acc_ref, prior_pad):
    acc_ref[...] = jnp.zeros_like(acc_ref)
    feat_ref[...] = jnp.zeros_like(feat_ref)
    knot_id = lax.broadcasted_iota(jnp.int32, (64, 128), 0)

    def group(g, carry):
        first = pl.multiple_of(g * 40, 8)
        slots = slots_ref.at[pl.ds(first, 40), :]
        time8, d0, d1, d2, fp = [slots[pl.ds(k, 8, stride=5), :] for k in range(5)]
        direction = [d0, d1, d2]
        floor8, splines = spline_weights(time8)
        for number, (m, n) in enumerate(spline_pairs):
            feat_ref[number * 8 : number * 8 + 8, :] = splines[m] * splines[n]
        for m in range(4):
            feat_ref[80 + m * 8 : 88 + m * 8, :] = splines[m]
        for number, (i, j) in enumerate(sym_pairs):
            feat_ref[112 + number * 8 : 120 + number * 8, :] = direction[i] * direction[j]
        for i in range(3):
            feat_ref[176 + i * 8 : 184 + i * 8, :] = direction[i] * fp
        for k in range(8):
            outer = feat_ref[pl.ds(112 + k, 8, stride=8), :]
            right = feat_ref[pl.ds(176 + k, 8, stride=8), :]
            rows = []
            for c in range(14):
                coeff = jnp.broadcast_to(feat_ref[c * 8 + k : c * 8 + k + 1, :], (8, 128))
                rows.append(coeff * (outer if c < 10 else right))
            high, low = split_parts(jnp.concatenate(rows, 0))
            a_ref[0:112, k * 128 : (k + 1) * 128] = high
            a_ref[112:224, k * 128 : (k + 1) * 128] = low
            hot = jnp.broadcast_to(floor8[k : k + 1], (64, 128)) == knot_id
            o_ref[:, k * 128 : (k + 1) * 128] = jnp.where(hot, 1.0, 0.0).astype(jnp.bfloat16)
        acc_ref[:, 0:64] += lax.dot_general(a_ref[...], o_ref[...], NT, preferred_element_type=jnp.float32)
        return carry

    lax.fori_loop(0, 16, group, 0)
    prior_pad[...] = jnp.zeros_like(prior_pad)
    prior_pad[3:6, 0:64] = prior_ref[...]

    def tile(c, shift):
        return pltpu.roll(acc_ref[c * 8 : c * 8 + 8, :] + acc_ref[112 + c * 8 : 120 + c * 8, :], shift, 1)

    for d in range(4):
        total = None
        for number, (m, n) in enumerate(spline_pairs):
            if n - m == d:
                term = tile(number, LEFT - 1 + m)
                total = term if total is None else total + term
        frame_ref[d * 8 : d * 8 + 8, :] = total
    total = pltpu.roll(prior_pad[...], LEFT, 1)
    for m in range(4):
        total = total + tile(10 + m, LEFT - 1 + m)
    frame_ref[32:40, :] = total


def sym_columns(e):
    pad = [jnp.zeros((5, 128), jnp.float32)]
    return [
        jnp.concatenate([e[0], e[1], e[2]] + pad, 0),
        jnp.concatenate([e[1], e[3], e[4]] + pad, 0),
        jnp.concatenate([e[2], e[4], e[5]] + pad, 0),
    ]


def columns_apply(columns, vector):
    total = None
    for j in range(3):
        term = columns[j] * jnp.broadcast_to(vector[j : j + 1], (8, 128))
        total = term if total is None else total + term
    return total


def attitude_kernel(place_ref, own_ref, even_ref, odd_ref, slots_ref, att_ref, corr_ref, *, knots_total):
    place = place_ref[0]
    lane = lax.broadcasted_iota(jnp.int32, (1, 128), 1)
    lane8 = lax.broadcasted_iota(jnp.int32, (8, 128), 1)
    is_even = place % 2 == 0
    knot = place * 64 + lane - LEFT
    valid = (knot >= 0) & (knot < knots_total)

    def frame(row):
        swap_first = even_ref[row : row + 8, :]
        swap_next = odd_ref[row : row + 8, :]
        left = jnp.where(is_even, swap_next, swap_first)
        right = jnp.where(is_even, swap_first, swap_next)
        return own_ref[row : row + 8, :] + pltpu.roll(jnp.where(lane8 < 64, right, left), 64, 1)

    uppers = [frame(8 * d) for d in range(4)]
    last = frame(32)
    e = [uppers[0][n : n + 1] for n in range(6)]
    e[0] = e[0] + last[3:4]
    e[3] = e[3] + last[4:5]
    e[5] = e[5] + last[5:6]
    c00 = e[3] * e[5] - e[4] * e[4]
    c01 = e[2] * e[4] - e[1] * e[5]
    c02 = e[1] * e[4] - e[2] * e[3]
    c11 = e[0] * e[5] - e[2] * e[2]
    c12 = e[1] * e[2] - e[0] * e[4]
    c22 = e[0] * e[3] - e[1] * e[1]
    determinant = e[0] * c00 + e[1] * c01 + e[2] * c02
    scale = jnp.where(valid, DAMPING / jnp.where(valid, determinant, 1.0), 0.0)
    inverse = sym_columns([c * scale for c in (c00, c01, c02, c11, c12, c22)])
    diag = sym_columns(e)
    upper_cols = [sym_columns([u[n : n + 1] for n in range(6)]) for u in uppers[1:]]
    rhs = last
    att = columns_apply(inverse, rhs)
    for _ in range(1, ITERS_ATT):
        applied = columns_apply(diag, att)
        for d in range(1, 4):
            applied = applied + columns_apply(upper_cols[d - 1], pltpu.roll(att, 128 - d, 1))
            applied = applied + pltpu.roll(columns_apply(upper_cols[d - 1], att), d, 1)
        att = att + columns_apply(inverse, rhs - applied)
    att_ref[...] = pltpu.roll(att, 128 - LEFT, 1)[0:3, 0:64]
    tables = [jnp.broadcast_to(att[j : j + 1], (8, 128)) for j in range(3)]

    def group(g, carry):
        slots = slots_ref.at[pl.ds(pl.multiple_of(g * 40, 8), 40), :]
        time8, d0, d1, d2 = [slots[pl.ds(k, 8, stride=5), :] for k in range(4)]
        direction = [d0, d1, d2]
        floor8, splines = spline_weights(time8)
        total = jnp.zeros((8, 128), jnp.float32)
        for m in range(4):
            at = floor8 + (LEFT - 1 + m)
            part = None
            for j in range(3):
                term = direction[j] * jnp.take_along_axis(tables[j], at, axis=1, mode="promise_in_bounds")
                part = term if part is None else part + term
            total = total + splines[m] * part
        corr_ref[pl.ds(pl.multiple_of(g * 8, 8), 8), :] = total
        return carry

    lax.fori_loop(0, 16, group, 0, unroll=4)


def call(kernel, outs, n_in, smem_at=(), scratch=(), name=None):
    shapes = [jax.ShapeDtypeStruct(s, jnp.float32) for s in outs]
    return pl.pallas_call(
        kernel,
        out_shape=shapes,
        in_specs=[SMEM_SPEC if i in smem_at else VMEM_SPEC for i in range(n_in)],
        out_specs=[VMEM_SPEC] * len(shapes),
        scratch_shapes=list(scratch),
        name=name,
    )


def body(residual, obs_weight, time_frac, src_partials, att_dir, src_prior, att_prior, obs_source, obs_interval, obs_count):
    devices = lax.axis_size("src") * lax.axis_size("seg")
    square = lambda a: a.reshape(128, 128)
    res, weight, frac, src, interval = map(square, (residual, obs_weight, time_frac, obs_source, obs_interval))
    sums, live = call(
        source_sums_kernel,
        [(4, 320, 128), (128, 128)],
        5,
        (0,),
        [pltpu.VMEM((320, 1024), jnp.bfloat16), pltpu.VMEM((256, 1024), jnp.bfloat16), pltpu.VMEM((320, 256), jnp.float32)],
        "source_sums",
    )(obs_count, res, weight, src_partials, src)
    gathered = lax.all_to_all(sums, "seg", split_axis=0, concat_axis=0, tiled=True)
    src_update, packed, base, scale = call(
        source_solve_kernel,
        [(5, 2048), (640, 128), (128, 128), (128, 128)],
        9,
        (),
        [pltpu.VMEM((8, 2048), jnp.float32), pltpu.VMEM((128, 128), jnp.float32), pltpu.VMEM((128, 128), jnp.float32)],
        "source_solve",
    )(gathered, src_prior, res, live, src_partials, src, frac, interval, att_dir)
    arrived = lax.all_to_all(packed.reshape(128, 1, 640), "src", split_axis=0, concat_axis=0, tiled=True).reshape(640, 128)
    (frame,) = call(
        band_sums_kernel,
        [(40, 128)],
        2,
        (),
        [
            pltpu.VMEM((240, 128), jnp.float32),
            pltpu.VMEM((224, 1024), jnp.bfloat16),
            pltpu.VMEM((64, 1024), jnp.bfloat16),
            pltpu.VMEM((224, 128), jnp.float32),
            pltpu.VMEM((8, 128), jnp.float32),
        ],
        "band_sums",
    )(arrived, att_prior)
    both = ("src", "seg")
    swaps = []
    for start in (0, 1):
        pairs = [(i, i + 1) for i in range(start, devices - 1, 2)]
        swaps.append(lax.ppermute(frame, both, pairs + [(b, a) for a, b in pairs]))
    place = lax.axis_index(both).astype(jnp.int32).reshape(1)
    att_update, correction = call(
        functools.partial(attitude_kernel, knots_total=devices * 64),
        [(3, 64), (128, 128)],
        5,
        (0,),
        (),
        "attitude",
    )(place, frame, swaps[0], swaps[1], arrived)
    returned = lax.all_to_all(correction.reshape(128, 1, 128), "src", split_axis=0, concat_axis=0, tiled=True)
    residual_out = base - scale * returned.reshape(128, 128)
    return src_update, att_update, residual_out.reshape(-1)


def solution(mesh):
    pair = ("src", "seg")
    in_specs = (
        P(pair), P(pair), P(pair), P(None, pair), P(None, pair), P(None, "src"), P(None, pair), P(pair), P(pair), P(pair, None),
    )
    out_specs = (P(None, "src"), P(None, pair), P(pair))
    return jax.shard_map(body, mesh=mesh, in_specs=in_specs, out_specs=out_specs, check_vma=False)
```

```python
import functools

import jax
import jax.numpy as jnp
from jax import lax
from jax.experimental import pallas as pl
from jax.experimental.pallas import tpu as pltpu
from jax.sharding import PartitionSpec as P

ITERS_ATT = 6
DAMPING = 0.5
LEFT = 20

param_pairs = [(i, j) for i in range(5) for j in range(i, 5)]
sym_pairs = [(0, 0), (0, 1), (0, 2), (1, 1), (1, 2), (2, 2)]
spline_pairs = [(m, m + d) for d in range(4) for m in range(4 - d)]

VMEM_SPEC = pl.BlockSpec(memory_space=pltpu.VMEM)
SMEM_SPEC = pl.BlockSpec(memory_space=pltpu.SMEM)
NT = (((1,), (1,)), ((), ()))
SUMS_UNROLL = 4
BAND_UNROLL = 4


def split_parts(values):
    high = values.astype(jnp.bfloat16)
    low = (values - high.astype(jnp.float32)).astype(jnp.bfloat16)
    return high, low


def spline_weights(local_time):
    floor_part = jnp.floor(local_time)
    frac = local_time - floor_part
    square = frac * frac
    cube = square * frac
    rest = 1.0 - frac
    sixth = 1.0 / 6.0
    splines = [
        rest * rest * rest * sixth,
        (3.0 * cube - 6.0 * square + 4.0) * sixth,
        (-3.0 * cube + 3.0 * square + 3.0 * frac + 1.0) * sixth,
        cube * sixth,
    ]
    return floor_part.astype(jnp.int32), splines


def side_by_side(ref):
    return jnp.concatenate([ref[k] for k in range(8)], 1)


def hot_rows(ids, row):
    wide = jnp.broadcast_to(row, (16, 128)).astype(jnp.bfloat16)
    one, zero = jnp.ones((16, 128), jnp.bfloat16), jnp.zeros((16, 128), jnp.bfloat16)
    count = ids.shape[0] // 16
    return jnp.concatenate([jnp.where(ids[16 * n : 16 * n + 16] == wide, one, zero) for n in range(count)], 0)


def source_sums_kernel(
    count_ref, res_ref, weight_ref, part_ref, src_ref, out_ref, live_ref, acc_ref, rows_refs, feat_refs
):
    acc_ref[...] = jnp.zeros_like(acc_ref)
    ids = lax.broadcasted_iota(jnp.int32, (256, 128), 0).astype(jnp.float32).astype(jnp.bfloat16)
    lane8 = lax.broadcasted_iota(jnp.int32, (8, 128), 1)
    sub8 = lax.broadcasted_iota(jnp.int32, (8, 128), 0)
    sub16 = lax.broadcasted_iota(jnp.int32, (16, 128), 0)
    zero = jnp.zeros((16, 128), jnp.bfloat16)

    def group(g, feat_ref, rows_ref):
        first = pl.multiple_of(g * 8, 8)
        res8 = res_ref[pl.ds(first, 8), :]
        src8 = src_ref[pl.ds(first, 8), :]
        low8 = (src8 & 255).astype(jnp.float32)
        high8 = (src8 >> 8).astype(jnp.float32)
        count8 = jnp.zeros((8, 128), jnp.int32)
        for k in range(8):
            count8 = jnp.where(sub8 == k, count_ref[0, g * 8 + k], count8)
            rows_ref[pl.ds(k, 5, stride=8), :] = part_ref[:, pl.ds(pl.multiple_of((g * 8 + k) * 128, 128), 128)]
        weight8 = jnp.where(lane8 < count8, weight_ref[pl.ds(first, 8), :], 0.0)
        live_ref[pl.ds(first, 8), :] = weight8
        part8 = [rows_ref[p * 8 : p * 8 + 8, :] for p in range(5)]
        weighted = [weight8 * p for p in part8]
        features = [weighted[i] * part8[j] for i, j in param_pairs] + [weighted[i] * res8 for i in range(5)]
        for f, feature in enumerate(features):
            high = feature.astype(jnp.bfloat16).astype(jnp.float32)
            feat_ref[f * 8 : f * 8 + 8, :] = high
            feat_ref[160 + f * 8 : 168 + f * 8, :] = feature - high
        hots = []
        blocks = []
        for k in range(8):
            body = [feat_ref[pl.ds(128 * n + k, 16, stride=8), :].astype(jnp.bfloat16) for n in range(2)]
            tail = feat_ref[pl.ds(256 + k, 8, stride=8), :]
            tail = jnp.concatenate([tail, tail], 0).astype(jnp.bfloat16)
            high = jnp.broadcast_to(high8[k : k + 1], (16, 128)).astype(jnp.bfloat16)
            tiles = []
            for pair in range(4):
                for e in range(2):
                    mask = high == jnp.bfloat16(2 * pair + e)
                    tiles.append(jnp.where(mask, body[0], zero))
                    tiles.append(jnp.where(mask, body[1], zero))
                mixed = jnp.where(sub16 < 8, 2.0 * pair, 2.0 * pair + 1.0).astype(jnp.bfloat16)
                tiles.append(jnp.where(high == mixed, tail, zero))
            blocks.append(jnp.concatenate(tiles, 0))
            hots.append(hot_rows(ids, low8[k : k + 1]))
        sums = lax.dot_general(jnp.concatenate(blocks, 1), jnp.concatenate(hots, 1), NT, preferred_element_type=jnp.float32)
        for h in range(2):
            acc_ref[h] += sums[:, h * 128 : (h + 1) * 128]

    def groups(step, carry):
        for n in range(SUMS_UNROLL):
            group(step * SUMS_UNROLL + n, feat_refs.at[n], rows_refs.at[n])
        return carry

    lax.fori_loop(0, 16 // SUMS_UNROLL, groups, 0)

    def rows_of(q, e, h):
        at = 32 * e + q if q < 32 else 64 + 8 * e + q - 32
        return acc_ref[h, pl.ds(at, 4, stride=80), :]

    for f in range(20):
        for h in range(2):
            total = jnp.concatenate([rows_of(f, e, h) + rows_of(20 + f, e, h) for e in range(2)], 0)
            for q in range(4):
                out_ref[q, (h * 20 + f) * 8 : (h * 20 + f) * 8 + 8, :] = total


HIGH_ORDER = (0, 2, 4, 6, 1, 3, 5, 7)


def cholesky_solve5(normal, rhs_terms):
    matrix = {}
    for number, (i, j) in enumerate(param_pairs):
        matrix[i, j] = normal[number]
        matrix[j, i] = normal[number]
    factor = {}
    inverse_diag = []
    for row_at in range(5):
        for col_at in range(row_at + 1):
            running = matrix[row_at, col_at]
            for inner_k in range(col_at):
                running = running - factor[row_at, inner_k] * factor[col_at, inner_k]
            if row_at == col_at:
                factor[row_at, row_at] = jnp.sqrt(running)
                inverse_diag.append(1.0 / factor[row_at, row_at])
            else:
                factor[row_at, col_at] = running * inverse_diag[col_at]
    forward = []
    for row_at in range(5):
        running = rhs_terms[row_at]
        for inner_k in range(row_at):
            running = running - factor[row_at, inner_k] * forward[inner_k]
        forward.append(running * inverse_diag[row_at])
    backward = [None] * 5
    for row_at in reversed(range(5)):
        running = forward[row_at]
        for inner_k in range(row_at + 1, 5):
            running = running - factor[inner_k, row_at] * backward[inner_k]
        backward[row_at] = running * inverse_diag[row_at]
    return backward


def source_solve_kernel(
    sums_ref, prior_ref, res_ref, live_ref, part_ref, src_ref, frac_ref, interval_ref, dir_ref,
    update_ref, pack_ref, base_ref, scale_ref, table_ref, root_ref, corr_ref,
):
    table_ref[...] = jnp.zeros_like(table_ref)
    for h in range(2):
        terms = []
        for f in range(20):
            at = (h * 20 + f) * 8
            terms.append(
                (sums_ref[0, at : at + 8, :] + sums_ref[1, at : at + 8, :])
                + (sums_ref[2, at : at + 8, :] + sums_ref[3, at : at + 8, :])
            )
        for number, (i, j) in enumerate(param_pairs):
            if i == j:
                prior = [prior_ref[i : i + 1, (2 * r + h) * 128 : (2 * r + h + 1) * 128] for r in HIGH_ORDER]
                terms[number] = terms[number] + jnp.concatenate(prior, 0)
        solved = cholesky_solve5(terms[:15], terms[15:])
        for p in range(5):
            for n, r in enumerate(HIGH_ORDER):
                table_ref[p : p + 1, (2 * r + h) * 128 : (2 * r + h + 1) * 128] = solved[p][n : n + 1]
    update_ref[...] = table_ref[0:5, :]
    root_ref[...] = jnp.sqrt(live_ref[...])

    def group(g, carry):
        first = pl.multiple_of(g * 8, 8)
        res8 = res_ref[pl.ds(first, 8), :]
        src8 = src_ref[pl.ds(first, 8), :]
        root8 = root_ref[pl.ds(first, 8), :]
        time8 = (interval_ref[pl.ds(first, 8), :] & 63).astype(jnp.float32) + frac_ref[pl.ds(first, 8), :]
        low8 = src8 & 127
        high8 = src8 >> 7
        pack = pack_ref.at[pl.ds(pl.multiple_of(g * 40, 8), 40), :]
        corr_rows = []
        for k in range(8):
            at = pl.multiple_of((g * 8 + k) * 128, 128)
            low = jnp.broadcast_to(low8[k : k + 1], (8, 128))
            high = jnp.broadcast_to(high8[k : k + 1], (8, 128))
            found = jnp.zeros((8, 128), jnp.float32)
            for c in range(16):
                taken = jnp.take_along_axis(table_ref[:, c * 128 : (c + 1) * 128], low, axis=1, mode="promise_in_bounds")
                found = jnp.where(high == c, taken, found)
            corr = jnp.sum(part_ref[:, pl.ds(at, 128)] * found[0:5], 0, keepdims=True)
            corr_rows.append(corr)
            root = root8[k : k + 1]
            first_pass = root * (res8[k : k + 1] - corr)
            pack[k * 5 : k * 5 + 5, :] = jnp.concatenate([time8[k : k + 1], root * dir_ref[:, pl.ds(at, 128)], first_pass], 0)
        corr_ref[pl.ds(first, 8), :] = jnp.concatenate(corr_rows, 0)
        return carry

    lax.fori_loop(0, 16, group, 0)
    live = root_ref[...] > 0.0
    base_ref[...] = res_ref[...] - jnp.where(live, corr_ref[...], 0.0)
    scale_ref[...] = jnp.where(live, 1.0 / jnp.where(live, root_ref[...], 1.0), 0.0)


def band_sums_kernel(slots_ref, prior_ref, frame_ref, feat_refs, a_refs, acc_ref, prior_pad):
    acc_ref[...] = jnp.zeros_like(acc_ref)
    ids = lax.broadcasted_iota(jnp.int32, (64, 128), 0).astype(jnp.float32).astype(jnp.bfloat16)

    def group(g, a_ref, feat_ref):
        slots = slots_ref.at[pl.ds(pl.multiple_of(g * 40, 8), 40), :]
        time8, d0, d1, d2, fp = [slots[pl.ds(k, 8, stride=5), :] for k in range(5)]
        direction = [d0, d1, d2]
        floor8 = jnp.floor(time8)
        _, splines = spline_weights(time8)
        outer = [direction[i] * direction[j] for i, j in sym_pairs]
        right = [direction[i] * fp for i in range(3)]
        at = 0
        for m, n in spline_pairs:
            coeff = splines[m] * splines[n]
            for entry in outer:
                feat_ref[at : at + 8, :] = coeff * entry
                at += 8
        for m in range(4):
            for entry in right:
                feat_ref[at : at + 8, :] = splines[m] * entry
                at += 8
        hots = []
        for k in range(8):
            for n in range(5):
                size = 16 if n < 4 else 8
                rows = feat_ref[pl.ds(128 * n + k, size, stride=8), :]
                high = rows.astype(jnp.bfloat16)
                rest = rows - high.astype(jnp.float32)
                if n < 4:
                    a_ref[k, 16 * n : 16 * n + 16, :] = high
                    a_ref[k, 64 + 16 * n : 80 + 16 * n, :] = rest.astype(jnp.bfloat16)
                else:
                    a_ref[k, 128:144, :] = jnp.concatenate([high.astype(jnp.float32), rest], 0).astype(jnp.bfloat16)
            hots.append(hot_rows(ids, floor8[k : k + 1]))
        acc_ref[:, 0:64] += lax.dot_general(side_by_side(a_ref), jnp.concatenate(hots, 1), NT, preferred_element_type=jnp.float32)

    def groups(step, carry):
        for n in range(BAND_UNROLL):
            group(step * BAND_UNROLL + n, a_refs.at[n], feat_refs.at[n])
        return carry

    lax.fori_loop(0, 16 // BAND_UNROLL, groups, 0)
    prior_pad[...] = jnp.zeros_like(prior_pad)
    prior_pad[3:6, 0:64] = prior_ref[...]
    sums = jnp.concatenate([acc_ref[0:64, :] + acc_ref[64:128, :], acc_ref[128:136, :] + acc_ref[136:144, :]], 0)

    def tile(first, count, shift):
        rows = sums[first : first + count]
        return pltpu.roll(jnp.concatenate([rows, jnp.zeros((8 - count, 128), jnp.float32)], 0), shift, 1)

    for d in range(4):
        total = None
        for number, (m, n) in enumerate(spline_pairs):
            if n - m == d:
                term = tile(6 * number, 6, LEFT - 1 + m)
                total = term if total is None else total + term
        frame_ref[d * 8 : d * 8 + 8, :] = total
    total = pltpu.roll(prior_pad[...], LEFT, 1)
    for m in range(4):
        total = total + tile(60 + 3 * m, 3, LEFT - 1 + m)
    frame_ref[32:40, :] = total


def sym_columns(e):
    pad = [jnp.zeros((5, 128), jnp.float32)]
    return [
        jnp.concatenate([e[0], e[1], e[2]] + pad, 0),
        jnp.concatenate([e[1], e[3], e[4]] + pad, 0),
        jnp.concatenate([e[2], e[4], e[5]] + pad, 0),
    ]


def columns_apply(columns, vector):
    total = None
    for j in range(3):
        term = columns[j] * jnp.broadcast_to(vector[j : j + 1], (8, 128))
        total = term if total is None else total + term
    return total


def attitude_kernel(place_ref, own_ref, even_ref, odd_ref, slots_ref, att_ref, corr_ref, *, knots_total):
    place = place_ref[0]
    lane = lax.broadcasted_iota(jnp.int32, (1, 128), 1)
    lane8 = lax.broadcasted_iota(jnp.int32, (8, 128), 1)
    is_even = place % 2 == 0
    knot = place * 64 + lane - LEFT
    valid = (knot >= 0) & (knot < knots_total)

    def frame(row):
        swap_first = even_ref[row : row + 8, :]
        swap_next = odd_ref[row : row + 8, :]
        left = jnp.where(is_even, swap_next, swap_first)
        right = jnp.where(is_even, swap_first, swap_next)
        return own_ref[row : row + 8, :] + pltpu.roll(jnp.where(lane8 < 64, right, left), 64, 1)

    uppers = [frame(8 * d) for d in range(4)]
    last = frame(32)
    e = [uppers[0][n : n + 1] for n in range(6)]
    e[0] = e[0] + last[3:4]
    e[3] = e[3] + last[4:5]
    e[5] = e[5] + last[5:6]
    c00 = e[3] * e[5] - e[4] * e[4]
    c01 = e[2] * e[4] - e[1] * e[5]
    c02 = e[1] * e[4] - e[2] * e[3]
    c11 = e[0] * e[5] - e[2] * e[2]
    c12 = e[1] * e[2] - e[0] * e[4]
    c22 = e[0] * e[3] - e[1] * e[1]
    determinant = e[0] * c00 + e[1] * c01 + e[2] * c02
    scale = jnp.where(valid, DAMPING / jnp.where(valid, determinant, 1.0), 0.0)
    inverse = sym_columns([c * scale for c in (c00, c01, c02, c11, c12, c22)])
    diag = sym_columns(e)
    upper_cols = [sym_columns([u[n : n + 1] for n in range(6)]) for u in uppers[1:]]
    rhs = last
    att = columns_apply(inverse, rhs)
    for _ in range(1, ITERS_ATT):
        applied = columns_apply(diag, att)
        for d in range(1, 4):
            applied = applied + columns_apply(upper_cols[d - 1], pltpu.roll(att, 128 - d, 1))
            applied = applied + pltpu.roll(columns_apply(upper_cols[d - 1], att), d, 1)
        att = att + columns_apply(inverse, rhs - applied)
    att_ref[...] = pltpu.roll(att, 128 - LEFT, 1)[0:3, 0:64]
    tables = [jnp.broadcast_to(att[j : j + 1], (8, 128)) for j in range(3)]

    def group(g, carry):
        slots = slots_ref.at[pl.ds(pl.multiple_of(g * 40, 8), 40), :]
        time8, d0, d1, d2 = [slots[pl.ds(k, 8, stride=5), :] for k in range(4)]
        direction = [d0, d1, d2]
        floor8, splines = spline_weights(time8)
        total = jnp.zeros((8, 128), jnp.float32)
        for m in range(4):
            at = floor8 + (LEFT - 1 + m)
            part = None
            for j in range(3):
                term = direction[j] * jnp.take_along_axis(tables[j], at, axis=1, mode="promise_in_bounds")
                part = term if part is None else part + term
            total = total + splines[m] * part
        corr_ref[pl.ds(pl.multiple_of(g * 8, 8), 8), :] = total
        return carry

    lax.fori_loop(0, 16, group, 0, unroll=4)


def call(kernel, outs, n_in, smem_at=(), scratch=(), name=None, far_out=(), far_in=()):
    shapes = [jax.ShapeDtypeStruct(s, jnp.float32) if i in far_out else pltpu.VMEM(s, jnp.float32) for i, s in enumerate(outs)]
    run = pl.pallas_call(
        kernel,
        out_shape=shapes,
        in_specs=[SMEM_SPEC if i in smem_at else VMEM_SPEC for i in range(n_in)],
        out_specs=[VMEM_SPEC] * len(shapes),
        scratch_shapes=list(scratch),
        name=name,
    )

    def on_chip(*args):
        near = [a if i in smem_at or i in far_in else pltpu.with_memory_space_constraint(a, pltpu.VMEM) for i, a in enumerate(args)]
        return run(*near)

    return on_chip


def body(residual, obs_weight, time_frac, src_partials, att_dir, src_prior, att_prior, obs_source, obs_interval, obs_count):
    devices = lax.axis_size("src") * lax.axis_size("seg")
    square = lambda a: a.reshape(128, 128)
    res, weight, frac, src, interval = map(square, (residual, obs_weight, time_frac, obs_source, obs_interval))
    sums, live = call(
        source_sums_kernel,
        [(4, 320, 128), (128, 128)],
        5,
        (0,),
        [
            pltpu.VMEM((2, 320, 128), jnp.float32),
            pltpu.VMEM((SUMS_UNROLL, 40, 128), jnp.float32),
            pltpu.VMEM((SUMS_UNROLL, 320, 128), jnp.float32),
        ],
        "source_sums",
        (),
        range(5),
    )(obs_count, res, weight, src_partials, src)
    gathered = lax.all_to_all(sums, "seg", split_axis=0, concat_axis=0, tiled=True)
    src_update, packed, base, scale = call(
        source_solve_kernel,
        [(5, 2048), (640, 128), (128, 128), (128, 128)],
        9,
        (),
        [pltpu.VMEM((8, 2048), jnp.float32), pltpu.VMEM((128, 128), jnp.float32), pltpu.VMEM((128, 128), jnp.float32)],
        "source_solve",
        (0,),
    )(gathered, src_prior, res, live, src_partials, src, frac, interval, att_dir)
    arrived = lax.all_to_all(packed.reshape(128, 1, 640), "src", split_axis=0, concat_axis=0, tiled=True).reshape(640, 128)
    (frame,) = call(
        band_sums_kernel,
        [(40, 128)],
        2,
        (),
        [
            pltpu.VMEM((BAND_UNROLL, 576, 128), jnp.float32),
            pltpu.VMEM((BAND_UNROLL, 8, 144, 128), jnp.bfloat16),
            pltpu.VMEM((144, 128), jnp.float32),
            pltpu.VMEM((8, 128), jnp.float32),
        ],
        "band_sums",
    )(arrived, att_prior)
    both = ("src", "seg")
    swaps = []
    for start in (0, 1):
        pairs = [(i, i + 1) for i in range(start, devices - 1, 2)]
        swaps.append(lax.ppermute(frame, both, pairs + [(b, a) for a, b in pairs]))
    place = lax.axis_index(both).astype(jnp.int32).reshape(1)
    att_update, correction = call(
        functools.partial(attitude_kernel, knots_total=devices * 64),
        [(3, 64), (128, 128)],
        5,
        (0,),
        (),
        "attitude",
        (0,),
    )(place, frame, swaps[0], swaps[1], arrived)
    returned = lax.all_to_all(correction.reshape(128, 1, 128), "src", split_axis=0, concat_axis=0, tiled=True)
    residual_out = base - scale * returned.reshape(128, 128)
    return src_update, att_update, residual_out.reshape(-1)


def solution(mesh):
    pair = ("src", "seg")
    in_specs = (
        P(pair), P(pair), P(pair), P(None, pair), P(None, pair), P(None, "src"), P(None, pair), P(pair), P(pair), P(pair, None),
    )
    out_specs = (P(None, "src"), P(None, pair), P(pair))
    return jax.shard_map(body, mesh=mesh, in_specs=in_specs, out_specs=out_specs, check_vma=False)
```

```python
import functools

import jax
import jax.numpy as jnp
from jax import lax
from jax.experimental import pallas as pl
from jax.experimental.pallas import tpu as pltpu
from jax.sharding import PartitionSpec as P


ITERS_ATT = 6
DAMPING = 0.5
LEFT = 20

param_pairs = [(i, j) for i in range(5) for j in range(i, 5)]
sym_pairs = [(0, 0), (0, 1), (0, 2), (1, 1), (1, 2), (2, 2)]
spline_pairs = [(m, m + d) for d in range(4) for m in range(4 - d)]

VMEM_SPEC = pl.BlockSpec(memory_space=pltpu.VMEM)
SMEM_SPEC = pl.BlockSpec(memory_space=pltpu.SMEM)
ANY_SPEC = pl.BlockSpec(memory_space=pl.ANY)
NT = (((1,), (1,)), ((), ()))
SUMS_UNROLL = 4
BAND_UNROLL = 4


def spline_weights(local_time):
    floor_part = jnp.floor(local_time)
    frac = local_time - floor_part
    square = frac * frac
    cube = square * frac
    rest = 1.0 - frac
    sixth = 1.0 / 6.0
    splines = [
        rest * rest * rest * sixth,
        (3.0 * cube - 6.0 * square + 4.0) * sixth,
        (-3.0 * cube + 3.0 * square + 3.0 * frac + 1.0) * sixth,
        cube * sixth,
    ]
    return floor_part.astype(jnp.int32), splines


def side_by_side(ref):
    return jnp.concatenate([ref[k] for k in range(8)], 1)


def hot_rows(ids, row):
    wide = jnp.broadcast_to(row, (16, 128)).astype(jnp.bfloat16)
    one, zero = jnp.ones((16, 128), jnp.bfloat16), jnp.zeros((16, 128), jnp.bfloat16)
    count = ids.shape[0] // 16
    return jnp.concatenate([jnp.where(ids[16 * n : 16 * n + 16] == wide, one, zero) for n in range(count)], 0)


def source_sums_kernel(
    count_ref, res_far, weight_far, part_far, src_far, out_ref, live_ref,
    acc_ref, rows_refs, feat_refs, res_ref, weight_ref, part_ref, src_ref, sems,
):
    chunks = 16 // SUMS_UNROLL

    def copies(n):
        rows = pl.ds(pl.multiple_of(n * (8 * SUMS_UNROLL), 8 * SUMS_UNROLL), 8 * SUMS_UNROLL)
        cols = pl.ds(pl.multiple_of(n * (1024 * SUMS_UNROLL), 1024 * SUMS_UNROLL), 1024 * SUMS_UNROLL)
        return [
            pltpu.make_async_copy(part_far.at[:, cols], part_ref.at[:, cols], sems.at[n, 0]),
            pltpu.make_async_copy(src_far.at[rows, :], src_ref.at[rows, :], sems.at[n, 1]),
            pltpu.make_async_copy(weight_far.at[rows, :], weight_ref.at[rows, :], sems.at[n, 2]),
            pltpu.make_async_copy(res_far.at[rows, :], res_ref.at[rows, :], sems.at[n, 3]),
        ]

    for n in range(chunks):
        for copy in copies(n):
            copy.start()
    acc_ref[...] = jnp.zeros_like(acc_ref)
    ids = lax.broadcasted_iota(jnp.int32, (256, 128), 0).astype(jnp.float32).astype(jnp.bfloat16)
    lane8 = lax.broadcasted_iota(jnp.int32, (8, 128), 1)
    sub8 = lax.broadcasted_iota(jnp.int32, (8, 128), 0)
    sub16 = lax.broadcasted_iota(jnp.int32, (16, 128), 0)
    zero = jnp.zeros((16, 128), jnp.bfloat16)

    def group(g, feat_ref, rows_ref):
        first = pl.multiple_of(g * 8, 8)
        res8 = res_ref[pl.ds(first, 8), :]
        src8 = src_ref[pl.ds(first, 8), :]
        low8 = (src8 & 255).astype(jnp.float32)
        high8 = (src8 >> 8).astype(jnp.float32)
        count8 = jnp.zeros((8, 128), jnp.int32)
        for k in range(8):
            count8 = jnp.where(sub8 == k, count_ref[0, g * 8 + k], count8)
            rows_ref[pl.ds(k, 5, stride=8), :] = part_ref[:, pl.ds(pl.multiple_of((g * 8 + k) * 128, 128), 128)]
        weight8 = jnp.where(lane8 < count8, weight_ref[pl.ds(first, 8), :], 0.0)
        live_ref[pl.ds(first, 8), :] = weight8
        part8 = [rows_ref[p * 8 : p * 8 + 8, :] for p in range(5)]
        weighted = [weight8 * p for p in part8]
        features = [weighted[i] * part8[j] for i, j in param_pairs] + [weighted[i] * res8 for i in range(5)]
        for f, feature in enumerate(features):
            high = feature.astype(jnp.bfloat16).astype(jnp.float32)
            feat_ref[f * 8 : f * 8 + 8, :] = high
            feat_ref[160 + f * 8 : 168 + f * 8, :] = feature - high
        hots = []
        blocks = []
        for k in range(8):
            body = [feat_ref[pl.ds(128 * n + k, 16, stride=8), :].astype(jnp.bfloat16) for n in range(2)]
            tail = feat_ref[pl.ds(256 + k, 8, stride=8), :]
            tail = jnp.concatenate([tail, tail], 0).astype(jnp.bfloat16)
            high = jnp.broadcast_to(high8[k : k + 1], (16, 128)).astype(jnp.bfloat16)
            tiles = []
            for pair in range(4):
                for e in range(2):
                    mask = high == jnp.bfloat16(2 * pair + e)
                    tiles.append(jnp.where(mask, body[0], zero))
                    tiles.append(jnp.where(mask, body[1], zero))
                mixed = jnp.where(sub16 < 8, 2.0 * pair, 2.0 * pair + 1.0).astype(jnp.bfloat16)
                tiles.append(jnp.where(high == mixed, tail, zero))
            blocks.append(jnp.concatenate(tiles, 0))
            hots.append(hot_rows(ids, low8[k : k + 1]))
        sums = lax.dot_general(jnp.concatenate(blocks, 1), jnp.concatenate(hots, 1), NT, preferred_element_type=jnp.float32)
        for h in range(2):
            acc_ref[h] += sums[:, h * 128 : (h + 1) * 128]

    def groups(step, carry):
        for copy in copies(step):
            copy.wait()
        for n in range(SUMS_UNROLL):
            group(step * SUMS_UNROLL + n, feat_refs.at[n], rows_refs.at[n])
        return carry

    lax.fori_loop(0, 16 // SUMS_UNROLL, groups, 0)

    def rows_of(q, e, h):
        at = 32 * e + q if q < 32 else 64 + 8 * e + q - 32
        return acc_ref[h, pl.ds(at, 4, stride=80), :]

    for f in range(20):
        for h in range(2):
            total = jnp.concatenate([rows_of(f, e, h) + rows_of(20 + f, e, h) for e in range(2)], 0)
            for q in range(4):
                out_ref[q, (h * 20 + f) * 8 : (h * 20 + f) * 8 + 8, :] = total


HIGH_ORDER = (0, 2, 4, 6, 1, 3, 5, 7)


def cholesky_solve5(normal, rhs_terms):
    matrix = {}
    for number, (i, j) in enumerate(param_pairs):
        matrix[i, j] = normal[number]
        matrix[j, i] = normal[number]
    factor = {}
    inverse_diag = []
    for row_at in range(5):
        for col_at in range(row_at + 1):
            running = matrix[row_at, col_at]
            for inner_k in range(col_at):
                running = running - factor[row_at, inner_k] * factor[col_at, inner_k]
            if row_at == col_at:
                factor[row_at, row_at] = jnp.sqrt(running)
                inverse_diag.append(1.0 / factor[row_at, row_at])
            else:
                factor[row_at, col_at] = running * inverse_diag[col_at]
    forward = []
    for row_at in range(5):
        running = rhs_terms[row_at]
        for inner_k in range(row_at):
            running = running - factor[row_at, inner_k] * forward[inner_k]
        forward.append(running * inverse_diag[row_at])
    backward = [None] * 5
    for row_at in reversed(range(5)):
        running = forward[row_at]
        for inner_k in range(row_at + 1, 5):
            running = running - factor[inner_k, row_at] * backward[inner_k]
        backward[row_at] = running * inverse_diag[row_at]
    return backward


def source_solve_kernel(
    sums_ref, prior_ref, res_ref, live_ref, part_ref, src_ref, frac_ref, interval_ref, dir_ref,
    update_far, pack_ref, base_ref, scale_ref, update_ref, root_ref, corr_ref, sem,
):
    tables = []
    for h in range(2):
        terms = []
        for f in range(20):
            at = (h * 20 + f) * 8
            terms.append(
                (sums_ref[0, at : at + 8, :] + sums_ref[1, at : at + 8, :])
                + (sums_ref[2, at : at + 8, :] + sums_ref[3, at : at + 8, :])
            )
        for number, (i, j) in enumerate(param_pairs):
            if i == j:
                prior = [prior_ref[i : i + 1, (2 * r + h) * 128 : (2 * r + h + 1) * 128] for r in HIGH_ORDER]
                terms[number] = terms[number] + jnp.concatenate(prior, 0)
        solved = cholesky_solve5(terms[:15], terms[15:])
        tables.append(solved)
        for p in range(5):
            for n, r in enumerate(HIGH_ORDER):
                update_ref[p : p + 1, (2 * r + h) * 128 : (2 * r + h + 1) * 128] = solved[p][n : n + 1]
    update_copy = pltpu.make_async_copy(update_ref, update_far, sem)
    update_copy.start()
    root_ref[...] = jnp.sqrt(live_ref[...])
    sub8 = lax.broadcasted_iota(jnp.int32, (8, 128), 0)

    def group(g, carry):
        first = pl.multiple_of(g * 8, 8)
        res8 = res_ref[pl.ds(first, 8), :]
        src8 = src_ref[pl.ds(first, 8), :]
        root8 = root_ref[pl.ds(first, 8), :]
        time8 = (interval_ref[pl.ds(first, 8), :] & 63).astype(jnp.float32) + frac_ref[pl.ds(first, 8), :]
        low8 = src8 & 127
        high8 = src8 >> 8
        place8 = (high8 >> 1) + ((high8 & 1) << 2) + (((src8 >> 7) & 1) << 3)
        pack = pack_ref.at[pl.ds(pl.multiple_of(g * 40, 8), 40), :]
        corr_rows = []
        for k in range(8):
            at = pl.multiple_of((g * 8 + k) * 128, 128)
            low = jnp.broadcast_to(low8[k : k + 1], (8, 128))
            place = jnp.broadcast_to(place8[k : k + 1], (8, 128))
            part = part_ref[:, pl.ds(at, 128)]
            found = None
            masks = [place == sub8, place == sub8 + 8]
            for p in range(5):
                wide = jnp.broadcast_to(part[p : p + 1], (8, 128))
                for h in range(2):
                    taken = jnp.take_along_axis(tables[h][p], low, axis=1, mode="promise_in_bounds")
                    term = jnp.where(masks[h], taken * wide, 0.0)
                    found = term if found is None else found + term
            corr = jnp.sum(found, 0, keepdims=True)
            corr_rows.append(corr)
            root = root8[k : k + 1]
            first_pass = root * (res8[k : k + 1] - corr)
            pack[k * 5 : k * 5 + 5, :] = jnp.concatenate([time8[k : k + 1], root * dir_ref[:, pl.ds(at, 128)], first_pass], 0)
        corr_ref[pl.ds(first, 8), :] = jnp.concatenate(corr_rows, 0)
        return carry

    lax.fori_loop(0, 16, group, 0, unroll=4)
    live = root_ref[...] > 0.0
    base_ref[...] = res_ref[...] - jnp.where(live, corr_ref[...], 0.0)
    scale_ref[...] = jnp.where(live, 1.0 / jnp.where(live, root_ref[...], 1.0), 0.0)
    update_copy.wait()


def band_sums_kernel(slots_ref, prior_ref, frame_ref, feat_refs, a_refs, acc_ref, prior_pad):
    acc_ref[...] = jnp.zeros_like(acc_ref)
    ids = lax.broadcasted_iota(jnp.int32, (64, 128), 0).astype(jnp.float32).astype(jnp.bfloat16)

    def group(g, a_ref, feat_ref):
        slots = slots_ref.at[pl.ds(pl.multiple_of(g * 40, 8), 40), :]
        time8, d0, d1, d2, fp = [slots[pl.ds(k, 8, stride=5), :] for k in range(5)]
        direction = [d0, d1, d2]
        floor8 = jnp.floor(time8)
        _, splines = spline_weights(time8)
        outer = [direction[i] * direction[j] for i, j in sym_pairs]
        right = [direction[i] * fp for i in range(3)]
        at = 0
        for m, n in spline_pairs:
            coeff = splines[m] * splines[n]
            for entry in outer:
                feat_ref[at : at + 8, :] = coeff * entry
                at += 8
        for m in range(4):
            for entry in right:
                feat_ref[at : at + 8, :] = splines[m] * entry
                at += 8
        hots = []
        for k in range(8):
            for n in range(5):
                size = 16 if n < 4 else 8
                rows = feat_ref[pl.ds(128 * n + k, size, stride=8), :]
                high = rows.astype(jnp.bfloat16)
                rest = rows - high.astype(jnp.float32)
                if n < 4:
                    a_ref[k, 16 * n : 16 * n + 16, :] = high
                    a_ref[k, 64 + 16 * n : 80 + 16 * n, :] = rest.astype(jnp.bfloat16)
                else:
                    a_ref[k, 128:144, :] = jnp.concatenate([high.astype(jnp.float32), rest], 0).astype(jnp.bfloat16)
            hots.append(hot_rows(ids, floor8[k : k + 1]))
        acc_ref[:, 0:64] += lax.dot_general(side_by_side(a_ref), jnp.concatenate(hots, 1), NT, preferred_element_type=jnp.float32)

    def groups(step, carry):
        for n in range(BAND_UNROLL):
            group(step * BAND_UNROLL + n, a_refs.at[n], feat_refs.at[n])
        return carry

    lax.fori_loop(0, 16 // BAND_UNROLL, groups, 0)
    prior_pad[...] = jnp.zeros_like(prior_pad)
    prior_pad[3:6, 0:64] = prior_ref[...]
    sums = jnp.concatenate([acc_ref[0:64, :] + acc_ref[64:128, :], acc_ref[128:136, :] + acc_ref[136:144, :]], 0)

    def tile(first, count, shift):
        rows = sums[first : first + count]
        return pltpu.roll(jnp.concatenate([rows, jnp.zeros((8 - count, 128), jnp.float32)], 0), shift, 1)

    for d in range(4):
        total = None
        for number, (m, n) in enumerate(spline_pairs):
            if n - m == d:
                term = tile(6 * number, 6, LEFT - 1 + m)
                total = term if total is None else total + term
        frame_ref[d * 8 : d * 8 + 8, :] = total
    total = pltpu.roll(prior_pad[...], LEFT, 1)
    for m in range(4):
        total = total + tile(60 + 3 * m, 3, LEFT - 1 + m)
    frame_ref[32:40, :] = total


def sym_columns(e):
    pad = [jnp.zeros((5, 128), jnp.float32)]
    return [
        jnp.concatenate([e[0], e[1], e[2]] + pad, 0),
        jnp.concatenate([e[1], e[3], e[4]] + pad, 0),
        jnp.concatenate([e[2], e[4], e[5]] + pad, 0),
    ]


def columns_apply(columns, vector):
    total = None
    for j in range(3):
        term = columns[j] * jnp.broadcast_to(vector[j : j + 1], (8, 128))
        total = term if total is None else total + term
    return total


def attitude_kernel(place_ref, own_ref, even_ref, odd_ref, slots_ref, att_far, corr_ref, att_ref, sem, *, knots_total):
    place = place_ref[0]
    lane = lax.broadcasted_iota(jnp.int32, (1, 128), 1)
    lane8 = lax.broadcasted_iota(jnp.int32, (8, 128), 1)
    is_even = place % 2 == 0
    knot = place * 64 + lane - LEFT
    valid = (knot >= 0) & (knot < knots_total)

    def frame(row):
        swap_first = even_ref[row : row + 8, :]
        swap_next = odd_ref[row : row + 8, :]
        left = jnp.where(is_even, swap_next, swap_first)
        right = jnp.where(is_even, swap_first, swap_next)
        return own_ref[row : row + 8, :] + pltpu.roll(jnp.where(lane8 < 64, right, left), 64, 1)

    uppers = [frame(8 * d) for d in range(4)]
    last = frame(32)
    e = [uppers[0][n : n + 1] for n in range(6)]
    e[0] = e[0] + last[3:4]
    e[3] = e[3] + last[4:5]
    e[5] = e[5] + last[5:6]
    c00 = e[3] * e[5] - e[4] * e[4]
    c01 = e[2] * e[4] - e[1] * e[5]
    c02 = e[1] * e[4] - e[2] * e[3]
    c11 = e[0] * e[5] - e[2] * e[2]
    c12 = e[1] * e[2] - e[0] * e[4]
    c22 = e[0] * e[3] - e[1] * e[1]
    determinant = e[0] * c00 + e[1] * c01 + e[2] * c02
    scale = jnp.where(valid, DAMPING / jnp.where(valid, determinant, 1.0), 0.0)
    inverse = sym_columns([c * scale for c in (c00, c01, c02, c11, c12, c22)])
    diag = sym_columns(e)
    upper_cols = [sym_columns([u[n : n + 1] for n in range(6)]) for u in uppers[1:]]
    rhs = last
    att = columns_apply(inverse, rhs)
    for _ in range(1, ITERS_ATT):
        applied = columns_apply(diag, att)
        for d in range(1, 4):
            applied = applied + columns_apply(upper_cols[d - 1], pltpu.roll(att, 128 - d, 1))
            applied = applied + pltpu.roll(columns_apply(upper_cols[d - 1], att), d, 1)
        att = att + columns_apply(inverse, rhs - applied)
    att_ref[...] = pltpu.roll(att, 128 - LEFT, 1)[0:3, 0:64]
    att_copy = pltpu.make_async_copy(att_ref, att_far, sem)
    att_copy.start()
    tables = [jnp.broadcast_to(att[j : j + 1], (8, 128)) for j in range(3)]

    def group(g, carry):
        slots = slots_ref.at[pl.ds(pl.multiple_of(g * 40, 8), 40), :]
        time8, d0, d1, d2 = [slots[pl.ds(k, 8, stride=5), :] for k in range(4)]
        direction = [d0, d1, d2]
        floor8, splines = spline_weights(time8)
        total = jnp.zeros((8, 128), jnp.float32)
        for m in range(4):
            at = floor8 + (LEFT - 1 + m)
            part = None
            for j in range(3):
                term = direction[j] * jnp.take_along_axis(tables[j], at, axis=1, mode="promise_in_bounds")
                part = term if part is None else part + term
            total = total + splines[m] * part
        corr_ref[pl.ds(pl.multiple_of(g * 8, 8), 8), :] = total
        return carry

    lax.fori_loop(0, 16, group, 0, unroll=4)
    att_copy.wait()


def call(kernel, outs, n_in, smem_at=(), scratch=(), far_in=(), far_out=()):
    shapes = [jax.ShapeDtypeStruct(s, jnp.float32) if i in far_out else pltpu.VMEM(s, jnp.float32) for i, s in enumerate(outs)]
    run = pl.pallas_call(
        kernel,
        out_shape=shapes,
        in_specs=[SMEM_SPEC if i in smem_at else ANY_SPEC if i in far_in else VMEM_SPEC for i in range(n_in)],
        out_specs=[ANY_SPEC if i in far_out else VMEM_SPEC for i in range(len(shapes))],
        scratch_shapes=list(scratch),
    )

    def on_chip(*args):
        near = [a if i in smem_at or i in far_in else pltpu.with_memory_space_constraint(a, pltpu.VMEM) for i, a in enumerate(args)]
        return run(*near)

    return on_chip


def body(residual, obs_weight, time_frac, src_partials, att_dir, src_prior, att_prior, obs_source, obs_interval, obs_count):
    devices = lax.axis_size("src") * lax.axis_size("seg")
    square = lambda a: a.reshape(128, 128)
    res, weight, frac, src, interval = map(square, (residual, obs_weight, time_frac, obs_source, obs_interval))
    sums, live = call(
        source_sums_kernel,
        [(4, 320, 128), (128, 128)],
        5,
        (0,),
        [
            pltpu.VMEM((2, 320, 128), jnp.float32),
            pltpu.VMEM((SUMS_UNROLL, 40, 128), jnp.float32),
            pltpu.VMEM((SUMS_UNROLL, 320, 128), jnp.float32),
            pltpu.VMEM((128, 128), jnp.float32),
            pltpu.VMEM((128, 128), jnp.float32),
            pltpu.VMEM((5, 16384), jnp.float32),
            pltpu.VMEM((128, 128), jnp.int32),
            pltpu.SemaphoreType.DMA((16 // SUMS_UNROLL, 4)),
        ],
        range(1, 5),
    )(obs_count, res, weight, src_partials, src)
    gathered = lax.all_to_all(sums, "seg", split_axis=0, concat_axis=0, tiled=True)
    src_update, packed, base, scale = call(
        source_solve_kernel,
        [(5, 2048), (640, 128), (128, 128), (128, 128)],
        9,
        (),
        [
            pltpu.VMEM((5, 2048), jnp.float32),
            pltpu.VMEM((128, 128), jnp.float32),
            pltpu.VMEM((128, 128), jnp.float32),
            pltpu.SemaphoreType.DMA,
        ],
        (),
        (0,),
    )(gathered, src_prior, res, live, src_partials, src, frac, interval, att_dir)
    arrived = lax.all_to_all(packed.reshape(128, 1, 640), "src", split_axis=0, concat_axis=0, tiled=True).reshape(640, 128)
    (frame,) = call(
        band_sums_kernel,
        [(40, 128)],
        2,
        (),
        [
            pltpu.VMEM((BAND_UNROLL, 576, 128), jnp.float32),
            pltpu.VMEM((BAND_UNROLL, 8, 144, 128), jnp.bfloat16),
            pltpu.VMEM((144, 128), jnp.float32),
            pltpu.VMEM((8, 128), jnp.float32),
        ],
    )(arrived, att_prior)
    both = ("src", "seg")
    swaps = {}
    for start in (1, 0):
        pairs = [(i, i + 1) for i in range(start, devices - 1, 2)]
        swaps[start] = lax.ppermute(frame, both, pairs + [(b, a) for a, b in pairs])
    place = lax.axis_index(both).astype(jnp.int32).reshape(1)
    att_update, correction = call(
        functools.partial(attitude_kernel, knots_total=devices * 64),
        [(3, 64), (128, 128)],
        5,
        (0,),
        [pltpu.VMEM((3, 64), jnp.float32), pltpu.SemaphoreType.DMA],
        (),
        (0,),
    )(place, frame, swaps[0], swaps[1], arrived)
    returned = lax.all_to_all(correction.reshape(128, 1, 128), "src", split_axis=0, concat_axis=0, tiled=True)
    residual_out = base - scale * returned.reshape(128, 128)
    return src_update, att_update, residual_out.reshape(-1)


def solution(mesh):
    pair = ("src", "seg")
    in_specs = (
        P(pair), P(pair), P(pair), P(None, pair), P(None, pair), P(None, "src"), P(None, pair), P(pair), P(pair), P(pair, None),
    )
    out_specs = (P(None, "src"), P(None, pair), P(pair))
    return jax.shard_map(body, mesh=mesh, in_specs=in_specs, out_specs=out_specs, check_vma=False)
```

```python
import functools

import jax
import jax.numpy as jnp
from jax import lax
from jax.experimental import pallas as pl
from jax.experimental.pallas import tpu as pltpu
from jax.sharding import PartitionSpec as P


ITERS_ATT = 6
DAMPING = 0.5
LEFT = 20

param_pairs = [(i, j) for i in range(5) for j in range(i, 5)]
sym_pairs = [(0, 0), (0, 1), (0, 2), (1, 1), (1, 2), (2, 2)]
spline_pairs = [(m, m + d) for d in range(4) for m in range(4 - d)]

VMEM_SPEC = pl.BlockSpec(memory_space=pltpu.VMEM)
SMEM_SPEC = pl.BlockSpec(memory_space=pltpu.SMEM)
ANY_SPEC = pl.BlockSpec(memory_space=pl.ANY)
NT = (((1,), (1,)), ((), ()))
SUMS_UNROLL = 8
BAND_UNROLL = 8


def spline_weights(local_time):
    floor_part = jnp.floor(local_time)
    frac = local_time - floor_part
    square = frac * frac
    cube = square * frac
    rest = 1.0 - frac
    sixth = 1.0 / 6.0
    splines = [
        rest * rest * rest * sixth,
        (3.0 * cube - 6.0 * square + 4.0) * sixth,
        (-3.0 * cube + 3.0 * square + 3.0 * frac + 1.0) * sixth,
        cube * sixth,
    ]
    return floor_part.astype(jnp.int32), splines


def side_by_side(ref):
    return jnp.concatenate([ref[k] for k in range(8)], 1)


def hot_rows(ids, row):
    wide = jnp.broadcast_to(row, (16, 128)).astype(jnp.bfloat16)
    one, zero = jnp.ones((16, 128), jnp.bfloat16), jnp.zeros((16, 128), jnp.bfloat16)
    count = ids.shape[0] // 16
    return jnp.concatenate([jnp.where(ids[16 * n : 16 * n + 16] == wide, one, zero) for n in range(count)], 0)


def source_sums_kernel(
    count_ref, res_ref, weight_ref, part_ref, src_ref, out_ref, live_ref, acc_ref, rows_refs, feat_refs
):
    acc_ref[...] = jnp.zeros_like(acc_ref)
    ids = lax.broadcasted_iota(jnp.int32, (256, 128), 0).astype(jnp.float32).astype(jnp.bfloat16)
    lane8 = lax.broadcasted_iota(jnp.int32, (8, 128), 1)
    sub8 = lax.broadcasted_iota(jnp.int32, (8, 128), 0)
    sub16 = lax.broadcasted_iota(jnp.int32, (16, 128), 0)
    zero = jnp.zeros((16, 128), jnp.bfloat16)

    def group(g, feat_ref, rows_ref):
        first = pl.multiple_of(g * 8, 8)
        res8 = res_ref[pl.ds(first, 8), :]
        src8 = src_ref[pl.ds(first, 8), :]
        low8 = (src8 & 255).astype(jnp.float32)
        high8 = (src8 >> 8).astype(jnp.float32)
        count8 = jnp.zeros((8, 128), jnp.int32)
        for k in range(8):
            count8 = jnp.where(sub8 == k, count_ref[0, g * 8 + k], count8)
            rows_ref[pl.ds(k, 5, stride=8), :] = part_ref[:, pl.ds(pl.multiple_of((g * 8 + k) * 128, 128), 128)]
        weight8 = jnp.where(lane8 < count8, weight_ref[pl.ds(first, 8), :], 0.0)
        live_ref[pl.ds(first, 8), :] = weight8
        part8 = [rows_ref[p * 8 : p * 8 + 8, :] for p in range(5)]
        weighted = [weight8 * p for p in part8]
        features = [weighted[i] * part8[j] for i, j in param_pairs] + [weighted[i] * res8 for i in range(5)]
        for f, feature in enumerate(features):
            high = feature.astype(jnp.bfloat16).astype(jnp.float32)
            feat_ref[f * 8 : f * 8 + 8, :] = high
            feat_ref[160 + f * 8 : 168 + f * 8, :] = feature - high
        hots = []
        blocks = []
        for k in range(8):
            body = [feat_ref[pl.ds(128 * n + k, 16, stride=8), :].astype(jnp.bfloat16) for n in range(2)]
            tail = feat_ref[pl.ds(256 + k, 8, stride=8), :]
            tail = jnp.concatenate([tail, tail], 0).astype(jnp.bfloat16)
            high = jnp.broadcast_to(high8[k : k + 1], (16, 128)).astype(jnp.bfloat16)
            tiles = []
            for pair in range(4):
                for e in range(2):
                    mask = high == jnp.bfloat16(2 * pair + e)
                    tiles.append(jnp.where(mask, body[0], zero))
                    tiles.append(jnp.where(mask, body[1], zero))
                mixed = jnp.where(sub16 < 8, 2.0 * pair, 2.0 * pair + 1.0).astype(jnp.bfloat16)
                tiles.append(jnp.where(high == mixed, tail, zero))
            blocks.append(jnp.concatenate(tiles, 0))
            hots.append(hot_rows(ids, low8[k : k + 1]))
        sums = lax.dot_general(jnp.concatenate(blocks, 1), jnp.concatenate(hots, 1), NT, preferred_element_type=jnp.float32)
        for h in range(2):
            acc_ref[h] += sums[:, h * 128 : (h + 1) * 128]

    def groups(step, carry):
        for n in range(SUMS_UNROLL):
            group(step * SUMS_UNROLL + n, feat_refs.at[n], rows_refs.at[n])
        return carry

    lax.fori_loop(0, 16 // SUMS_UNROLL, groups, 0)

    def rows_of(q, e, h):
        at = 32 * e + q if q < 32 else 64 + 8 * e + q - 32
        return acc_ref[h, pl.ds(at, 4, stride=80), :]

    for f in range(20):
        for h in range(2):
            total = jnp.concatenate([rows_of(f, e, h) + rows_of(20 + f, e, h) for e in range(2)], 0)
            for q in range(4):
                out_ref[q, (h * 20 + f) * 8 : (h * 20 + f) * 8 + 8, :] = total


HIGH_ORDER = (0, 2, 4, 6, 1, 3, 5, 7)


def cholesky_solve5(normal, rhs_terms):
    matrix = {}
    for number, (i, j) in enumerate(param_pairs):
        matrix[i, j] = normal[number]
        matrix[j, i] = normal[number]
    factor = {}
    inverse_diag = []
    for row_at in range(5):
        for col_at in range(row_at + 1):
            running = matrix[row_at, col_at]
            for inner_k in range(col_at):
                running = running - factor[row_at, inner_k] * factor[col_at, inner_k]
            if row_at == col_at:
                factor[row_at, row_at] = jnp.sqrt(running)
                inverse_diag.append(1.0 / factor[row_at, row_at])
            else:
                factor[row_at, col_at] = running * inverse_diag[col_at]
    forward = []
    for row_at in range(5):
        running = rhs_terms[row_at]
        for inner_k in range(row_at):
            running = running - factor[row_at, inner_k] * forward[inner_k]
        forward.append(running * inverse_diag[row_at])
    backward = [None] * 5
    for row_at in reversed(range(5)):
        running = forward[row_at]
        for inner_k in range(row_at + 1, 5):
            running = running - factor[inner_k, row_at] * backward[inner_k]
        backward[row_at] = running * inverse_diag[row_at]
    return backward


def source_solve_kernel(
    sums_ref, prior_ref, res_ref, live_ref, part_ref, src_ref, frac_ref, interval_ref, dir_ref,
    update_far, pack_ref, base_ref, scale_ref, update_ref, root_ref, corr_ref, sem,
):
    tables = []
    for h in range(2):
        terms = []
        for f in range(20):
            at = (h * 20 + f) * 8
            terms.append(
                (sums_ref[0, at : at + 8, :] + sums_ref[1, at : at + 8, :])
                + (sums_ref[2, at : at + 8, :] + sums_ref[3, at : at + 8, :])
            )
        for number, (i, j) in enumerate(param_pairs):
            if i == j:
                prior = [prior_ref[i : i + 1, (2 * r + h) * 128 : (2 * r + h + 1) * 128] for r in HIGH_ORDER]
                terms[number] = terms[number] + jnp.concatenate(prior, 0)
        solved = cholesky_solve5(terms[:15], terms[15:])
        tables.append(solved)
        for p in range(5):
            for n, r in enumerate(HIGH_ORDER):
                update_ref[p : p + 1, (2 * r + h) * 128 : (2 * r + h + 1) * 128] = solved[p][n : n + 1]
    update_copy = pltpu.make_async_copy(update_ref, update_far, sem)
    update_copy.start()
    root_ref[...] = jnp.sqrt(live_ref[...])
    sub8 = lax.broadcasted_iota(jnp.int32, (8, 128), 0)

    def group(g, carry):
        first = pl.multiple_of(g * 8, 8)
        res8 = res_ref[pl.ds(first, 8), :]
        src8 = src_ref[pl.ds(first, 8), :]
        root8 = root_ref[pl.ds(first, 8), :]
        time8 = (interval_ref[pl.ds(first, 8), :] & 63).astype(jnp.float32) + frac_ref[pl.ds(first, 8), :]
        low8 = src8 & 127
        high8 = src8 >> 8
        place8 = (high8 >> 1) + ((high8 & 1) << 2) + (((src8 >> 7) & 1) << 3)
        pack = pack_ref.at[pl.ds(pl.multiple_of(g * 40, 8), 40), :]
        corr_rows = []
        for k in range(8):
            at = pl.multiple_of((g * 8 + k) * 128, 128)
            low = jnp.broadcast_to(low8[k : k + 1], (8, 128))
            place = jnp.broadcast_to(place8[k : k + 1], (8, 128))
            part = part_ref[:, pl.ds(at, 128)]
            found = None
            masks = [place == sub8, place == sub8 + 8]
            for p in range(5):
                wide = jnp.broadcast_to(part[p : p + 1], (8, 128))
                for h in range(2):
                    taken = jnp.take_along_axis(tables[h][p], low, axis=1, mode="promise_in_bounds")
                    term = jnp.where(masks[h], taken * wide, 0.0)
                    found = term if found is None else found + term
            corr = jnp.sum(found, 0, keepdims=True)
            corr_rows.append(corr)
            root = root8[k : k + 1]
            first_pass = root * (res8[k : k + 1] - corr)
            pack[k * 5 : k * 5 + 5, :] = jnp.concatenate([time8[k : k + 1], root * dir_ref[:, pl.ds(at, 128)], first_pass], 0)
        corr_ref[pl.ds(first, 8), :] = jnp.concatenate(corr_rows, 0)
        return carry

    lax.fori_loop(0, 16, group, 0, unroll=4)
    live = root_ref[...] > 0.0
    base_ref[...] = res_ref[...] - jnp.where(live, corr_ref[...], 0.0)
    scale_ref[...] = jnp.where(live, 1.0 / jnp.where(live, root_ref[...], 1.0), 0.0)
    update_copy.wait()


def band_sums_kernel(slots_ref, prior_ref, frame_ref, feat_refs, a_refs, acc_ref, prior_pad):
    acc_ref[...] = jnp.zeros_like(acc_ref)
    ids = lax.broadcasted_iota(jnp.int32, (128, 128), 0).astype(jnp.float32).astype(jnp.bfloat16)

    def group(g, a_ref, feat_ref):
        slots = slots_ref.at[pl.ds(pl.multiple_of(g * 40, 8), 40), :]
        time8, d0, d1, d2, fp = [slots[pl.ds(k, 8, stride=5), :] for k in range(5)]
        direction = [d0, d1, d2]
        floor8 = jnp.floor(time8)
        _, splines = spline_weights(time8)
        outer = [direction[i] * direction[j] for i, j in sym_pairs]
        right = [direction[i] * fp for i in range(3)]
        at = 0
        for m, n in spline_pairs:
            coeff = splines[m] * splines[n]
            for entry in outer:
                feat_ref[at : at + 8, :] = coeff * entry
                at += 8
        for m in range(4):
            for entry in right:
                feat_ref[at : at + 8, :] = splines[m] * entry
                at += 8
        hots = []
        for k in range(8):
            for n in range(5):
                size = 16 if n < 4 else 8
                rows = feat_ref[pl.ds(128 * n + k, size, stride=8), :]
                high = rows.astype(jnp.bfloat16)
                rest = rows - high.astype(jnp.float32)
                if n < 4:
                    a_ref[k, 16 * n : 16 * n + 16, :] = high
                    a_ref[k, 64 + 16 * n : 80 + 16 * n, :] = rest.astype(jnp.bfloat16)
                else:
                    a_ref[k, 128:144, :] = jnp.concatenate([high.astype(jnp.float32), rest], 0).astype(jnp.bfloat16)
            hots.append(hot_rows(ids, floor8[k : k + 1]))
        acc_ref[...] += lax.dot_general(side_by_side(a_ref), jnp.concatenate(hots, 1), NT, preferred_element_type=jnp.float32)

    def groups(step, carry):
        for n in range(BAND_UNROLL):
            group(step * BAND_UNROLL + n, a_refs.at[n], feat_refs.at[n])
        return carry

    lax.fori_loop(0, 16 // BAND_UNROLL, groups, 0)
    prior_pad[...] = jnp.zeros_like(prior_pad)
    prior_pad[3:6, 0:64] = prior_ref[...]
    sums = jnp.concatenate([acc_ref[0:64, :] + acc_ref[64:128, :], acc_ref[128:136, :] + acc_ref[136:144, :]], 0)

    def tile(first, count, shift):
        rows = sums[first : first + count]
        return pltpu.roll(jnp.concatenate([rows, jnp.zeros((8 - count, 128), jnp.float32)], 0), shift, 1)

    for d in range(4):
        total = None
        for number, (m, n) in enumerate(spline_pairs):
            if n - m == d:
                term = tile(6 * number, 6, LEFT - 1 + m)
                total = term if total is None else total + term
        frame_ref[d * 8 : d * 8 + 8, :] = total
    total = pltpu.roll(prior_pad[...], LEFT, 1)
    for m in range(4):
        total = total + tile(60 + 3 * m, 3, LEFT - 1 + m)
    frame_ref[32:40, :] = total


def sym_columns(e):
    pad = [jnp.zeros((5, 128), jnp.float32)]
    return [
        jnp.concatenate([e[0], e[1], e[2]] + pad, 0),
        jnp.concatenate([e[1], e[3], e[4]] + pad, 0),
        jnp.concatenate([e[2], e[4], e[5]] + pad, 0),
    ]


def columns_apply(columns, vector):
    total = None
    for j in range(3):
        term = columns[j] * jnp.broadcast_to(vector[j : j + 1], (8, 128))
        total = term if total is None else total + term
    return total


def attitude_kernel(place_ref, own_ref, even_ref, odd_ref, slots_ref, att_far, corr_ref, att_ref, sem, *, knots_total):
    place = place_ref[0]
    lane = lax.broadcasted_iota(jnp.int32, (1, 128), 1)
    lane8 = lax.broadcasted_iota(jnp.int32, (8, 128), 1)
    is_even = place % 2 == 0
    knot = place * 64 + lane - LEFT
    valid = (knot >= 0) & (knot < knots_total)

    def frame(row):
        swap_first = even_ref[row : row + 8, :]
        swap_next = odd_ref[row : row + 8, :]
        left = jnp.where(is_even, swap_next, swap_first)
        right = jnp.where(is_even, swap_first, swap_next)
        return own_ref[row : row + 8, :] + pltpu.roll(jnp.where(lane8 < 64, right, left), 64, 1)

    uppers = [frame(8 * d) for d in range(4)]
    last = frame(32)
    e = [uppers[0][n : n + 1] for n in range(6)]
    e[0] = e[0] + last[3:4]
    e[3] = e[3] + last[4:5]
    e[5] = e[5] + last[5:6]
    c00 = e[3] * e[5] - e[4] * e[4]
    c01 = e[2] * e[4] - e[1] * e[5]
    c02 = e[1] * e[4] - e[2] * e[3]
    c11 = e[0] * e[5] - e[2] * e[2]
    c12 = e[1] * e[2] - e[0] * e[4]
    c22 = e[0] * e[3] - e[1] * e[1]
    determinant = e[0] * c00 + e[1] * c01 + e[2] * c02
    scale = jnp.where(valid, DAMPING / jnp.where(valid, determinant, 1.0), 0.0)
    inverse = sym_columns([c * scale for c in (c00, c01, c02, c11, c12, c22)])
    diag = sym_columns(e)
    upper_cols = [sym_columns([u[n : n + 1] for n in range(6)]) for u in uppers[1:]]
    rhs = last
    att = columns_apply(inverse, rhs)
    for _ in range(1, ITERS_ATT):
        applied = columns_apply(diag, att)
        for d in range(1, 4):
            applied = applied + columns_apply(upper_cols[d - 1], pltpu.roll(att, 128 - d, 1))
            applied = applied + pltpu.roll(columns_apply(upper_cols[d - 1], att), d, 1)
        att = att + columns_apply(inverse, rhs - applied)
    att_ref[...] = pltpu.roll(att, 128 - LEFT, 1)[0:3, 0:64]
    att_copy = pltpu.make_async_copy(att_ref, att_far, sem)
    att_copy.start()
    tables = [jnp.broadcast_to(att[j : j + 1], (8, 128)) for j in range(3)]

    def group(g, carry):
        slots = slots_ref.at[pl.ds(pl.multiple_of(g * 40, 8), 40), :]
        time8, d0, d1, d2 = [slots[pl.ds(k, 8, stride=5), :] for k in range(4)]
        direction = [d0, d1, d2]
        floor8, splines = spline_weights(time8)
        total = jnp.zeros((8, 128), jnp.float32)
        for m in range(4):
            at = floor8 + (LEFT - 1 + m)
            part = None
            for j in range(3):
                term = direction[j] * jnp.take_along_axis(tables[j], at, axis=1, mode="promise_in_bounds")
                part = term if part is None else part + term
            total = total + splines[m] * part
        corr_ref[pl.ds(pl.multiple_of(g * 8, 8), 8), :] = total
        return carry

    lax.fori_loop(0, 16, group, 0, unroll=4)
    att_copy.wait()


def call(kernel, outs, n_in, smem_at=(), scratch=(), far_in=(), far_out=()):
    shapes = [jax.ShapeDtypeStruct(s, jnp.float32) if i in far_out else pltpu.VMEM(s, jnp.float32) for i, s in enumerate(outs)]
    run = pl.pallas_call(
        kernel,
        out_shape=shapes,
        in_specs=[SMEM_SPEC if i in smem_at else VMEM_SPEC for i in range(n_in)],
        out_specs=[ANY_SPEC if i in far_out else VMEM_SPEC for i in range(len(shapes))],
        scratch_shapes=list(scratch),
    )

    def on_chip(*args):
        near = [a if i in smem_at or i in far_in else pltpu.with_memory_space_constraint(a, pltpu.VMEM) for i, a in enumerate(args)]
        return run(*near)

    return on_chip


def body(residual, obs_weight, time_frac, src_partials, att_dir, src_prior, att_prior, obs_source, obs_interval, obs_count):
    devices = lax.axis_size("src") * lax.axis_size("seg")
    square = lambda a: a.reshape(128, 128)
    res, weight, frac, src, interval = map(square, (residual, obs_weight, time_frac, obs_source, obs_interval))
    sums, live = call(
        source_sums_kernel,
        [(4, 320, 128), (128, 128)],
        5,
        (0,),
        [
            pltpu.VMEM((2, 320, 128), jnp.float32),
            pltpu.VMEM((SUMS_UNROLL, 40, 128), jnp.float32),
            pltpu.VMEM((SUMS_UNROLL, 320, 128), jnp.float32),
        ],
        range(1, 5),
    )(obs_count, res, weight, src_partials, src)
    gathered = lax.all_to_all(sums, "seg", split_axis=0, concat_axis=0, tiled=True)
    src_update, packed, base, scale = call(
        source_solve_kernel,
        [(5, 2048), (640, 128), (128, 128), (128, 128)],
        9,
        (),
        [
            pltpu.VMEM((5, 2048), jnp.float32),
            pltpu.VMEM((128, 128), jnp.float32),
            pltpu.VMEM((128, 128), jnp.float32),
            pltpu.SemaphoreType.DMA,
        ],
        (),
        (0,),
    )(gathered, src_prior, res, live, src_partials, src, frac, interval, att_dir)
    arrived = lax.all_to_all(packed.reshape(128, 1, 640), "src", split_axis=0, concat_axis=0, tiled=True).reshape(640, 128)
    (frame,) = call(
        band_sums_kernel,
        [(40, 128)],
        2,
        (),
        [
            pltpu.VMEM((BAND_UNROLL, 576, 128), jnp.float32),
            pltpu.VMEM((BAND_UNROLL, 8, 144, 128), jnp.bfloat16),
            pltpu.VMEM((144, 128), jnp.float32),
            pltpu.VMEM((8, 128), jnp.float32),
        ],
    )(arrived, att_prior)
    both = ("src", "seg")
    swaps = {}
    for start in (1, 0):
        pairs = [(i, i + 1) for i in range(start, devices - 1, 2)]
        swaps[start] = lax.ppermute(frame, both, pairs + [(b, a) for a, b in pairs])
    place = lax.axis_index(both).astype(jnp.int32).reshape(1)
    att_update, correction = call(
        functools.partial(attitude_kernel, knots_total=devices * 64),
        [(3, 64), (128, 128)],
        5,
        (0,),
        [pltpu.VMEM((3, 64), jnp.float32), pltpu.SemaphoreType.DMA],
        (),
        (0,),
    )(place, frame, swaps[0], swaps[1], arrived)
    returned = lax.all_to_all(correction.reshape(128, 1, 128), "src", split_axis=0, concat_axis=0, tiled=True)
    residual_out = base - scale * returned.reshape(128, 128)
    return src_update, att_update, residual_out.reshape(-1)


def solution(mesh):
    pair = ("src", "seg")
    in_specs = (
        P(pair), P(pair), P(pair), P(None, pair), P(None, pair), P(None, "src"), P(None, pair), P(pair), P(pair), P(pair, None),
    )
    out_specs = (P(None, "src"), P(None, pair), P(pair))
    return jax.shard_map(body, mesh=mesh, in_specs=in_specs, out_specs=out_specs, check_vma=False)
```

```python
import functools

import jax
import jax.numpy as jnp
from jax import lax
from jax.experimental import pallas as pl
from jax.experimental.pallas import tpu as pltpu
from jax.sharding import PartitionSpec as P


ITERS_ATT = 6
DAMPING = 0.5
LEFT = 20

param_pairs = [(i, j) for i in range(5) for j in range(i, 5)]
sym_pairs = [(0, 0), (0, 1), (0, 2), (1, 1), (1, 2), (2, 2)]
spline_pairs = [(m, m + d) for d in range(4) for m in range(4 - d)]

VMEM_SPEC = pl.BlockSpec(memory_space=pltpu.VMEM)
SMEM_SPEC = pl.BlockSpec(memory_space=pltpu.SMEM)
ANY_SPEC = pl.BlockSpec(memory_space=pl.ANY)
NT = (((1,), (1,)), ((), ()))
SUMS_UNROLL = 8
BAND_UNROLL = 8


def spline_weights(local_time):
    floor_part = jnp.floor(local_time)
    frac = local_time - floor_part
    square = frac * frac
    cube = square * frac
    rest = 1.0 - frac
    sixth = 1.0 / 6.0
    splines = [
        rest * rest * rest * sixth,
        (3.0 * cube - 6.0 * square + 4.0) * sixth,
        (-3.0 * cube + 3.0 * square + 3.0 * frac + 1.0) * sixth,
        cube * sixth,
    ]
    return floor_part.astype(jnp.int32), splines


def side_by_side(ref):
    return jnp.concatenate([ref[k] for k in range(8)], 1)


def hot_rows(ids, row):
    wide = jnp.broadcast_to(row, (16, 128)).astype(jnp.bfloat16)
    one, zero = jnp.ones((16, 128), jnp.bfloat16), jnp.zeros((16, 128), jnp.bfloat16)
    count = ids.shape[0] // 16
    return jnp.concatenate([jnp.where(ids[16 * n : 16 * n + 16] == wide, one, zero) for n in range(count)], 0)


def slot_pack_kernel(count_ref, weight_ref, frac_ref, interval_ref, dir_ref, pack_ref, live_ref, root_ref):
    lane8 = lax.broadcasted_iota(jnp.int32, (8, 128), 1)
    sub8 = lax.broadcasted_iota(jnp.int32, (8, 128), 0)

    def group(g, carry):
        first = pl.multiple_of(g * 8, 8)
        count8 = jnp.zeros((8, 128), jnp.int32)
        for k in range(8):
            count8 = jnp.where(sub8 == k, count_ref[0, g * 8 + k], count8)
        live8 = jnp.where(lane8 < count8, weight_ref[pl.ds(first, 8), :], 0.0)
        root8 = jnp.sqrt(live8)
        live_ref[pl.ds(first, 8), :] = live8
        root_ref[pl.ds(first, 8), :] = root8
        time8 = (interval_ref[pl.ds(first, 8), :] & 63).astype(jnp.float32) + frac_ref[pl.ds(first, 8), :]
        pack = pack_ref.at[pl.ds(pl.multiple_of(g * 32, 8), 32), :]
        for k in range(8):
            at = pl.multiple_of((g * 8 + k) * 128, 128)
            pack[k * 4 : k * 4 + 4, :] = jnp.concatenate([time8[k : k + 1], root8[k : k + 1] * dir_ref[:, pl.ds(at, 128)]], 0)
        return carry

    lax.fori_loop(0, 16, group, 0, unroll=4)


def source_sums_kernel(live_ref, res_ref, part_ref, src_ref, out_ref, acc_ref, rows_refs, feat_refs):
    acc_ref[...] = jnp.zeros_like(acc_ref)
    ids = lax.broadcasted_iota(jnp.int32, (256, 128), 0).astype(jnp.float32).astype(jnp.bfloat16)
    sub16 = lax.broadcasted_iota(jnp.int32, (16, 128), 0)
    zero = jnp.zeros((16, 128), jnp.bfloat16)

    def group(g, feat_ref, rows_ref):
        first = pl.multiple_of(g * 8, 8)
        res8 = res_ref[pl.ds(first, 8), :]
        src8 = src_ref[pl.ds(first, 8), :]
        low8 = (src8 & 255).astype(jnp.float32)
        high8 = (src8 >> 8).astype(jnp.float32)
        for k in range(8):
            rows_ref[pl.ds(k, 5, stride=8), :] = part_ref[:, pl.ds(pl.multiple_of((g * 8 + k) * 128, 128), 128)]
        weight8 = live_ref[pl.ds(first, 8), :]
        part8 = [rows_ref[p * 8 : p * 8 + 8, :] for p in range(5)]
        weighted = [weight8 * p for p in part8]
        features = [weighted[i] * part8[j] for i, j in param_pairs] + [weighted[i] * res8 for i in range(5)]
        for f, feature in enumerate(features):
            high = feature.astype(jnp.bfloat16).astype(jnp.float32)
            feat_ref[f * 8 : f * 8 + 8, :] = high
            feat_ref[160 + f * 8 : 168 + f * 8, :] = feature - high
        hots = []
        blocks = []
        for k in range(8):
            body = [feat_ref[pl.ds(128 * n + k, 16, stride=8), :].astype(jnp.bfloat16) for n in range(2)]
            tail = feat_ref[pl.ds(256 + k, 8, stride=8), :]
            tail = jnp.concatenate([tail, tail], 0).astype(jnp.bfloat16)
            high = jnp.broadcast_to(high8[k : k + 1], (16, 128)).astype(jnp.bfloat16)
            tiles = []
            for pair in range(4):
                for e in range(2):
                    mask = high == jnp.bfloat16(2 * pair + e)
                    tiles.append(jnp.where(mask, body[0], zero))
                    tiles.append(jnp.where(mask, body[1], zero))
                mixed = jnp.where(sub16 < 8, 2.0 * pair, 2.0 * pair + 1.0).astype(jnp.bfloat16)
                tiles.append(jnp.where(high == mixed, tail, zero))
            blocks.append(jnp.concatenate(tiles, 0))
            hots.append(hot_rows(ids, low8[k : k + 1]))
        sums = lax.dot_general(jnp.concatenate(blocks, 1), jnp.concatenate(hots, 1), NT, preferred_element_type=jnp.float32)
        for h in range(2):
            acc_ref[h] += sums[:, h * 128 : (h + 1) * 128]

    def groups(step, carry):
        for n in range(SUMS_UNROLL):
            group(step * SUMS_UNROLL + n, feat_refs.at[n], rows_refs.at[n])
        return carry

    lax.fori_loop(0, 16 // SUMS_UNROLL, groups, 0)

    def rows_of(q, e, h):
        at = 32 * e + q if q < 32 else 64 + 8 * e + q - 32
        return acc_ref[h, pl.ds(at, 4, stride=80), :]

    for f in range(20):
        for h in range(2):
            total = jnp.concatenate([rows_of(f, e, h) + rows_of(20 + f, e, h) for e in range(2)], 0)
            out_ref[(h * 20 + f) * 8 : (h * 20 + f) * 8 + 8, :] = total


HIGH_ORDER = (0, 2, 4, 6, 1, 3, 5, 7)


def cholesky_solve5(normal, rhs_terms):
    matrix = {}
    for number, (i, j) in enumerate(param_pairs):
        matrix[i, j] = normal[number]
        matrix[j, i] = normal[number]
    factor = {}
    inverse_diag = []
    for row_at in range(5):
        for col_at in range(row_at + 1):
            running = matrix[row_at, col_at]
            for inner_k in range(col_at):
                running = running - factor[row_at, inner_k] * factor[col_at, inner_k]
            if row_at == col_at:
                factor[row_at, row_at] = jnp.sqrt(running)
                inverse_diag.append(1.0 / factor[row_at, row_at])
            else:
                factor[row_at, col_at] = running * inverse_diag[col_at]
    forward = []
    for row_at in range(5):
        running = rhs_terms[row_at]
        for inner_k in range(row_at):
            running = running - factor[row_at, inner_k] * forward[inner_k]
        forward.append(running * inverse_diag[row_at])
    backward = [None] * 5
    for row_at in reversed(range(5)):
        running = forward[row_at]
        for inner_k in range(row_at + 1, 5):
            running = running - factor[inner_k, row_at] * backward[inner_k]
        backward[row_at] = running * inverse_diag[row_at]
    return backward


def source_solve_kernel(
    after_ref, sums_0, sums_1, sums_2, sums_3, prior_ref, res_ref, root_ref, part_ref, src_ref,
    update_far, first_ref, base_ref, scale_ref, update_ref, corr_ref, sem,
):
    tables = []
    for h in range(2):
        terms = []
        for f in range(20):
            at = (h * 20 + f) * 8
            terms.append(
                (sums_0[at : at + 8, :] + sums_1[at : at + 8, :])
                + (sums_2[at : at + 8, :] + sums_3[at : at + 8, :])
            )
        for number, (i, j) in enumerate(param_pairs):
            if i == j:
                prior = [prior_ref[i : i + 1, (2 * r + h) * 128 : (2 * r + h + 1) * 128] for r in HIGH_ORDER]
                terms[number] = terms[number] + jnp.concatenate(prior, 0)
        solved = cholesky_solve5(terms[:15], terms[15:])
        tables.append(solved)
        for p in range(5):
            for n, r in enumerate(HIGH_ORDER):
                update_ref[p : p + 1, (2 * r + h) * 128 : (2 * r + h + 1) * 128] = solved[p][n : n + 1]
    update_copy = pltpu.make_async_copy(update_ref, update_far, sem)
    update_copy.start()
    sub8 = lax.broadcasted_iota(jnp.int32, (8, 128), 0)

    def group(g, carry):
        first = pl.multiple_of(g * 8, 8)
        src8 = src_ref[pl.ds(first, 8), :]
        low8 = src8 & 127
        high8 = src8 >> 8
        place8 = (high8 >> 1) + ((high8 & 1) << 2) + (((src8 >> 7) & 1) << 3)
        corr_rows = []
        for k in range(8):
            at = pl.multiple_of((g * 8 + k) * 128, 128)
            low = jnp.broadcast_to(low8[k : k + 1], (8, 128))
            place = jnp.broadcast_to(place8[k : k + 1], (8, 128))
            part = part_ref[:, pl.ds(at, 128)]
            found = None
            masks = [place == sub8, place == sub8 + 8]
            for p in range(5):
                wide = jnp.broadcast_to(part[p : p + 1], (8, 128))
                for h in range(2):
                    taken = jnp.take_along_axis(tables[h][p], low, axis=1, mode="promise_in_bounds")
                    term = jnp.where(masks[h], taken * wide, 0.0)
                    found = term if found is None else found + term
            corr = jnp.sum(found, 0, keepdims=True)
            corr_rows.append(corr)
        corr_ref[pl.ds(first, 8), :] = jnp.concatenate(corr_rows, 0)
        return carry

    lax.fori_loop(0, 16, group, 0, unroll=4)
    live = root_ref[...] > 0.0
    base_ref[...] = res_ref[...] - jnp.where(live, corr_ref[...], 0.0)
    first_ref[...] = root_ref[...] * (res_ref[...] - corr_ref[...])
    scale_ref[...] = jnp.where(live, 1.0 / jnp.where(live, root_ref[...], 1.0), 0.0)
    update_copy.wait()


def band_sums_kernel(slots_ref, first_ref, prior_ref, frame_ref, feat_refs, a_refs, acc_ref, prior_pad):
    acc_ref[...] = jnp.zeros_like(acc_ref)
    ids = lax.broadcasted_iota(jnp.int32, (128, 128), 0).astype(jnp.float32).astype(jnp.bfloat16)

    def group(g, a_ref, feat_ref):
        slots = slots_ref.at[pl.ds(pl.multiple_of(g * 32, 8), 32), :]
        time8, d0, d1, d2 = [slots[pl.ds(k, 8, stride=4), :] for k in range(4)]
        fp = first_ref[pl.ds(pl.multiple_of(g * 8, 8), 8), :]
        direction = [d0, d1, d2]
        floor8 = jnp.floor(time8)
        _, splines = spline_weights(time8)
        outer = [direction[i] * direction[j] for i, j in sym_pairs]
        right = [direction[i] * fp for i in range(3)]
        at = 0
        for m, n in spline_pairs:
            coeff = splines[m] * splines[n]
            for entry in outer:
                feat_ref[at : at + 8, :] = coeff * entry
                at += 8
        for m in range(4):
            for entry in right:
                feat_ref[at : at + 8, :] = splines[m] * entry
                at += 8
        hots = []
        for k in range(8):
            for n in range(5):
                size = 16 if n < 4 else 8
                rows = feat_ref[pl.ds(128 * n + k, size, stride=8), :]
                high = rows.astype(jnp.bfloat16)
                rest = rows - high.astype(jnp.float32)
                if n < 4:
                    a_ref[k, 16 * n : 16 * n + 16, :] = high
                    a_ref[k, 64 + 16 * n : 80 + 16 * n, :] = rest.astype(jnp.bfloat16)
                else:
                    a_ref[k, 128:144, :] = jnp.concatenate([high.astype(jnp.float32), rest], 0).astype(jnp.bfloat16)
            hots.append(hot_rows(ids, floor8[k : k + 1]))
        acc_ref[...] += lax.dot_general(side_by_side(a_ref), jnp.concatenate(hots, 1), NT, preferred_element_type=jnp.float32)

    def groups(step, carry):
        for n in range(BAND_UNROLL):
            group(step * BAND_UNROLL + n, a_refs.at[n], feat_refs.at[n])
        return carry

    lax.fori_loop(0, 16 // BAND_UNROLL, groups, 0)
    prior_pad[...] = jnp.zeros_like(prior_pad)
    prior_pad[3:6, 0:64] = prior_ref[...]
    sums = jnp.concatenate([acc_ref[0:64, :] + acc_ref[64:128, :], acc_ref[128:136, :] + acc_ref[136:144, :]], 0)

    def tile(first, count, shift):
        rows = sums[first : first + count]
        return pltpu.roll(jnp.concatenate([rows, jnp.zeros((8 - count, 128), jnp.float32)], 0), shift, 1)

    for d in range(4):
        total = None
        for number, (m, n) in enumerate(spline_pairs):
            if n - m == d:
                term = tile(6 * number, 6, LEFT - 1 + m)
                total = term if total is None else total + term
        frame_ref[d * 8 : d * 8 + 8, :] = total
    total = pltpu.roll(prior_pad[...], LEFT, 1)
    for m in range(4):
        total = total + tile(60 + 3 * m, 3, LEFT - 1 + m)
    frame_ref[32:40, :] = total


def sym_columns(e):
    pad = [jnp.zeros((5, 128), jnp.float32)]
    return [
        jnp.concatenate([e[0], e[1], e[2]] + pad, 0),
        jnp.concatenate([e[1], e[3], e[4]] + pad, 0),
        jnp.concatenate([e[2], e[4], e[5]] + pad, 0),
    ]


def columns_apply(columns, vector):
    total = None
    for j in range(3):
        term = columns[j] * jnp.broadcast_to(vector[j : j + 1], (8, 128))
        total = term if total is None else total + term
    return total


def attitude_kernel(place_ref, own_ref, even_ref, odd_ref, slots_ref, att_far, corr_ref, att_ref, sem, *, knots_total):
    place = place_ref[0]
    lane = lax.broadcasted_iota(jnp.int32, (1, 128), 1)
    lane8 = lax.broadcasted_iota(jnp.int32, (8, 128), 1)
    is_even = place % 2 == 0
    knot = place * 64 + lane - LEFT
    valid = (knot >= 0) & (knot < knots_total)

    def frame(row):
        swap_first = even_ref[row : row + 8, :]
        swap_next = odd_ref[row : row + 8, :]
        left = jnp.where(is_even, swap_next, swap_first)
        right = jnp.where(is_even, swap_first, swap_next)
        return own_ref[row : row + 8, :] + pltpu.roll(jnp.where(lane8 < 64, right, left), 64, 1)

    uppers = [frame(8 * d) for d in range(4)]
    last = frame(32)
    e = [uppers[0][n : n + 1] for n in range(6)]
    e[0] = e[0] + last[3:4]
    e[3] = e[3] + last[4:5]
    e[5] = e[5] + last[5:6]
    c00 = e[3] * e[5] - e[4] * e[4]
    c01 = e[2] * e[4] - e[1] * e[5]
    c02 = e[1] * e[4] - e[2] * e[3]
    c11 = e[0] * e[5] - e[2] * e[2]
    c12 = e[1] * e[2] - e[0] * e[4]
    c22 = e[0] * e[3] - e[1] * e[1]
    determinant = e[0] * c00 + e[1] * c01 + e[2] * c02
    scale = jnp.where(valid, DAMPING / jnp.where(valid, determinant, 1.0), 0.0)
    inverse = sym_columns([c * scale for c in (c00, c01, c02, c11, c12, c22)])
    diag = sym_columns(e)
    upper_cols = [sym_columns([u[n : n + 1] for n in range(6)]) for u in uppers[1:]]
    rhs = last
    att = columns_apply(inverse, rhs)
    for _ in range(1, ITERS_ATT):
        applied = columns_apply(diag, att)
        for d in range(1, 4):
            applied = applied + columns_apply(upper_cols[d - 1], pltpu.roll(att, 128 - d, 1))
            applied = applied + pltpu.roll(columns_apply(upper_cols[d - 1], att), d, 1)
        att = att + columns_apply(inverse, rhs - applied)
    att_ref[...] = pltpu.roll(att, 128 - LEFT, 1)[0:3, 0:64]
    att_copy = pltpu.make_async_copy(att_ref, att_far, sem)
    att_copy.start()
    tables = [jnp.broadcast_to(att[j : j + 1], (8, 128)) for j in range(3)]

    def group(g, carry):
        slots = slots_ref.at[pl.ds(pl.multiple_of(g * 32, 8), 32), :]
        time8, d0, d1, d2 = [slots[pl.ds(k, 8, stride=4), :] for k in range(4)]
        direction = [d0, d1, d2]
        floor8, splines = spline_weights(time8)
        total = jnp.zeros((8, 128), jnp.float32)
        for m in range(4):
            at = floor8 + (LEFT - 1 + m)
            part = None
            for j in range(3):
                term = direction[j] * jnp.take_along_axis(tables[j], at, axis=1, mode="promise_in_bounds")
                part = term if part is None else part + term
            total = total + splines[m] * part
        corr_ref[pl.ds(pl.multiple_of(g * 8, 8), 8), :] = total
        return carry

    lax.fori_loop(0, 16, group, 0, unroll=4)
    att_copy.wait()


def call(kernel, outs, n_in, smem_at=(), scratch=(), far_in=(), far_out=(), plain_out=()):
    shapes = [jax.ShapeDtypeStruct(s, jnp.float32) if i in far_out or i in plain_out else pltpu.VMEM(s, jnp.float32) for i, s in enumerate(outs)]
    run = pl.pallas_call(
        kernel,
        out_shape=shapes,
        in_specs=[SMEM_SPEC if i in smem_at else VMEM_SPEC for i in range(n_in)],
        out_specs=[ANY_SPEC if i in far_out else VMEM_SPEC for i in range(len(shapes))],
        scratch_shapes=list(scratch),
    )

    def on_chip(*args):
        near = [a if i in smem_at or i in far_in else pltpu.with_memory_space_constraint(a, pltpu.VMEM) for i, a in enumerate(args)]
        return run(*near)

    return on_chip


def body(residual, obs_weight, time_frac, src_partials, att_dir, src_prior, att_prior, obs_source, obs_interval, obs_count):
    devices = lax.axis_size("src") * lax.axis_size("seg")
    square = lambda a: a.reshape(128, 128)
    res, weight, frac, src, interval = map(square, (residual, obs_weight, time_frac, obs_source, obs_interval))
    pack, live, root = call(
        slot_pack_kernel, [(512, 128), (128, 128), (128, 128)], 5, (0,), (), range(1, 5), (), (0,)
    )(obs_count, weight, frac, interval, att_dir)
    packed = lax.all_to_all(pack.reshape(128, 1, 512), "src", split_axis=0, concat_axis=0, tiled=True)
    (sums,) = call(
        source_sums_kernel,
        [(320, 128)],
        4,
        (),
        [
            pltpu.VMEM((2, 320, 128), jnp.float32),
            pltpu.VMEM((SUMS_UNROLL, 40, 128), jnp.float32),
            pltpu.VMEM((SUMS_UNROLL, 320, 128), jnp.float32),
        ],
        range(1, 4),
    )(live, res, src_partials, src)
    arrived = packed.reshape(512, 128)
    segs = lax.axis_size("seg")
    others = [lax.ppermute(sums, "seg", [(i, (i + k) % segs) for i in range(segs)]) for k in (2, 1, 3)]
    src_update, first_pass, base, scale = call(
        source_solve_kernel,
        [(5, 2048), (128, 128), (128, 128), (128, 128)],
        10,
        (),
        [pltpu.VMEM((5, 2048), jnp.float32), pltpu.VMEM((128, 128), jnp.float32), pltpu.SemaphoreType.DMA],
        (),
        (0,),
    )(arrived, sums, *others, src_prior, res, root, src_partials, src)
    arrived_first = lax.all_to_all(first_pass.reshape(128, 1, 128), "src", split_axis=0, concat_axis=0, tiled=True).reshape(128, 128)
    (frame,) = call(
        band_sums_kernel,
        [(40, 128)],
        3,
        (),
        [
            pltpu.VMEM((BAND_UNROLL, 576, 128), jnp.float32),
            pltpu.VMEM((BAND_UNROLL, 8, 144, 128), jnp.bfloat16),
            pltpu.VMEM((144, 128), jnp.float32),
            pltpu.VMEM((8, 128), jnp.float32),
        ],
    )(arrived, arrived_first, att_prior)
    both = ("src", "seg")
    swaps = {}
    for start in (1, 0):
        pairs = [(i, i + 1) for i in range(start, devices - 1, 2)]
        swaps[start] = lax.ppermute(frame, both, pairs + [(b, a) for a, b in pairs])
    place = lax.axis_index(both).astype(jnp.int32).reshape(1)
    att_update, correction = call(
        functools.partial(attitude_kernel, knots_total=devices * 64),
        [(3, 64), (128, 128)],
        5,
        (0,),
        [pltpu.VMEM((3, 64), jnp.float32), pltpu.SemaphoreType.DMA],
        (),
        (0,),
    )(place, frame, swaps[0], swaps[1], arrived)
    returned = lax.all_to_all(correction.reshape(128, 1, 128), "src", split_axis=0, concat_axis=0, tiled=True)
    residual_out = base - scale * returned.reshape(128, 128)
    return src_update, att_update, residual_out.reshape(-1)


def solution(mesh):
    pair = ("src", "seg")
    in_specs = (
        P(pair), P(pair), P(pair), P(None, pair), P(None, pair), P(None, "src"), P(None, pair), P(pair), P(pair), P(pair, None),
    )
    out_specs = (P(None, "src"), P(None, pair), P(pair))
    return jax.shard_map(body, mesh=mesh, in_specs=in_specs, out_specs=out_specs, check_vma=False)
```

```python
import functools

import jax
import jax.numpy as jnp
from jax import lax
from jax.experimental import pallas as pl
from jax.experimental.pallas import tpu as pltpu
from jax.sharding import PartitionSpec as P


ITERS_ATT = 6
DAMPING = 0.5
LEFT = 20

param_pairs = [(i, j) for i in range(5) for j in range(i, 5)]
sym_pairs = [(0, 0), (0, 1), (0, 2), (1, 1), (1, 2), (2, 2)]
spline_pairs = [(m, m + d) for d in range(4) for m in range(4 - d)]

VMEM_SPEC = pl.BlockSpec(memory_space=pltpu.VMEM)
SMEM_SPEC = pl.BlockSpec(memory_space=pltpu.SMEM)
ANY_SPEC = pl.BlockSpec(memory_space=pl.ANY)
NT = (((1,), (1,)), ((), ()))
SUMS_UNROLL = 8
BAND_UNROLL = 8


def spline_weights(local_time):
    floor_part = jnp.floor(local_time)
    frac = local_time - floor_part
    square = frac * frac
    cube = square * frac
    rest = 1.0 - frac
    sixth = 1.0 / 6.0
    splines = [
        rest * rest * rest * sixth,
        (3.0 * cube - 6.0 * square + 4.0) * sixth,
        (-3.0 * cube + 3.0 * square + 3.0 * frac + 1.0) * sixth,
        cube * sixth,
    ]
    return floor_part.astype(jnp.int32), splines


def side_by_side(ref):
    return jnp.concatenate([ref[k] for k in range(8)], 1)


def hot_rows(ids, row):
    wide = jnp.broadcast_to(row, (16, 128)).astype(jnp.bfloat16)
    one, zero = jnp.ones((16, 128), jnp.bfloat16), jnp.zeros((16, 128), jnp.bfloat16)
    count = ids.shape[0] // 16
    return jnp.concatenate([jnp.where(ids[16 * n : 16 * n + 16] == wide, one, zero) for n in range(count)], 0)


def source_sums_kernel(
    count_ref, res_ref, weight_ref, part_ref, src_ref, out_ref, live_ref, acc_ref, rows_refs, feat_refs
):
    acc_ref[...] = jnp.zeros_like(acc_ref)
    ids = lax.broadcasted_iota(jnp.int32, (256, 128), 0).astype(jnp.float32).astype(jnp.bfloat16)
    lane8 = lax.broadcasted_iota(jnp.int32, (8, 128), 1)
    sub8 = lax.broadcasted_iota(jnp.int32, (8, 128), 0)
    sub16 = lax.broadcasted_iota(jnp.int32, (16, 128), 0)
    zero = jnp.zeros((16, 128), jnp.bfloat16)

    def group(g, feat_ref, rows_ref):
        first = pl.multiple_of(g * 8, 8)
        res8 = res_ref[pl.ds(first, 8), :]
        src8 = src_ref[pl.ds(first, 8), :]
        low8 = (src8 & 255).astype(jnp.float32)
        high8 = (src8 >> 8).astype(jnp.float32)
        count8 = jnp.zeros((8, 128), jnp.int32)
        for k in range(8):
            count8 = jnp.where(sub8 == k, count_ref[0, g * 8 + k], count8)
            rows_ref[pl.ds(k, 5, stride=8), :] = part_ref[:, pl.ds(pl.multiple_of((g * 8 + k) * 128, 128), 128)]
        weight8 = jnp.where(lane8 < count8, weight_ref[pl.ds(first, 8), :], 0.0)
        live_ref[pl.ds(first, 8), :] = weight8
        part8 = [rows_ref[p * 8 : p * 8 + 8, :] for p in range(5)]
        weighted = [weight8 * p for p in part8]
        features = [weighted[i] * part8[j] for i, j in param_pairs] + [weighted[i] * res8 for i in range(5)]
        for f, feature in enumerate(features):
            high = feature.astype(jnp.bfloat16).astype(jnp.float32)
            feat_ref[f * 8 : f * 8 + 8, :] = high
            feat_ref[160 + f * 8 : 168 + f * 8, :] = feature - high
        hots = []
        blocks = []
        for k in range(8):
            body = [feat_ref[pl.ds(128 * n + k, 16, stride=8), :].astype(jnp.bfloat16) for n in range(2)]
            tail = feat_ref[pl.ds(256 + k, 8, stride=8), :]
            tail = jnp.concatenate([tail, tail], 0).astype(jnp.bfloat16)
            high = jnp.broadcast_to(high8[k : k + 1], (16, 128)).astype(jnp.bfloat16)
            tiles = []
            for pair in range(4):
                for e in range(2):
                    mask = high == jnp.bfloat16(2 * pair + e)
                    tiles.append(jnp.where(mask, body[0], zero))
                    tiles.append(jnp.where(mask, body[1], zero))
                mixed = jnp.where(sub16 < 8, 2.0 * pair, 2.0 * pair + 1.0).astype(jnp.bfloat16)
                tiles.append(jnp.where(high == mixed, tail, zero))
            blocks.append(jnp.concatenate(tiles, 0))
            hots.append(hot_rows(ids, low8[k : k + 1]))
        sums = lax.dot_general(jnp.concatenate(blocks, 1), jnp.concatenate(hots, 1), NT, preferred_element_type=jnp.float32)
        for h in range(2):
            acc_ref[h] += sums[:, h * 128 : (h + 1) * 128]

    def groups(step, carry):
        for n in range(SUMS_UNROLL):
            group(step * SUMS_UNROLL + n, feat_refs.at[n], rows_refs.at[n])
        return carry

    lax.fori_loop(0, 16 // SUMS_UNROLL, groups, 0)

    def rows_of(q, e, h):
        at = 32 * e + q if q < 32 else 64 + 8 * e + q - 32
        return acc_ref[h, pl.ds(at, 4, stride=80), :]

    for f in range(20):
        for h in range(2):
            total = jnp.concatenate([rows_of(f, e, h) + rows_of(20 + f, e, h) for e in range(2)], 0)
            for q in range(4):
                out_ref[q, (h * 20 + f) * 8 : (h * 20 + f) * 8 + 8, :] = total


HIGH_ORDER = (0, 2, 4, 6, 1, 3, 5, 7)


def cholesky_solve5(normal, rhs_terms):
    matrix = {}
    for number, (i, j) in enumerate(param_pairs):
        matrix[i, j] = normal[number]
        matrix[j, i] = normal[number]
    factor = {}
    inverse_diag = []
    for row_at in range(5):
        for col_at in range(row_at + 1):
            running = matrix[row_at, col_at]
            for inner_k in range(col_at):
                running = running - factor[row_at, inner_k] * factor[col_at, inner_k]
            if row_at == col_at:
                factor[row_at, row_at] = jnp.sqrt(running)
                inverse_diag.append(1.0 / factor[row_at, row_at])
            else:
                factor[row_at, col_at] = running * inverse_diag[col_at]
    forward = []
    for row_at in range(5):
        running = rhs_terms[row_at]
        for inner_k in range(row_at):
            running = running - factor[row_at, inner_k] * forward[inner_k]
        forward.append(running * inverse_diag[row_at])
    backward = [None] * 5
    for row_at in reversed(range(5)):
        running = forward[row_at]
        for inner_k in range(row_at + 1, 5):
            running = running - factor[inner_k, row_at] * backward[inner_k]
        backward[row_at] = running * inverse_diag[row_at]
    return backward


def row_sums(tiles):
    sub = lax.broadcasted_iota(jnp.int32, (8, 128), 0)
    for width in (4, 2, 1):
        mask = (sub & width) == 0
        half = len(tiles) // 2
        folded = []
        for x, y in zip(tiles[:half], tiles[half:]):
            other = jnp.where(mask, y, x)
            if width == 4:
                moved = pltpu.roll(other, 4, 0)
            else:
                moved = jnp.where(mask, pltpu.roll(other, 8 - width, 0), pltpu.roll(other, width, 0))
            folded.append(jnp.where(mask, x, y) + moved)
        tiles = folded
    return tiles[0]


def source_solve_kernel(
    sums_ref, prior_ref, res_ref, live_ref, part_ref, src_ref, frac_ref, interval_ref, dir_ref,
    update_far, pack_ref, base_ref, scale_ref, update_ref, root_ref, corr_ref, sem,
):
    tables = []
    for h in range(2):
        terms = []
        for f in range(20):
            at = (h * 20 + f) * 8
            terms.append(
                (sums_ref[0, at : at + 8, :] + sums_ref[1, at : at + 8, :])
                + (sums_ref[2, at : at + 8, :] + sums_ref[3, at : at + 8, :])
            )
        for number, (i, j) in enumerate(param_pairs):
            if i == j:
                prior = [prior_ref[i : i + 1, (2 * r + h) * 128 : (2 * r + h + 1) * 128] for r in HIGH_ORDER]
                terms[number] = terms[number] + jnp.concatenate(prior, 0)
        solved = cholesky_solve5(terms[:15], terms[15:])
        tables.append(solved)
        for p in range(5):
            for n, r in enumerate(HIGH_ORDER):
                update_ref[p : p + 1, (2 * r + h) * 128 : (2 * r + h + 1) * 128] = solved[p][n : n + 1]
    update_copy = pltpu.make_async_copy(update_ref, update_far, sem)
    update_copy.start()
    root_ref[...] = jnp.sqrt(live_ref[...])
    sub8 = lax.broadcasted_iota(jnp.int32, (8, 128), 0)

    def group(g, carry):
        first = pl.multiple_of(g * 8, 8)
        res8 = res_ref[pl.ds(first, 8), :]
        src8 = src_ref[pl.ds(first, 8), :]
        root8 = root_ref[pl.ds(first, 8), :]
        time8 = (interval_ref[pl.ds(first, 8), :] & 63).astype(jnp.float32) + frac_ref[pl.ds(first, 8), :]
        low8 = src8 & 127
        high8 = src8 >> 8
        place8 = (high8 >> 1) + ((high8 & 1) << 2) + (((src8 >> 7) & 1) << 3)
        pack = pack_ref.at[pl.ds(pl.multiple_of(g * 40, 8), 40), :]
        tiles = []
        for k in range(8):
            at = pl.multiple_of((g * 8 + k) * 128, 128)
            low = jnp.broadcast_to(low8[k : k + 1], (8, 128))
            place = jnp.broadcast_to(place8[k : k + 1], (8, 128))
            part = part_ref[:, pl.ds(at, 128)]
            found = None
            masks = [place == sub8, place == sub8 + 8]
            for p in range(5):
                taken = [jnp.take_along_axis(tables[h][p], low, axis=1, mode="promise_in_bounds") for h in range(2)]
                picked = jnp.where(masks[0], taken[0], jnp.where(masks[1], taken[1], 0.0))
                term = picked * jnp.broadcast_to(part[p : p + 1], (8, 128))
                found = term if found is None else found + term
            tiles.append(found)
            pack[k * 5 + 1 : k * 5 + 4, :] = root8[k : k + 1] * dir_ref[:, pl.ds(at, 128)]
        corr8 = row_sums(tiles)
        corr_ref[pl.ds(first, 8), :] = corr8
        pack[pl.ds(0, 8, stride=5), :] = time8
        pack[pl.ds(4, 8, stride=5), :] = root8 * (res8 - corr8)
        return carry

    lax.fori_loop(0, 16, group, 0, unroll=8)
    live = root_ref[...] > 0.0
    base_ref[...] = res_ref[...] - jnp.where(live, corr_ref[...], 0.0)
    scale_ref[...] = jnp.where(live, 1.0 / jnp.where(live, root_ref[...], 1.0), 0.0)
    update_copy.wait()


def band_sums_kernel(slots_ref, prior_ref, frame_ref, feat_refs, a_refs, acc_ref, prior_pad):
    acc_ref[...] = jnp.zeros_like(acc_ref)
    ids = lax.broadcasted_iota(jnp.int32, (128, 128), 0).astype(jnp.float32).astype(jnp.bfloat16)

    def group(g, a_ref, feat_ref):
        slots = slots_ref.at[pl.ds(pl.multiple_of(g * 40, 8), 40), :]
        time8, d0, d1, d2, fp = [slots[pl.ds(k, 8, stride=5), :] for k in range(5)]
        direction = [d0, d1, d2]
        floor8 = jnp.floor(time8)
        _, splines = spline_weights(time8)
        outer = [direction[i] * direction[j] for i, j in sym_pairs]
        right = [direction[i] * fp for i in range(3)]
        at = 0
        for m, n in spline_pairs:
            coeff = splines[m] * splines[n]
            for entry in outer:
                feat_ref[at : at + 8, :] = coeff * entry
                at += 8
        for m in range(4):
            for entry in right:
                feat_ref[at : at + 8, :] = splines[m] * entry
                at += 8
        hots = []
        for k in range(8):
            for n in range(5):
                size = 16 if n < 4 else 8
                rows = feat_ref[pl.ds(128 * n + k, size, stride=8), :]
                high = rows.astype(jnp.bfloat16)
                rest = rows - high.astype(jnp.float32)
                if n < 4:
                    a_ref[k, 16 * n : 16 * n + 16, :] = high
                    a_ref[k, 64 + 16 * n : 80 + 16 * n, :] = rest.astype(jnp.bfloat16)
                else:
                    a_ref[k, 128:144, :] = jnp.concatenate([high.astype(jnp.float32), rest], 0).astype(jnp.bfloat16)
            hots.append(hot_rows(ids, floor8[k : k + 1]))
        acc_ref[...] += lax.dot_general(side_by_side(a_ref), jnp.concatenate(hots, 1), NT, preferred_element_type=jnp.float32)

    def groups(step, carry):
        for n in range(BAND_UNROLL):
            group(step * BAND_UNROLL + n, a_refs.at[n], feat_refs.at[n])
        return carry

    lax.fori_loop(0, 16 // BAND_UNROLL, groups, 0)
    prior_pad[...] = jnp.zeros_like(prior_pad)
    prior_pad[3:6, 0:64] = prior_ref[...]
    sums = jnp.concatenate([acc_ref[0:64, :] + acc_ref[64:128, :], acc_ref[128:136, :] + acc_ref[136:144, :]], 0)

    def tile(first, count, shift):
        rows = sums[first : first + count]
        return pltpu.roll(jnp.concatenate([rows, jnp.zeros((8 - count, 128), jnp.float32)], 0), shift, 1)

    for d in range(4):
        total = None
        for number, (m, n) in enumerate(spline_pairs):
            if n - m == d:
                term = tile(6 * number, 6, LEFT - 1 + m)
                total = term if total is None else total + term
        frame_ref[d * 8 : d * 8 + 8, :] = total
    total = pltpu.roll(prior_pad[...], LEFT, 1)
    for m in range(4):
        total = total + tile(60 + 3 * m, 3, LEFT - 1 + m)
    frame_ref[32:40, :] = total


def sym_columns(e):
    pad = [jnp.zeros((5, 128), jnp.float32)]
    return [
        jnp.concatenate([e[0], e[1], e[2]] + pad, 0),
        jnp.concatenate([e[1], e[3], e[4]] + pad, 0),
        jnp.concatenate([e[2], e[4], e[5]] + pad, 0),
    ]


def columns_apply(columns, vector):
    total = None
    for j in range(3):
        term = columns[j] * jnp.broadcast_to(vector[j : j + 1], (8, 128))
        total = term if total is None else total + term
    return total


def attitude_kernel(place_ref, own_ref, even_ref, odd_ref, slots_ref, att_far, corr_ref, att_ref, sem, *, knots_total):
    place = place_ref[0]
    lane = lax.broadcasted_iota(jnp.int32, (1, 128), 1)
    lane8 = lax.broadcasted_iota(jnp.int32, (8, 128), 1)
    is_even = place % 2 == 0
    knot = place * 64 + lane - LEFT
    valid = (knot >= 0) & (knot < knots_total)

    def frame(row):
        swap_first = even_ref[row : row + 8, :]
        swap_next = odd_ref[row : row + 8, :]
        left = jnp.where(is_even, swap_next, swap_first)
        right = jnp.where(is_even, swap_first, swap_next)
        return own_ref[row : row + 8, :] + pltpu.roll(jnp.where(lane8 < 64, right, left), 64, 1)

    uppers = [frame(8 * d) for d in range(4)]
    last = frame(32)
    e = [uppers[0][n : n + 1] for n in range(6)]
    e[0] = e[0] + last[3:4]
    e[3] = e[3] + last[4:5]
    e[5] = e[5] + last[5:6]
    c00 = e[3] * e[5] - e[4] * e[4]
    c01 = e[2] * e[4] - e[1] * e[5]
    c02 = e[1] * e[4] - e[2] * e[3]
    c11 = e[0] * e[5] - e[2] * e[2]
    c12 = e[1] * e[2] - e[0] * e[4]
    c22 = e[0] * e[3] - e[1] * e[1]
    determinant = e[0] * c00 + e[1] * c01 + e[2] * c02
    scale = jnp.where(valid, DAMPING / jnp.where(valid, determinant, 1.0), 0.0)
    inverse = sym_columns([c * scale for c in (c00, c01, c02, c11, c12, c22)])
    diag = sym_columns(e)
    upper_cols = [sym_columns([u[n : n + 1] for n in range(6)]) for u in uppers[1:]]
    rhs = last
    att = columns_apply(inverse, rhs)
    for _ in range(1, ITERS_ATT):
        applied = columns_apply(diag, att)
        for d in range(1, 4):
            applied = applied + columns_apply(upper_cols[d - 1], pltpu.roll(att, 128 - d, 1))
            applied = applied + pltpu.roll(columns_apply(upper_cols[d - 1], att), d, 1)
        att = att + columns_apply(inverse, rhs - applied)
    att_ref[...] = pltpu.roll(att, 128 - LEFT, 1)[0:3, 0:64]
    att_copy = pltpu.make_async_copy(att_ref, att_far, sem)
    att_copy.start()
    tables = [jnp.broadcast_to(att[j : j + 1], (8, 128)) for j in range(3)]

    def group(g, carry):
        slots = slots_ref.at[pl.ds(pl.multiple_of(g * 40, 8), 40), :]
        time8, d0, d1, d2 = [slots[pl.ds(k, 8, stride=5), :] for k in range(4)]
        direction = [d0, d1, d2]
        floor8, splines = spline_weights(time8)
        total = jnp.zeros((8, 128), jnp.float32)
        for m in range(4):
            at = floor8 + (LEFT - 1 + m)
            part = None
            for j in range(3):
                term = direction[j] * jnp.take_along_axis(tables[j], at, axis=1, mode="promise_in_bounds")
                part = term if part is None else part + term
            total = total + splines[m] * part
        corr_ref[pl.ds(pl.multiple_of(g * 8, 8), 8), :] = total
        return carry

    lax.fori_loop(0, 16, group, 0, unroll=8)
    att_copy.wait()


def call(kernel, outs, n_in, smem_at=(), scratch=(), far_in=(), far_out=()):
    shapes = [jax.ShapeDtypeStruct(s, jnp.float32) if i in far_out else pltpu.VMEM(s, jnp.float32) for i, s in enumerate(outs)]
    run = pl.pallas_call(
        kernel,
        out_shape=shapes,
        in_specs=[SMEM_SPEC if i in smem_at else VMEM_SPEC for i in range(n_in)],
        out_specs=[ANY_SPEC if i in far_out else VMEM_SPEC for i in range(len(shapes))],
        scratch_shapes=list(scratch),
    )

    def on_chip(*args):
        near = [a if i in smem_at or i in far_in else pltpu.with_memory_space_constraint(a, pltpu.VMEM) for i, a in enumerate(args)]
        return run(*near)

    return on_chip


def body(residual, obs_weight, time_frac, src_partials, att_dir, src_prior, att_prior, obs_source, obs_interval, obs_count):
    devices = lax.axis_size("src") * lax.axis_size("seg")
    square = lambda a: a.reshape(128, 128)
    res, weight, frac, src, interval = map(square, (residual, obs_weight, time_frac, obs_source, obs_interval))
    sums, live = call(
        source_sums_kernel,
        [(4, 320, 128), (128, 128)],
        5,
        (0,),
        [
            pltpu.VMEM((2, 320, 128), jnp.float32),
            pltpu.VMEM((SUMS_UNROLL, 40, 128), jnp.float32),
            pltpu.VMEM((SUMS_UNROLL, 320, 128), jnp.float32),
        ],
        range(1, 5),
    )(obs_count, res, weight, src_partials, src)
    gathered = lax.all_to_all(sums, "seg", split_axis=0, concat_axis=0, tiled=True)
    src_update, packed, base, scale = call(
        source_solve_kernel,
        [(5, 2048), (640, 128), (128, 128), (128, 128)],
        9,
        (),
        [
            pltpu.VMEM((5, 2048), jnp.float32),
            pltpu.VMEM((128, 128), jnp.float32),
            pltpu.VMEM((128, 128), jnp.float32),
            pltpu.SemaphoreType.DMA,
        ],
        (),
        (0,),
    )(gathered, src_prior, res, live, src_partials, src, frac, interval, att_dir)
    arrived = lax.all_to_all(packed.reshape(128, 1, 640), "src", split_axis=0, concat_axis=0, tiled=True).reshape(640, 128)
    (frame,) = call(
        band_sums_kernel,
        [(40, 128)],
        2,
        (),
        [
            pltpu.VMEM((BAND_UNROLL, 576, 128), jnp.float32),
            pltpu.VMEM((BAND_UNROLL, 8, 144, 128), jnp.bfloat16),
            pltpu.VMEM((144, 128), jnp.float32),
            pltpu.VMEM((8, 128), jnp.float32),
        ],
    )(arrived, att_prior)
    both = ("src", "seg")
    swaps = {}
    for start in (1, 0):
        pairs = [(i, i + 1) for i in range(start, devices - 1, 2)]
        swaps[start] = lax.ppermute(frame, both, pairs + [(b, a) for a, b in pairs])
    place = lax.axis_index(both).astype(jnp.int32).reshape(1)
    att_update, correction = call(
        functools.partial(attitude_kernel, knots_total=devices * 64),
        [(3, 64), (128, 128)],
        5,
        (0,),
        [pltpu.VMEM((3, 64), jnp.float32), pltpu.SemaphoreType.DMA],
        (),
        (0,),
    )(place, frame, swaps[0], swaps[1], arrived)
    returned = lax.all_to_all(correction.reshape(128, 1, 128), "src", split_axis=0, concat_axis=0, tiled=True)
    residual_out = base - scale * returned.reshape(128, 128)
    return src_update, att_update, residual_out.reshape(-1)


def solution(mesh):
    pair = ("src", "seg")
    in_specs = (
        P(pair), P(pair), P(pair), P(None, pair), P(None, pair), P(None, "src"), P(None, pair), P(pair), P(pair), P(pair, None),
    )
    out_specs = (P(None, "src"), P(None, pair), P(pair))
    return jax.shard_map(body, mesh=mesh, in_specs=in_specs, out_specs=out_specs, check_vma=False)
```

```python
import functools

import jax
import jax.numpy as jnp
from jax import lax
from jax.experimental import pallas as pl
from jax.experimental.pallas import tpu as pltpu
from jax.sharding import PartitionSpec as P


ITERS_ATT = 6
DAMPING = 0.5
LEFT = 20

param_pairs = [(i, j) for i in range(5) for j in range(i, 5)]
sym_pairs = [(0, 0), (0, 1), (0, 2), (1, 1), (1, 2), (2, 2)]
spline_pairs = [(m, m + d) for d in range(4) for m in range(4 - d)]

VMEM_SPEC = pl.BlockSpec(memory_space=pltpu.VMEM)
SMEM_SPEC = pl.BlockSpec(memory_space=pltpu.SMEM)
ANY_SPEC = pl.BlockSpec(memory_space=pl.ANY)
NT = (((1,), (1,)), ((), ()))
SUMS_UNROLL = 8
BAND_UNROLL = 8


def spline_weights(local_time):
    floor_part = jnp.floor(local_time)
    frac = local_time - floor_part
    square = frac * frac
    cube = square * frac
    rest = 1.0 - frac
    sixth = 1.0 / 6.0
    splines = [
        rest * rest * rest * sixth,
        (3.0 * cube - 6.0 * square + 4.0) * sixth,
        (-3.0 * cube + 3.0 * square + 3.0 * frac + 1.0) * sixth,
        cube * sixth,
    ]
    return floor_part.astype(jnp.int32), splines


def side_by_side(ref):
    return jnp.concatenate([ref[k] for k in range(8)], 1)


def hot_rows(ids, row):
    wide = jnp.broadcast_to(row, (16, 128)).astype(jnp.bfloat16)
    one, zero = jnp.ones((16, 128), jnp.bfloat16), jnp.zeros((16, 128), jnp.bfloat16)
    count = ids.shape[0] // 16
    return jnp.concatenate([jnp.where(ids[16 * n : 16 * n + 16] == wide, one, zero) for n in range(count)], 0)


def source_sums_kernel(
    count_ref, res_ref, weight_ref, part_ref, src_ref, out_ref, live_ref, acc_ref, rows_refs, feat_refs
):
    acc_ref[...] = jnp.zeros_like(acc_ref)
    ids = lax.broadcasted_iota(jnp.int32, (256, 128), 0).astype(jnp.float32).astype(jnp.bfloat16)
    lane8 = lax.broadcasted_iota(jnp.int32, (8, 128), 1)
    sub8 = lax.broadcasted_iota(jnp.int32, (8, 128), 0)
    sub16 = lax.broadcasted_iota(jnp.int32, (16, 128), 0)
    zero = jnp.zeros((16, 128), jnp.bfloat16)

    def group(g, feat_ref, rows_ref):
        first = pl.multiple_of(g * 8, 8)
        res8 = res_ref[pl.ds(first, 8), :]
        src8 = src_ref[pl.ds(first, 8), :]
        low8 = (src8 & 255).astype(jnp.float32)
        high8 = (src8 >> 8).astype(jnp.float32)
        count8 = jnp.zeros((8, 128), jnp.int32)
        for k in range(8):
            count8 = jnp.where(sub8 == k, count_ref[0, g * 8 + k], count8)
            rows_ref[pl.ds(k, 5, stride=8), :] = part_ref[:, pl.ds(pl.multiple_of((g * 8 + k) * 128, 128), 128)]
        weight8 = jnp.where(lane8 < count8, weight_ref[pl.ds(first, 8), :], 0.0)
        live_ref[pl.ds(first, 8), :] = weight8
        part8 = [rows_ref[p * 8 : p * 8 + 8, :] for p in range(5)]
        weighted = [weight8 * p for p in part8]
        features = [weighted[i] * part8[j] for i, j in param_pairs] + [weighted[i] * res8 for i in range(5)]
        for f, feature in enumerate(features):
            high = feature.astype(jnp.bfloat16).astype(jnp.float32)
            feat_ref[f * 8 : f * 8 + 8, :] = high
            feat_ref[160 + f * 8 : 168 + f * 8, :] = feature - high
        hots = []
        blocks = []
        for k in range(8):
            body = [feat_ref[pl.ds(128 * n + k, 16, stride=8), :].astype(jnp.bfloat16) for n in range(2)]
            tail = feat_ref[pl.ds(256 + k, 8, stride=8), :]
            tail = jnp.concatenate([tail, tail], 0).astype(jnp.bfloat16)
            high = jnp.broadcast_to(high8[k : k + 1], (16, 128)).astype(jnp.bfloat16)
            tiles = []
            for pair in range(4):
                for e in range(2):
                    mask = high == jnp.bfloat16(2 * pair + e)
                    tiles.append(jnp.where(mask, body[0], zero))
                    tiles.append(jnp.where(mask, body[1], zero))
                mixed = jnp.where(sub16 < 8, 2.0 * pair, 2.0 * pair + 1.0).astype(jnp.bfloat16)
                tiles.append(jnp.where(high == mixed, tail, zero))
            blocks.append(jnp.concatenate(tiles, 0))
            hots.append(hot_rows(ids, low8[k : k + 1]))
        sums = lax.dot_general(jnp.concatenate(blocks, 1), jnp.concatenate(hots, 1), NT, preferred_element_type=jnp.float32)
        for h in range(2):
            acc_ref[h] += sums[:, h * 128 : (h + 1) * 128]

    def groups(step, carry):
        for n in range(SUMS_UNROLL):
            group(step * SUMS_UNROLL + n, feat_refs.at[n], rows_refs.at[n])
        return carry

    lax.fori_loop(0, 16 // SUMS_UNROLL, groups, 0)

    def rows_of(q, e, h):
        at = 32 * e + q if q < 32 else 64 + 8 * e + q - 32
        return acc_ref[h, pl.ds(at, 4, stride=80), :]

    for f in range(20):
        for h in range(2):
            total = jnp.concatenate([rows_of(f, e, h) + rows_of(20 + f, e, h) for e in range(2)], 0)
            for q in range(4):
                out_ref[q, (h * 20 + f) * 8 : (h * 20 + f) * 8 + 8, :] = total


HIGH_ORDER = (0, 2, 4, 6, 1, 3, 5, 7)


def cholesky_solve5(normal, rhs_terms):
    matrix = {}
    for number, (i, j) in enumerate(param_pairs):
        matrix[i, j] = normal[number]
        matrix[j, i] = normal[number]
    factor = {}
    inverse_diag = []
    for row_at in range(5):
        for col_at in range(row_at + 1):
            running = matrix[row_at, col_at]
            for inner_k in range(col_at):
                running = running - factor[row_at, inner_k] * factor[col_at, inner_k]
            if row_at == col_at:
                factor[row_at, row_at] = jnp.sqrt(running)
                inverse_diag.append(1.0 / factor[row_at, row_at])
            else:
                factor[row_at, col_at] = running * inverse_diag[col_at]
    forward = []
    for row_at in range(5):
        running = rhs_terms[row_at]
        for inner_k in range(row_at):
            running = running - factor[row_at, inner_k] * forward[inner_k]
        forward.append(running * inverse_diag[row_at])
    backward = [None] * 5
    for row_at in reversed(range(5)):
        running = forward[row_at]
        for inner_k in range(row_at + 1, 5):
            running = running - factor[inner_k, row_at] * backward[inner_k]
        backward[row_at] = running * inverse_diag[row_at]
    return backward


def row_sums(tiles):
    sub = lax.broadcasted_iota(jnp.int32, (8, 128), 0)
    for width in (4, 2, 1):
        mask = (sub & width) == 0
        half = len(tiles) // 2
        folded = []
        for x, y in zip(tiles[:half], tiles[half:]):
            other = jnp.where(mask, y, x)
            if width == 4:
                moved = pltpu.roll(other, 4, 0)
            else:
                moved = jnp.where(mask, pltpu.roll(other, 8 - width, 0), pltpu.roll(other, width, 0))
            folded.append(jnp.where(mask, x, y) + moved)
        tiles = folded
    return tiles[0]


def source_solve_kernel(
    sums_ref, prior_ref, res_ref, live_ref, part_ref, src_ref, frac_ref, interval_ref, dir_ref,
    update_far, pack_ref, base_ref, scale_ref, update_ref, root_ref, corr_ref, sem,
):
    tables = []
    for h in range(2):
        terms = []
        for f in range(20):
            at = (h * 20 + f) * 8
            terms.append(
                (sums_ref[0, at : at + 8, :] + sums_ref[1, at : at + 8, :])
                + (sums_ref[2, at : at + 8, :] + sums_ref[3, at : at + 8, :])
            )
        for number, (i, j) in enumerate(param_pairs):
            if i == j:
                prior = [prior_ref[i : i + 1, (2 * r + h) * 128 : (2 * r + h + 1) * 128] for r in HIGH_ORDER]
                terms[number] = terms[number] + jnp.concatenate(prior, 0)
        solved = cholesky_solve5(terms[:15], terms[15:])
        tables.append(solved)
        for p in range(5):
            for n, r in enumerate(HIGH_ORDER):
                update_ref[p : p + 1, (2 * r + h) * 128 : (2 * r + h + 1) * 128] = solved[p][n : n + 1]
    update_copy = pltpu.make_async_copy(update_ref, update_far, sem)
    update_copy.start()
    root_ref[...] = jnp.sqrt(live_ref[...])
    sub8 = lax.broadcasted_iota(jnp.int32, (8, 128), 0)

    def group(g, carry):
        first = pl.multiple_of(g * 8, 8)
        res8 = res_ref[pl.ds(first, 8), :]
        src8 = src_ref[pl.ds(first, 8), :]
        root8 = root_ref[pl.ds(first, 8), :]
        time8 = (interval_ref[pl.ds(first, 8), :] & 63).astype(jnp.float32) + frac_ref[pl.ds(first, 8), :]
        low8 = src8 & 127
        high8 = src8 >> 8
        place8 = (high8 >> 1) + ((high8 & 1) << 2) + (((src8 >> 7) & 1) << 3)
        pack = pack_ref.at[pl.ds(pl.multiple_of(g * 40, 8), 40), :]
        tiles = []
        for k in range(8):
            at = pl.multiple_of((g * 8 + k) * 128, 128)
            low = jnp.broadcast_to(low8[k : k + 1], (8, 128))
            place = jnp.broadcast_to(place8[k : k + 1], (8, 128))
            part = part_ref[:, pl.ds(at, 128)]
            found = None
            masks = [place == sub8, place == sub8 + 8]
            for p in range(5):
                taken = [jnp.take_along_axis(tables[h][p], low, axis=1, mode="promise_in_bounds") for h in range(2)]
                picked = jnp.where(masks[0], taken[0], jnp.where(masks[1], taken[1], 0.0))
                term = picked * jnp.broadcast_to(part[p : p + 1], (8, 128))
                found = term if found is None else found + term
            tiles.append(found)
            pack[k * 5 + 1 : k * 5 + 4, :] = root8[k : k + 1] * dir_ref[:, pl.ds(at, 128)]
        corr8 = row_sums(tiles)
        corr_ref[pl.ds(first, 8), :] = corr8
        pack[pl.ds(0, 8, stride=5), :] = time8
        pack[pl.ds(4, 8, stride=5), :] = root8 * (res8 - corr8)
        return carry

    lax.fori_loop(0, 16, group, 0, unroll=8)
    live = root_ref[...] > 0.0
    base_ref[...] = res_ref[...] - jnp.where(live, corr_ref[...], 0.0)
    scale_ref[...] = jnp.where(live, 1.0 / jnp.where(live, root_ref[...], 1.0), 0.0)
    update_copy.wait()


def band_sums_kernel(slots_ref, prior_ref, frame_ref, feat_refs, a_refs, acc_ref, prior_pad):
    acc_ref[...] = jnp.zeros_like(acc_ref)
    ids = lax.broadcasted_iota(jnp.int32, (128, 128), 0).astype(jnp.float32).astype(jnp.bfloat16)

    def group(g, a_ref, feat_ref):
        slots = slots_ref.at[pl.ds(pl.multiple_of(g * 40, 8), 40), :]
        time8, d0, d1, d2, fp = [slots[pl.ds(k, 8, stride=5), :] for k in range(5)]
        direction = [d0, d1, d2]
        floor8 = jnp.floor(time8)
        _, splines = spline_weights(time8)
        outer = [direction[i] * direction[j] for i, j in sym_pairs]
        right = [direction[i] * fp for i in range(3)]
        at = 0
        for m, n in spline_pairs:
            coeff = splines[m] * splines[n]
            for entry in outer:
                feat_ref[at : at + 8, :] = coeff * entry
                at += 8
        for m in range(4):
            for entry in right:
                feat_ref[at : at + 8, :] = splines[m] * entry
                at += 8
        hots = []
        for k in range(8):
            for n in range(5):
                size = 16 if n < 4 else 8
                rows = feat_ref[pl.ds(128 * n + k, size, stride=8), :]
                high = rows.astype(jnp.bfloat16)
                rest = rows - high.astype(jnp.float32)
                if n < 4:
                    a_ref[k, 16 * n : 16 * n + 16, :] = high
                    a_ref[k, 64 + 16 * n : 80 + 16 * n, :] = rest.astype(jnp.bfloat16)
                else:
                    a_ref[k, 128:144, :] = jnp.concatenate([high.astype(jnp.float32), rest], 0).astype(jnp.bfloat16)
            hots.append(hot_rows(ids, floor8[k : k + 1]))
        acc_ref[...] += lax.dot_general(side_by_side(a_ref), jnp.concatenate(hots, 1), NT, preferred_element_type=jnp.float32)

    def groups(step, carry):
        for n in range(BAND_UNROLL):
            group(step * BAND_UNROLL + n, a_refs.at[n], feat_refs.at[n])
        return carry

    lax.fori_loop(0, 16 // BAND_UNROLL, groups, 0)
    prior_pad[...] = jnp.zeros_like(prior_pad)
    prior_pad[3:6, 0:64] = prior_ref[...]
    sums = jnp.concatenate([acc_ref[0:64, :] + acc_ref[64:128, :], acc_ref[128:136, :] + acc_ref[136:144, :]], 0)

    def tile(first, count, shift):
        rows = sums[first : first + count]
        return pltpu.roll(jnp.concatenate([rows, jnp.zeros((8 - count, 128), jnp.float32)], 0), shift, 1)

    for d in range(4):
        total = None
        for number, (m, n) in enumerate(spline_pairs):
            if n - m == d:
                term = tile(6 * number, 6, LEFT - 1 + m)
                total = term if total is None else total + term
        frame_ref[d * 8 : d * 8 + 8, :] = total
    total = pltpu.roll(prior_pad[...], LEFT, 1)
    for m in range(4):
        total = total + tile(60 + 3 * m, 3, LEFT - 1 + m)
    frame_ref[32:40, :] = total


def sym_columns(e):
    pad = [jnp.zeros((5, 128), jnp.float32)]
    return [
        jnp.concatenate([e[0], e[1], e[2]] + pad, 0),
        jnp.concatenate([e[1], e[3], e[4]] + pad, 0),
        jnp.concatenate([e[2], e[4], e[5]] + pad, 0),
    ]


def columns_apply(columns, vector):
    total = None
    for j in range(3):
        term = columns[j] * jnp.broadcast_to(vector[j : j + 1], (8, 128))
        total = term if total is None else total + term
    return total


def attitude_kernel(place_ref, own_ref, even_ref, odd_ref, slots_ref, att_ref, corr_ref, *, knots_total):
    place = place_ref[0]
    lane = lax.broadcasted_iota(jnp.int32, (1, 128), 1)
    lane8 = lax.broadcasted_iota(jnp.int32, (8, 128), 1)
    is_even = place % 2 == 0
    knot = place * 64 + lane - LEFT
    valid = (knot >= 0) & (knot < knots_total)

    def frame(row):
        swap_first = even_ref[row : row + 8, :]
        swap_next = odd_ref[row : row + 8, :]
        left = jnp.where(is_even, swap_next, swap_first)
        right = jnp.where(is_even, swap_first, swap_next)
        return own_ref[row : row + 8, :] + pltpu.roll(jnp.where(lane8 < 64, right, left), 64, 1)

    uppers = [frame(8 * d) for d in range(4)]
    last = frame(32)
    e = [uppers[0][n : n + 1] for n in range(6)]
    e[0] = e[0] + last[3:4]
    e[3] = e[3] + last[4:5]
    e[5] = e[5] + last[5:6]
    c00 = e[3] * e[5] - e[4] * e[4]
    c01 = e[2] * e[4] - e[1] * e[5]
    c02 = e[1] * e[4] - e[2] * e[3]
    c11 = e[0] * e[5] - e[2] * e[2]
    c12 = e[1] * e[2] - e[0] * e[4]
    c22 = e[0] * e[3] - e[1] * e[1]
    determinant = e[0] * c00 + e[1] * c01 + e[2] * c02
    scale = jnp.where(valid, DAMPING / jnp.where(valid, determinant, 1.0), 0.0)
    inverse = sym_columns([c * scale for c in (c00, c01, c02, c11, c12, c22)])
    diag = sym_columns(e)
    upper_cols = [sym_columns([u[n : n + 1] for n in range(6)]) for u in uppers[1:]]
    rhs = last
    att = columns_apply(inverse, rhs)
    for _ in range(1, ITERS_ATT):
        applied = columns_apply(diag, att)
        for d in range(1, 4):
            applied = applied + columns_apply(upper_cols[d - 1], pltpu.roll(att, 128 - d, 1))
            applied = applied + pltpu.roll(columns_apply(upper_cols[d - 1], att), d, 1)
        att = att + columns_apply(inverse, rhs - applied)
    att_ref[...] = pltpu.roll(att, 128 - LEFT, 1)[0:3, 0:64]
    tables = [jnp.broadcast_to(att[j : j + 1], (8, 128)) for j in range(3)]

    def group(g, carry):
        slots = slots_ref.at[pl.ds(pl.multiple_of(g * 40, 8), 40), :]
        time8, d0, d1, d2 = [slots[pl.ds(k, 8, stride=5), :] for k in range(4)]
        direction = [d0, d1, d2]
        floor8, splines = spline_weights(time8)
        total = jnp.zeros((8, 128), jnp.float32)
        for m in range(4):
            at = floor8 + (LEFT - 1 + m)
            part = None
            for j in range(3):
                term = direction[j] * jnp.take_along_axis(tables[j], at, axis=1, mode="promise_in_bounds")
                part = term if part is None else part + term
            total = total + splines[m] * part
        corr_ref[pl.ds(pl.multiple_of(g * 8, 8), 8), :] = total
        return carry

    lax.fori_loop(0, 16, group, 0, unroll=8)


def finish_kernel(base_ref, scale_ref, returned_ref, att_ref, residual_far, att_far, residual_ref, sems):
    att_copy = pltpu.make_async_copy(att_ref, att_far, sems.at[0])
    att_copy.start()
    residual_ref[...] = base_ref[...] - scale_ref[...] * returned_ref[...]
    residual_copy = pltpu.make_async_copy(residual_ref, residual_far, sems.at[1])
    residual_copy.start()
    att_copy.wait()
    residual_copy.wait()


def call(kernel, outs, n_in, smem_at=(), scratch=(), far_in=(), far_out=()):
    shapes = [jax.ShapeDtypeStruct(s, jnp.float32) if i in far_out else pltpu.VMEM(s, jnp.float32) for i, s in enumerate(outs)]
    run = pl.pallas_call(
        kernel,
        out_shape=shapes,
        in_specs=[SMEM_SPEC if i in smem_at else VMEM_SPEC for i in range(n_in)],
        out_specs=[ANY_SPEC if i in far_out else VMEM_SPEC for i in range(len(shapes))],
        scratch_shapes=list(scratch),
    )

    def on_chip(*args):
        near = [a if i in smem_at or i in far_in else pltpu.with_memory_space_constraint(a, pltpu.VMEM) for i, a in enumerate(args)]
        return run(*near)

    return on_chip


def body(residual, obs_weight, time_frac, src_partials, att_dir, src_prior, att_prior, obs_source, obs_interval, obs_count):
    devices = lax.axis_size("src") * lax.axis_size("seg")
    square = lambda a: a.reshape(128, 128)
    res, weight, frac, src, interval = map(square, (residual, obs_weight, time_frac, obs_source, obs_interval))
    sums, live = call(
        source_sums_kernel,
        [(4, 320, 128), (128, 128)],
        5,
        (0,),
        [
            pltpu.VMEM((2, 320, 128), jnp.float32),
            pltpu.VMEM((SUMS_UNROLL, 40, 128), jnp.float32),
            pltpu.VMEM((SUMS_UNROLL, 320, 128), jnp.float32),
        ],
        range(1, 5),
    )(obs_count, res, weight, src_partials, src)
    gathered = lax.all_to_all(sums, "seg", split_axis=0, concat_axis=0, tiled=True)
    src_update, packed, base, scale = call(
        source_solve_kernel,
        [(5, 2048), (640, 128), (128, 128), (128, 128)],
        9,
        (),
        [
            pltpu.VMEM((5, 2048), jnp.float32),
            pltpu.VMEM((128, 128), jnp.float32),
            pltpu.VMEM((128, 128), jnp.float32),
            pltpu.SemaphoreType.DMA,
        ],
        (),
        (0,),
    )(gathered, src_prior, res, live, src_partials, src, frac, interval, att_dir)
    arrived = lax.all_to_all(packed.reshape(128, 1, 640), "src", split_axis=0, concat_axis=0, tiled=True).reshape(640, 128)
    (frame,) = call(
        band_sums_kernel,
        [(40, 128)],
        2,
        (),
        [
            pltpu.VMEM((BAND_UNROLL, 576, 128), jnp.float32),
            pltpu.VMEM((BAND_UNROLL, 8, 144, 128), jnp.bfloat16),
            pltpu.VMEM((144, 128), jnp.float32),
            pltpu.VMEM((8, 128), jnp.float32),
        ],
    )(arrived, att_prior)
    both = ("src", "seg")
    swaps = {}
    for start in (1, 0):
        pairs = [(i, i + 1) for i in range(start, devices - 1, 2)]
        swaps[start] = lax.ppermute(frame, both, pairs + [(b, a) for a, b in pairs])
    place = lax.axis_index(both).astype(jnp.int32).reshape(1)
    att_update, correction = call(
        functools.partial(attitude_kernel, knots_total=devices * 64), [(3, 64), (128, 128)], 5, (0,), ()
    )(place, frame, swaps[0], swaps[1], arrived)
    returned = lax.all_to_all(correction.reshape(128, 1, 128), "src", split_axis=0, concat_axis=0, tiled=True)
    residual_out, att_out = call(
        finish_kernel,
        [(128, 128), (3, 64)],
        4,
        (),
        [pltpu.VMEM((128, 128), jnp.float32), pltpu.SemaphoreType.DMA((2,))],
        (),
        (0, 1),
    )(base, scale, returned.reshape(128, 128), att_update)
    return src_update, att_out, residual_out.reshape(-1)


def solution(mesh):
    pair = ("src", "seg")
    in_specs = (
        P(pair), P(pair), P(pair), P(None, pair), P(None, pair), P(None, "src"), P(None, pair), P(pair), P(pair), P(pair, None),
    )
    out_specs = (P(None, "src"), P(None, pair), P(pair))
    return jax.shard_map(body, mesh=mesh, in_specs=in_specs, out_specs=out_specs, check_vma=False)
```

```python
import functools

import jax
import jax.numpy as jnp
from jax import lax
from jax.experimental import pallas as pl
from jax.experimental.pallas import tpu as pltpu
from jax.sharding import PartitionSpec as P


ITERS_ATT = 6
DAMPING = 0.5
LEFT = 20

param_pairs = [(i, j) for i in range(5) for j in range(i, 5)]
sym_pairs = [(0, 0), (0, 1), (0, 2), (1, 1), (1, 2), (2, 2)]
spline_pairs = [(m, m + d) for d in range(4) for m in range(4 - d)]

VMEM_SPEC = pl.BlockSpec(memory_space=pltpu.VMEM)
SMEM_SPEC = pl.BlockSpec(memory_space=pltpu.SMEM)
ANY_SPEC = pl.BlockSpec(memory_space=pl.ANY)
NT = (((1,), (1,)), ((), ()))
SUMS_UNROLL = 8
BAND_UNROLL = 8


def spline_weights(local_time):
    floor_part = jnp.floor(local_time)
    frac = local_time - floor_part
    square = frac * frac
    cube = square * frac
    rest = 1.0 - frac
    sixth = 1.0 / 6.0
    splines = [
        rest * rest * rest * sixth,
        (3.0 * cube - 6.0 * square + 4.0) * sixth,
        (-3.0 * cube + 3.0 * square + 3.0 * frac + 1.0) * sixth,
        cube * sixth,
    ]
    return floor_part.astype(jnp.int32), splines


def side_by_side(ref):
    return jnp.concatenate([ref[k] for k in range(8)], 1)


def hot_rows(ids, row):
    wide = jnp.broadcast_to(row, (16, 128)).astype(jnp.bfloat16)
    one, zero = jnp.ones((16, 128), jnp.bfloat16), jnp.zeros((16, 128), jnp.bfloat16)
    count = ids.shape[0] // 16
    return jnp.concatenate([jnp.where(ids[16 * n : 16 * n + 16] == wide, one, zero) for n in range(count)], 0)


def source_sums_kernel(
    count_ref, res_ref, weight_ref, part_ref, src_ref, out_ref, live_ref, acc_ref, rows_refs, feat_refs
):
    acc_ref[...] = jnp.zeros_like(acc_ref)
    ids = lax.broadcasted_iota(jnp.int32, (256, 128), 0).astype(jnp.float32).astype(jnp.bfloat16)
    lane8 = lax.broadcasted_iota(jnp.int32, (8, 128), 1)
    sub8 = lax.broadcasted_iota(jnp.int32, (8, 128), 0)
    sub16 = lax.broadcasted_iota(jnp.int32, (16, 128), 0)
    zero = jnp.zeros((16, 128), jnp.bfloat16)

    def group(g, feat_ref, rows_ref):
        first = pl.multiple_of(g * 8, 8)
        res8 = res_ref[pl.ds(first, 8), :]
        src8 = src_ref[pl.ds(first, 8), :]
        low8 = (src8 & 255).astype(jnp.float32)
        high8 = (src8 >> 8).astype(jnp.float32)
        count8 = jnp.zeros((8, 128), jnp.int32)
        for k in range(8):
            count8 = jnp.where(sub8 == k, count_ref[0, g * 8 + k], count8)
            rows_ref[pl.ds(k, 5, stride=8), :] = part_ref[:, pl.ds(pl.multiple_of((g * 8 + k) * 128, 128), 128)]
        weight8 = jnp.where(lane8 < count8, weight_ref[pl.ds(first, 8), :], 0.0)
        live_ref[pl.ds(first, 8), :] = weight8
        part8 = [rows_ref[p * 8 : p * 8 + 8, :] for p in range(5)]
        weighted = [weight8 * p for p in part8]
        features = [weighted[i] * part8[j] for i, j in param_pairs] + [weighted[i] * res8 for i in range(5)]
        for f, feature in enumerate(features):
            high = feature.astype(jnp.bfloat16).astype(jnp.float32)
            feat_ref[f * 8 : f * 8 + 8, :] = high
            feat_ref[160 + f * 8 : 168 + f * 8, :] = feature - high
        hots = []
        blocks = []
        for k in range(8):
            body = [feat_ref[pl.ds(128 * n + k, 16, stride=8), :].astype(jnp.bfloat16) for n in range(2)]
            tail = feat_ref[pl.ds(256 + k, 8, stride=8), :]
            tail = jnp.concatenate([tail, tail], 0).astype(jnp.bfloat16)
            high = jnp.broadcast_to(high8[k : k + 1], (16, 128)).astype(jnp.bfloat16)
            tiles = []
            for pair in range(4):
                for e in range(2):
                    mask = high == jnp.bfloat16(2 * pair + e)
                    tiles.append(jnp.where(mask, body[0], zero))
                    tiles.append(jnp.where(mask, body[1], zero))
                mixed = jnp.where(sub16 < 8, 2.0 * pair, 2.0 * pair + 1.0).astype(jnp.bfloat16)
                tiles.append(jnp.where(high == mixed, tail, zero))
            blocks.append(jnp.concatenate(tiles, 0))
            hots.append(hot_rows(ids, low8[k : k + 1]))
        sums = lax.dot_general(jnp.concatenate(blocks, 1), jnp.concatenate(hots, 1), NT, preferred_element_type=jnp.float32)
        for h in range(2):
            acc_ref[h] += sums[:, h * 128 : (h + 1) * 128]

    def groups(step, carry):
        for n in range(SUMS_UNROLL):
            group(step * SUMS_UNROLL + n, feat_refs.at[n], rows_refs.at[n])
        return carry

    lax.fori_loop(0, 16 // SUMS_UNROLL, groups, 0)

    def rows_of(q, e, h):
        at = 32 * e + q if q < 32 else 64 + 8 * e + q - 32
        return acc_ref[h, pl.ds(at, 4, stride=80), :]

    for f in range(20):
        for h in range(2):
            total = jnp.concatenate([rows_of(f, e, h) + rows_of(20 + f, e, h) for e in range(2)], 0)
            for q in range(4):
                out_ref[q, (h * 20 + f) * 8 : (h * 20 + f) * 8 + 8, :] = total


HIGH_ORDER = (0, 2, 4, 6, 1, 3, 5, 7)


def cholesky_solve5(normal, rhs_terms):
    matrix = {}
    for number, (i, j) in enumerate(param_pairs):
        matrix[i, j] = normal[number]
        matrix[j, i] = normal[number]
    factor = {}
    inverse_diag = []
    for row_at in range(5):
        for col_at in range(row_at + 1):
            running = matrix[row_at, col_at]
            for inner_k in range(col_at):
                running = running - factor[row_at, inner_k] * factor[col_at, inner_k]
            if row_at == col_at:
                factor[row_at, row_at] = jnp.sqrt(running)
                inverse_diag.append(1.0 / factor[row_at, row_at])
            else:
                factor[row_at, col_at] = running * inverse_diag[col_at]
    forward = []
    for row_at in range(5):
        running = rhs_terms[row_at]
        for inner_k in range(row_at):
            running = running - factor[row_at, inner_k] * forward[inner_k]
        forward.append(running * inverse_diag[row_at])
    backward = [None] * 5
    for row_at in reversed(range(5)):
        running = forward[row_at]
        for inner_k in range(row_at + 1, 5):
            running = running - factor[inner_k, row_at] * backward[inner_k]
        backward[row_at] = running * inverse_diag[row_at]
    return backward


def row_sums(tiles):
    sub = lax.broadcasted_iota(jnp.int32, (8, 128), 0)
    for width in (4, 2, 1):
        mask = (sub & width) == 0
        half = len(tiles) // 2
        folded = []
        for x, y in zip(tiles[:half], tiles[half:]):
            other = jnp.where(mask, y, x)
            if width == 4:
                moved = pltpu.roll(other, 4, 0)
            else:
                moved = jnp.where(mask, pltpu.roll(other, 8 - width, 0), pltpu.roll(other, width, 0))
            folded.append(jnp.where(mask, x, y) + moved)
        tiles = folded
    return tiles[0]


def source_solve_kernel(
    sums_ref, prior_ref, res_ref, live_ref, part_ref, src_ref, frac_ref, interval_ref, dir_ref,
    update_far, pack_ref, base_ref, scale_ref, update_ref, root_ref, corr_ref, sem,
):
    tables = []
    for h in range(2):
        terms = []
        for f in range(20):
            at = (h * 20 + f) * 8
            terms.append(
                (sums_ref[0, at : at + 8, :] + sums_ref[1, at : at + 8, :])
                + (sums_ref[2, at : at + 8, :] + sums_ref[3, at : at + 8, :])
            )
        for number, (i, j) in enumerate(param_pairs):
            if i == j:
                prior = [prior_ref[i : i + 1, (2 * r + h) * 128 : (2 * r + h + 1) * 128] for r in HIGH_ORDER]
                terms[number] = terms[number] + jnp.concatenate(prior, 0)
        solved = cholesky_solve5(terms[:15], terms[15:])
        tables.append(solved)
        for p in range(5):
            for n, r in enumerate(HIGH_ORDER):
                update_ref[p : p + 1, (2 * r + h) * 128 : (2 * r + h + 1) * 128] = solved[p][n : n + 1]
    update_copy = pltpu.make_async_copy(update_ref, update_far, sem)
    update_copy.start()
    root_ref[...] = jnp.sqrt(live_ref[...])
    sub8 = lax.broadcasted_iota(jnp.int32, (8, 128), 0)

    def group(g, carry):
        first = pl.multiple_of(g * 8, 8)
        res8 = res_ref[pl.ds(first, 8), :]
        src8 = src_ref[pl.ds(first, 8), :]
        root8 = root_ref[pl.ds(first, 8), :]
        time8 = (interval_ref[pl.ds(first, 8), :] & 63).astype(jnp.float32) + frac_ref[pl.ds(first, 8), :]
        low8 = src8 & 127
        high8 = src8 >> 8
        place8 = (high8 >> 1) + ((high8 & 1) << 2) + (((src8 >> 7) & 1) << 3)
        pack = pack_ref.at[pl.ds(pl.multiple_of(g * 40, 8), 40), :]
        tiles = []
        for k in range(8):
            at = pl.multiple_of((g * 8 + k) * 128, 128)
            low = jnp.broadcast_to(low8[k : k + 1], (8, 128))
            place = jnp.broadcast_to(place8[k : k + 1], (8, 128))
            part = part_ref[:, pl.ds(at, 128)]
            found = None
            masks = [place == sub8, place == sub8 + 8]
            for p in range(5):
                taken = [jnp.take_along_axis(tables[h][p], low, axis=1, mode="promise_in_bounds") for h in range(2)]
                picked = jnp.where(masks[0], taken[0], jnp.where(masks[1], taken[1], 0.0))
                term = picked * jnp.broadcast_to(part[p : p + 1], (8, 128))
                found = term if found is None else found + term
            tiles.append(found)
            pack[k * 5 + 1 : k * 5 + 4, :] = root8[k : k + 1] * dir_ref[:, pl.ds(at, 128)]
        corr8 = row_sums(tiles)
        corr_ref[pl.ds(first, 8), :] = corr8
        pack[pl.ds(0, 8, stride=5), :] = time8
        pack[pl.ds(4, 8, stride=5), :] = root8 * (res8 - corr8)
        return carry

    lax.fori_loop(0, 16, group, 0, unroll=8)
    live = root_ref[...] > 0.0
    base_ref[...] = res_ref[...] - jnp.where(live, corr_ref[...], 0.0)
    scale_ref[...] = jnp.where(live, 1.0 / jnp.where(live, root_ref[...], 1.0), 0.0)
    update_copy.wait()


def band_sums_kernel(slots_ref, prior_ref, frame_ref, feat_refs, a_refs, acc_ref, prior_pad):
    acc_ref[...] = jnp.zeros_like(acc_ref)
    ids = lax.broadcasted_iota(jnp.int32, (128, 128), 0).astype(jnp.float32).astype(jnp.bfloat16)

    def group(g, a_ref, feat_ref):
        slots = slots_ref.at[pl.ds(pl.multiple_of(g * 40, 8), 40), :]
        time8, d0, d1, d2, fp = [slots[pl.ds(k, 8, stride=5), :] for k in range(5)]
        direction = [d0, d1, d2]
        floor8 = jnp.floor(time8)
        _, splines = spline_weights(time8)
        outer = [direction[i] * direction[j] for i, j in sym_pairs]
        right = [direction[i] * fp for i in range(3)]
        at = 0
        for m, n in spline_pairs:
            coeff = splines[m] * splines[n]
            for entry in outer:
                feat_ref[at : at + 8, :] = coeff * entry
                at += 8
        for m in range(4):
            for entry in right:
                feat_ref[at : at + 8, :] = splines[m] * entry
                at += 8
        hots = []
        for k in range(8):
            for n in range(5):
                size = 16 if n < 4 else 8
                rows = feat_ref[pl.ds(128 * n + k, size, stride=8), :]
                high = rows.astype(jnp.bfloat16)
                rest = rows - high.astype(jnp.float32)
                if n < 4:
                    a_ref[k, 16 * n : 16 * n + 16, :] = high
                    a_ref[k, 64 + 16 * n : 80 + 16 * n, :] = rest.astype(jnp.bfloat16)
                else:
                    a_ref[k, 128:144, :] = jnp.concatenate([high.astype(jnp.float32), rest], 0).astype(jnp.bfloat16)
            hots.append(hot_rows(ids, floor8[k : k + 1]))
        acc_ref[...] += lax.dot_general(side_by_side(a_ref), jnp.concatenate(hots, 1), NT, preferred_element_type=jnp.float32)

    def groups(step, carry):
        for n in range(BAND_UNROLL):
            group(step * BAND_UNROLL + n, a_refs.at[n], feat_refs.at[n])
        return carry

    lax.fori_loop(0, 16 // BAND_UNROLL, groups, 0)
    prior_pad[...] = jnp.zeros_like(prior_pad)
    prior_pad[3:6, 0:64] = prior_ref[...]
    sums = jnp.concatenate([acc_ref[0:64, :] + acc_ref[64:128, :], acc_ref[128:136, :] + acc_ref[136:144, :]], 0)

    def tile(first, count, shift):
        rows = sums[first : first + count]
        return pltpu.roll(jnp.concatenate([rows, jnp.zeros((8 - count, 128), jnp.float32)], 0), shift, 1)

    for d in range(4):
        total = None
        for number, (m, n) in enumerate(spline_pairs):
            if n - m == d:
                term = tile(6 * number, 6, LEFT - 1 + m)
                total = term if total is None else total + term
        frame_ref[d * 8 : d * 8 + 8, :] = total
    total = pltpu.roll(prior_pad[...], LEFT, 1)
    for m in range(4):
        total = total + tile(60 + 3 * m, 3, LEFT - 1 + m)
    frame_ref[32:40, :] = total


def sym_columns(e):
    pad = [jnp.zeros((5, 128), jnp.float32)]
    return [
        jnp.concatenate([e[0], e[1], e[2]] + pad, 0),
        jnp.concatenate([e[1], e[3], e[4]] + pad, 0),
        jnp.concatenate([e[2], e[4], e[5]] + pad, 0),
    ]


def columns_apply(columns, vector):
    total = None
    for j in range(3):
        term = columns[j] * jnp.broadcast_to(vector[j : j + 1], (8, 128))
        total = term if total is None else total + term
    return total


def attitude_kernel(own_ref, even_ref, odd_ref, slots_ref, att_ref, corr_ref, *, knots_total):
    place = lax.axis_index(("src", "seg"))
    lane = lax.broadcasted_iota(jnp.int32, (1, 128), 1)
    lane8 = lax.broadcasted_iota(jnp.int32, (8, 128), 1)
    is_even = place % 2 == 0
    knot = place * 64 + lane - LEFT
    valid = (knot >= 0) & (knot < knots_total)

    def frame(row):
        swap_first = even_ref[row : row + 8, :]
        swap_next = odd_ref[row : row + 8, :]
        left = jnp.where(is_even, swap_next, swap_first)
        right = jnp.where(is_even, swap_first, swap_next)
        return own_ref[row : row + 8, :] + pltpu.roll(jnp.where(lane8 < 64, right, left), 64, 1)

    uppers = [frame(8 * d) for d in range(4)]
    last = frame(32)
    e = [uppers[0][n : n + 1] for n in range(6)]
    e[0] = e[0] + last[3:4]
    e[3] = e[3] + last[4:5]
    e[5] = e[5] + last[5:6]
    c00 = e[3] * e[5] - e[4] * e[4]
    c01 = e[2] * e[4] - e[1] * e[5]
    c02 = e[1] * e[4] - e[2] * e[3]
    c11 = e[0] * e[5] - e[2] * e[2]
    c12 = e[1] * e[2] - e[0] * e[4]
    c22 = e[0] * e[3] - e[1] * e[1]
    determinant = e[0] * c00 + e[1] * c01 + e[2] * c02
    scale = jnp.where(valid, DAMPING / jnp.where(valid, determinant, 1.0), 0.0)
    inverse = sym_columns([c * scale for c in (c00, c01, c02, c11, c12, c22)])
    diag = sym_columns(e)
    upper_cols = [sym_columns([u[n : n + 1] for n in range(6)]) for u in uppers[1:]]
    rhs = last
    att = columns_apply(inverse, rhs)
    for _ in range(1, ITERS_ATT):
        applied = columns_apply(diag, att)
        for d in range(1, 4):
            applied = applied + columns_apply(upper_cols[d - 1], pltpu.roll(att, 128 - d, 1))
            applied = applied + pltpu.roll(columns_apply(upper_cols[d - 1], att), d, 1)
        att = att + columns_apply(inverse, rhs - applied)
    att_ref[...] = pltpu.roll(att, 128 - LEFT, 1)[0:3, 0:64]
    tables = [jnp.broadcast_to(att[j : j + 1], (8, 128)) for j in range(3)]

    def group(g, carry):
        slots = slots_ref.at[pl.ds(pl.multiple_of(g * 40, 8), 40), :]
        time8, d0, d1, d2 = [slots[pl.ds(k, 8, stride=5), :] for k in range(4)]
        direction = [d0, d1, d2]
        floor8, splines = spline_weights(time8)
        total = jnp.zeros((8, 128), jnp.float32)
        for m in range(4):
            at = floor8 + (LEFT - 1 + m)
            part = None
            for j in range(3):
                term = direction[j] * jnp.take_along_axis(tables[j], at, axis=1, mode="promise_in_bounds")
                part = term if part is None else part + term
            total = total + splines[m] * part
        corr_ref[pl.ds(pl.multiple_of(g * 8, 8), 8), :] = total
        return carry

    lax.fori_loop(0, 16, group, 0, unroll=8)


def finish_kernel(base_ref, scale_ref, returned_ref, att_ref, residual_far, att_far, residual_ref, sems):
    att_copy = pltpu.make_async_copy(att_ref, att_far, sems.at[0])
    att_copy.start()
    residual_ref[...] = base_ref[...] - scale_ref[...] * returned_ref[...]
    residual_copy = pltpu.make_async_copy(residual_ref, residual_far, sems.at[1])
    residual_copy.start()
    att_copy.wait()
    residual_copy.wait()


def call(kernel, outs, n_in, smem_at=(), scratch=(), far_in=(), far_out=()):
    shapes = [jax.ShapeDtypeStruct(s, jnp.float32) if i in far_out else pltpu.VMEM(s, jnp.float32) for i, s in enumerate(outs)]
    run = pl.pallas_call(
        kernel,
        out_shape=shapes,
        in_specs=[SMEM_SPEC if i in smem_at else VMEM_SPEC for i in range(n_in)],
        out_specs=[ANY_SPEC if i in far_out else VMEM_SPEC for i in range(len(shapes))],
        scratch_shapes=list(scratch),
    )

    def on_chip(*args):
        near = [a if i in smem_at or i in far_in else pltpu.with_memory_space_constraint(a, pltpu.VMEM) for i, a in enumerate(args)]
        return run(*near)

    return on_chip


def body(residual, obs_weight, time_frac, src_partials, att_dir, src_prior, att_prior, obs_source, obs_interval, obs_count):
    devices = lax.axis_size("src") * lax.axis_size("seg")
    square = lambda a: a.reshape(128, 128)
    res, weight, frac, src, interval = map(square, (residual, obs_weight, time_frac, obs_source, obs_interval))
    sums, live = call(
        source_sums_kernel,
        [(4, 320, 128), (128, 128)],
        5,
        (0,),
        [
            pltpu.VMEM((2, 320, 128), jnp.float32),
            pltpu.VMEM((SUMS_UNROLL, 40, 128), jnp.float32),
            pltpu.VMEM((SUMS_UNROLL, 320, 128), jnp.float32),
        ],
        range(1, 5),
    )(obs_count, res, weight, src_partials, src)
    gathered = lax.all_to_all(sums, "seg", split_axis=0, concat_axis=0, tiled=True)
    src_update, packed, base, scale = call(
        source_solve_kernel,
        [(5, 2048), (640, 128), (128, 128), (128, 128)],
        9,
        (),
        [
            pltpu.VMEM((5, 2048), jnp.float32),
            pltpu.VMEM((128, 128), jnp.float32),
            pltpu.VMEM((128, 128), jnp.float32),
            pltpu.SemaphoreType.DMA,
        ],
        (),
        (0,),
    )(gathered, src_prior, res, live, src_partials, src, frac, interval, att_dir)
    arrived = lax.all_to_all(packed.reshape(128, 1, 640), "src", split_axis=0, concat_axis=0, tiled=True).reshape(640, 128)
    (frame,) = call(
        band_sums_kernel,
        [(40, 128)],
        2,
        (),
        [
            pltpu.VMEM((BAND_UNROLL, 576, 128), jnp.float32),
            pltpu.VMEM((BAND_UNROLL, 8, 144, 128), jnp.bfloat16),
            pltpu.VMEM((144, 128), jnp.float32),
            pltpu.VMEM((8, 128), jnp.float32),
        ],
    )(arrived, att_prior)
    both = ("src", "seg")
    swaps = {}
    for start in (1, 0):
        pairs = [(i, i + 1) for i in range(start, devices - 1, 2)]
        swaps[start] = lax.ppermute(frame, both, pairs + [(b, a) for a, b in pairs])
    att_update, correction = call(
        functools.partial(attitude_kernel, knots_total=devices * 64), [(3, 64), (128, 128)], 4, (), ()
    )(frame, swaps[0], swaps[1], arrived)
    returned = lax.all_to_all(correction.reshape(128, 1, 128), "src", split_axis=0, concat_axis=0, tiled=True)
    residual_out, att_out = call(
        finish_kernel,
        [(128, 128), (3, 64)],
        4,
        (),
        [pltpu.VMEM((128, 128), jnp.float32), pltpu.SemaphoreType.DMA((2,))],
        (),
        (0, 1),
    )(base, scale, returned.reshape(128, 128), att_update)
    return src_update, att_out, residual_out.reshape(-1)


def solution(mesh):
    pair = ("src", "seg")
    in_specs = (
        P(pair), P(pair), P(pair), P(None, pair), P(None, pair), P(None, "src"), P(None, pair), P(pair), P(pair), P(pair, None),
    )
    out_specs = (P(None, "src"), P(None, pair), P(pair))
    return jax.shard_map(body, mesh=mesh, in_specs=in_specs, out_specs=out_specs, check_vma=False)
```

```python
import functools

import jax
import jax.numpy as jnp
from jax import lax
from jax.experimental import pallas as pl
from jax.experimental.pallas import tpu as pltpu
from jax.sharding import PartitionSpec as P


ITERS_ATT = 6
DAMPING = 0.5
LEFT = 20

param_pairs = [(i, j) for i in range(5) for j in range(i, 5)]
sym_pairs = [(0, 0), (0, 1), (0, 2), (1, 1), (1, 2), (2, 2)]
spline_pairs = [(m, m + d) for d in range(4) for m in range(4 - d)]

VMEM_SPEC = pl.BlockSpec(memory_space=pltpu.VMEM)
SMEM_SPEC = pl.BlockSpec(memory_space=pltpu.SMEM)
ANY_SPEC = pl.BlockSpec(memory_space=pl.ANY)
NT = (((1,), (1,)), ((), ()))
SUMS_UNROLL = 16
BAND_UNROLL = 16


def spline_weights(local_time):
    floor_part = jnp.floor(local_time)
    frac = local_time - floor_part
    square = frac * frac
    cube = square * frac
    rest = 1.0 - frac
    sixth = 1.0 / 6.0
    splines = [
        rest * rest * rest * sixth,
        (3.0 * cube - 6.0 * square + 4.0) * sixth,
        (-3.0 * cube + 3.0 * square + 3.0 * frac + 1.0) * sixth,
        cube * sixth,
    ]
    return floor_part.astype(jnp.int32), splines


def side_by_side(ref):
    return jnp.concatenate([ref[k] for k in range(8)], 1)


def hot_rows(ids, row):
    wide = jnp.broadcast_to(row, (16, 128)).astype(jnp.bfloat16)
    one, zero = jnp.ones((16, 128), jnp.bfloat16), jnp.zeros((16, 128), jnp.bfloat16)
    count = ids.shape[0] // 16
    return jnp.concatenate([jnp.where(ids[16 * n : 16 * n + 16] == wide, one, zero) for n in range(count)], 0)


def source_sums_kernel(
    count_ref, res_ref, weight_ref, part_ref, src_ref, out_ref, live_ref, acc_ref, rows_refs, feat_refs
):
    acc_ref[...] = jnp.zeros_like(acc_ref)
    ids = lax.broadcasted_iota(jnp.int32, (256, 128), 0).astype(jnp.float32).astype(jnp.bfloat16)
    lane8 = lax.broadcasted_iota(jnp.int32, (8, 128), 1)
    sub8 = lax.broadcasted_iota(jnp.int32, (8, 128), 0)
    sub16 = lax.broadcasted_iota(jnp.int32, (16, 128), 0)
    zero = jnp.zeros((16, 128), jnp.bfloat16)

    def group(g, feat_ref, rows_ref):
        first = pl.multiple_of(g * 8, 8)
        res8 = res_ref[pl.ds(first, 8), :]
        src8 = src_ref[pl.ds(first, 8), :]
        low8 = (src8 & 255).astype(jnp.float32)
        high8 = (src8 >> 8).astype(jnp.float32)
        count8 = jnp.zeros((8, 128), jnp.int32)
        for k in range(8):
            count8 = jnp.where(sub8 == k, count_ref[0, g * 8 + k], count8)
            rows_ref[pl.ds(k, 5, stride=8), :] = part_ref[:, pl.ds(pl.multiple_of((g * 8 + k) * 128, 128), 128)]
        weight8 = jnp.where(lane8 < count8, weight_ref[pl.ds(first, 8), :], 0.0)
        live_ref[pl.ds(first, 8), :] = weight8
        part8 = [rows_ref[p * 8 : p * 8 + 8, :] for p in range(5)]
        weighted = [weight8 * p for p in part8]
        features = [weighted[i] * part8[j] for i, j in param_pairs] + [weighted[i] * res8 for i in range(5)]
        for f, feature in enumerate(features):
            high = feature.astype(jnp.bfloat16).astype(jnp.float32)
            feat_ref[f * 8 : f * 8 + 8, :] = high
            feat_ref[160 + f * 8 : 168 + f * 8, :] = feature - high
        hots = []
        blocks = []
        for k in range(8):
            body = [feat_ref[pl.ds(128 * n + k, 16, stride=8), :].astype(jnp.bfloat16) for n in range(2)]
            tail = feat_ref[pl.ds(256 + k, 8, stride=8), :]
            tail = jnp.concatenate([tail, tail], 0).astype(jnp.bfloat16)
            high = jnp.broadcast_to(high8[k : k + 1], (16, 128)).astype(jnp.bfloat16)
            tiles = []
            for pair in range(4):
                for e in range(2):
                    mask = high == jnp.bfloat16(2 * pair + e)
                    tiles.append(jnp.where(mask, body[0], zero))
                    tiles.append(jnp.where(mask, body[1], zero))
                mixed = jnp.where(sub16 < 8, 2.0 * pair, 2.0 * pair + 1.0).astype(jnp.bfloat16)
                tiles.append(jnp.where(high == mixed, tail, zero))
            blocks.append(jnp.concatenate(tiles, 0))
            hots.append(hot_rows(ids, low8[k : k + 1]))
        sums = lax.dot_general(jnp.concatenate(blocks, 1), jnp.concatenate(hots, 1), NT, preferred_element_type=jnp.float32)
        for h in range(2):
            acc_ref[h] += sums[:, h * 128 : (h + 1) * 128]

    def groups(step, carry):
        for n in range(SUMS_UNROLL):
            group(step * SUMS_UNROLL + n, feat_refs.at[n], rows_refs.at[n])
        return carry

    lax.fori_loop(0, 16 // SUMS_UNROLL, groups, 0)

    def rows_of(q, e, h):
        at = 32 * e + q if q < 32 else 64 + 8 * e + q - 32
        return acc_ref[h, pl.ds(at, 4, stride=80), :]

    for f in range(20):
        for h in range(2):
            total = jnp.concatenate([rows_of(f, e, h) + rows_of(20 + f, e, h) for e in range(2)], 0)
            for q in range(4):
                out_ref[q, (h * 20 + f) * 8 : (h * 20 + f) * 8 + 8, :] = total


HIGH_ORDER = (0, 2, 4, 6, 1, 3, 5, 7)


def cholesky_solve5(normal, rhs_terms):
    matrix = {}
    for number, (i, j) in enumerate(param_pairs):
        matrix[i, j] = normal[number]
        matrix[j, i] = normal[number]
    factor = {}
    inverse_diag = []
    for row_at in range(5):
        for col_at in range(row_at + 1):
            running = matrix[row_at, col_at]
            for inner_k in range(col_at):
                running = running - factor[row_at, inner_k] * factor[col_at, inner_k]
            if row_at == col_at:
                factor[row_at, row_at] = jnp.sqrt(running)
                inverse_diag.append(1.0 / factor[row_at, row_at])
            else:
                factor[row_at, col_at] = running * inverse_diag[col_at]
    forward = []
    for row_at in range(5):
        running = rhs_terms[row_at]
        for inner_k in range(row_at):
            running = running - factor[row_at, inner_k] * forward[inner_k]
        forward.append(running * inverse_diag[row_at])
    backward = [None] * 5
    for row_at in reversed(range(5)):
        running = forward[row_at]
        for inner_k in range(row_at + 1, 5):
            running = running - factor[inner_k, row_at] * backward[inner_k]
        backward[row_at] = running * inverse_diag[row_at]
    return backward


def row_sums(tiles):
    sub = lax.broadcasted_iota(jnp.int32, (8, 128), 0)
    for width in (4, 2, 1):
        mask = (sub & width) == 0
        half = len(tiles) // 2
        folded = []
        for x, y in zip(tiles[:half], tiles[half:]):
            other = jnp.where(mask, y, x)
            if width == 4:
                moved = pltpu.roll(other, 4, 0)
            else:
                moved = jnp.where(mask, pltpu.roll(other, 8 - width, 0), pltpu.roll(other, width, 0))
            folded.append(jnp.where(mask, x, y) + moved)
        tiles = folded
    return tiles[0]


def source_solve_kernel(
    sums_ref, prior_ref, res_ref, live_ref, part_ref, src_ref, frac_ref, interval_ref, dir_ref,
    update_far, pack_ref, base_ref, scale_ref, update_ref, root_ref, corr_ref, sem,
):
    tables = []
    for h in range(2):
        terms = []
        for f in range(20):
            at = (h * 20 + f) * 8
            terms.append(
                (sums_ref[0, at : at + 8, :] + sums_ref[1, at : at + 8, :])
                + (sums_ref[2, at : at + 8, :] + sums_ref[3, at : at + 8, :])
            )
        for number, (i, j) in enumerate(param_pairs):
            if i == j:
                prior = [prior_ref[i : i + 1, (2 * r + h) * 128 : (2 * r + h + 1) * 128] for r in HIGH_ORDER]
                terms[number] = terms[number] + jnp.concatenate(prior, 0)
        solved = cholesky_solve5(terms[:15], terms[15:])
        tables.append(solved)
        for p in range(5):
            for n, r in enumerate(HIGH_ORDER):
                update_ref[p : p + 1, (2 * r + h) * 128 : (2 * r + h + 1) * 128] = solved[p][n : n + 1]
    update_copy = pltpu.make_async_copy(update_ref, update_far, sem)
    update_copy.start()
    root_ref[...] = jnp.sqrt(live_ref[...])
    sub8 = lax.broadcasted_iota(jnp.int32, (8, 128), 0)

    def group(g, carry):
        first = pl.multiple_of(g * 8, 8)
        res8 = res_ref[pl.ds(first, 8), :]
        src8 = src_ref[pl.ds(first, 8), :]
        root8 = root_ref[pl.ds(first, 8), :]
        time8 = (interval_ref[pl.ds(first, 8), :] & 63).astype(jnp.float32) + frac_ref[pl.ds(first, 8), :]
        low8 = src8 & 127
        high8 = src8 >> 8
        place8 = (high8 >> 1) + ((high8 & 1) << 2) + (((src8 >> 7) & 1) << 3)
        pack = pack_ref.at[pl.ds(pl.multiple_of(g * 40, 8), 40), :]
        tiles = []
        for k in range(8):
            at = pl.multiple_of((g * 8 + k) * 128, 128)
            low = jnp.broadcast_to(low8[k : k + 1], (8, 128))
            place = jnp.broadcast_to(place8[k : k + 1], (8, 128))
            part = part_ref[:, pl.ds(at, 128)]
            found = None
            masks = [place == sub8, place == sub8 + 8]
            for p in range(5):
                taken = [jnp.take_along_axis(tables[h][p], low, axis=1, mode="promise_in_bounds") for h in range(2)]
                picked = jnp.where(masks[0], taken[0], jnp.where(masks[1], taken[1], 0.0))
                term = picked * jnp.broadcast_to(part[p : p + 1], (8, 128))
                found = term if found is None else found + term
            tiles.append(found)
            pack[k * 5 + 1 : k * 5 + 4, :] = root8[k : k + 1] * dir_ref[:, pl.ds(at, 128)]
        corr8 = row_sums(tiles)
        corr_ref[pl.ds(first, 8), :] = corr8
        pack[pl.ds(0, 8, stride=5), :] = time8
        pack[pl.ds(4, 8, stride=5), :] = root8 * (res8 - corr8)
        return carry

    lax.fori_loop(0, 16, group, 0, unroll=8)
    live = root_ref[...] > 0.0
    base_ref[...] = res_ref[...] - jnp.where(live, corr_ref[...], 0.0)
    scale_ref[...] = jnp.where(live, 1.0 / jnp.where(live, root_ref[...], 1.0), 0.0)
    update_copy.wait()


def band_sums_kernel(slots_ref, prior_ref, frame_ref, feat_refs, a_refs, acc_ref, prior_pad):
    acc_ref[...] = jnp.zeros_like(acc_ref)
    ids = lax.broadcasted_iota(jnp.int32, (128, 128), 0).astype(jnp.float32).astype(jnp.bfloat16)

    def group(g, a_ref, feat_ref):
        slots = slots_ref.at[pl.ds(pl.multiple_of(g * 40, 8), 40), :]
        time8, d0, d1, d2, fp = [slots[pl.ds(k, 8, stride=5), :] for k in range(5)]
        direction = [d0, d1, d2]
        floor8 = jnp.floor(time8)
        _, splines = spline_weights(time8)
        outer = [direction[i] * direction[j] for i, j in sym_pairs]
        right = [direction[i] * fp for i in range(3)]
        at = 0
        for m, n in spline_pairs:
            coeff = splines[m] * splines[n]
            for entry in outer:
                feat_ref[at : at + 8, :] = coeff * entry
                at += 8
        for m in range(4):
            for entry in right:
                feat_ref[at : at + 8, :] = splines[m] * entry
                at += 8
        hots = []
        for k in range(8):
            for n in range(5):
                size = 16 if n < 4 else 8
                rows = feat_ref[pl.ds(128 * n + k, size, stride=8), :]
                high = rows.astype(jnp.bfloat16)
                rest = rows - high.astype(jnp.float32)
                if n < 4:
                    a_ref[k, 16 * n : 16 * n + 16, :] = high
                    a_ref[k, 64 + 16 * n : 80 + 16 * n, :] = rest.astype(jnp.bfloat16)
                else:
                    a_ref[k, 128:144, :] = jnp.concatenate([high.astype(jnp.float32), rest], 0).astype(jnp.bfloat16)
            hots.append(hot_rows(ids, floor8[k : k + 1]))
        acc_ref[...] += lax.dot_general(side_by_side(a_ref), jnp.concatenate(hots, 1), NT, preferred_element_type=jnp.float32)

    def groups(step, carry):
        for n in range(BAND_UNROLL):
            group(step * BAND_UNROLL + n, a_refs.at[n], feat_refs.at[n])
        return carry

    lax.fori_loop(0, 16 // BAND_UNROLL, groups, 0)
    prior_pad[...] = jnp.zeros_like(prior_pad)
    prior_pad[3:6, 0:64] = prior_ref[...]
    sums = jnp.concatenate([acc_ref[0:64, :] + acc_ref[64:128, :], acc_ref[128:136, :] + acc_ref[136:144, :]], 0)

    def tile(first, count, shift):
        rows = sums[first : first + count]
        return pltpu.roll(jnp.concatenate([rows, jnp.zeros((8 - count, 128), jnp.float32)], 0), shift, 1)

    for d in range(4):
        total = None
        for number, (m, n) in enumerate(spline_pairs):
            if n - m == d:
                term = tile(6 * number, 6, LEFT - 1 + m)
                total = term if total is None else total + term
        frame_ref[d * 8 : d * 8 + 8, :] = total
    total = pltpu.roll(prior_pad[...], LEFT, 1)
    for m in range(4):
        total = total + tile(60 + 3 * m, 3, LEFT - 1 + m)
    frame_ref[32:40, :] = total


def sym_columns(e):
    pad = [jnp.zeros((5, 128), jnp.float32)]
    return [
        jnp.concatenate([e[0], e[1], e[2]] + pad, 0),
        jnp.concatenate([e[1], e[3], e[4]] + pad, 0),
        jnp.concatenate([e[2], e[4], e[5]] + pad, 0),
    ]


def columns_apply(columns, vector):
    total = None
    for j in range(3):
        term = columns[j] * jnp.broadcast_to(vector[j : j + 1], (8, 128))
        total = term if total is None else total + term
    return total


def attitude_kernel(own_ref, even_ref, odd_ref, slots_ref, att_far, corr_ref, att_ref, sem, *, knots_total):
    place = lax.axis_index(("src", "seg"))
    lane = lax.broadcasted_iota(jnp.int32, (1, 128), 1)
    lane8 = lax.broadcasted_iota(jnp.int32, (8, 128), 1)
    is_even = place % 2 == 0
    knot = place * 64 + lane - LEFT
    valid = (knot >= 0) & (knot < knots_total)

    def frame(row):
        swap_first = even_ref[row : row + 8, :]
        swap_next = odd_ref[row : row + 8, :]
        left = jnp.where(is_even, swap_next, swap_first)
        right = jnp.where(is_even, swap_first, swap_next)
        return own_ref[row : row + 8, :] + pltpu.roll(jnp.where(lane8 < 64, right, left), 64, 1)

    uppers = [frame(8 * d) for d in range(4)]
    last = frame(32)
    e = [uppers[0][n : n + 1] for n in range(6)]
    e[0] = e[0] + last[3:4]
    e[3] = e[3] + last[4:5]
    e[5] = e[5] + last[5:6]
    c00 = e[3] * e[5] - e[4] * e[4]
    c01 = e[2] * e[4] - e[1] * e[5]
    c02 = e[1] * e[4] - e[2] * e[3]
    c11 = e[0] * e[5] - e[2] * e[2]
    c12 = e[1] * e[2] - e[0] * e[4]
    c22 = e[0] * e[3] - e[1] * e[1]
    determinant = e[0] * c00 + e[1] * c01 + e[2] * c02
    scale = jnp.where(valid, DAMPING / jnp.where(valid, determinant, 1.0), 0.0)
    inverse = sym_columns([c * scale for c in (c00, c01, c02, c11, c12, c22)])
    diag = sym_columns(e)
    upper_cols = [sym_columns([u[n : n + 1] for n in range(6)]) for u in uppers[1:]]
    rhs = last
    att = columns_apply(inverse, rhs)
    for _ in range(1, ITERS_ATT):
        applied = columns_apply(diag, att)
        for d in range(1, 4):
            applied = applied + columns_apply(upper_cols[d - 1], pltpu.roll(att, 128 - d, 1))
            applied = applied + pltpu.roll(columns_apply(upper_cols[d - 1], att), d, 1)
        att = att + columns_apply(inverse, rhs - applied)
    att_ref[...] = pltpu.roll(att, 128 - LEFT, 1)[0:3, 0:64]
    att_copy = pltpu.make_async_copy(att_ref, att_far, sem)
    att_copy.start()
    tables = [jnp.broadcast_to(att[j : j + 1], (8, 128)) for j in range(3)]

    def group(g, carry):
        slots = slots_ref.at[pl.ds(pl.multiple_of(g * 40, 8), 40), :]
        time8, d0, d1, d2 = [slots[pl.ds(k, 8, stride=5), :] for k in range(4)]
        direction = [d0, d1, d2]
        floor8, splines = spline_weights(time8)
        total = jnp.zeros((8, 128), jnp.float32)
        for m in range(4):
            at = floor8 + (LEFT - 1 + m)
            part = None
            for j in range(3):
                term = direction[j] * jnp.take_along_axis(tables[j], at, axis=1, mode="promise_in_bounds")
                part = term if part is None else part + term
            total = total + splines[m] * part
        corr_ref[pl.ds(pl.multiple_of(g * 8, 8), 8), :] = total
        return carry

    lax.fori_loop(0, 16, group, 0, unroll=8)
    att_copy.wait()


def call(kernel, outs, n_in, smem_at=(), scratch=(), far_in=(), far_out=()):
    shapes = [jax.ShapeDtypeStruct(s, jnp.float32) if i in far_out else pltpu.VMEM(s, jnp.float32) for i, s in enumerate(outs)]
    run = pl.pallas_call(
        kernel,
        out_shape=shapes,
        in_specs=[SMEM_SPEC if i in smem_at else VMEM_SPEC for i in range(n_in)],
        out_specs=[ANY_SPEC if i in far_out else VMEM_SPEC for i in range(len(shapes))],
        scratch_shapes=list(scratch),
    )

    def on_chip(*args):
        near = [a if i in smem_at or i in far_in else pltpu.with_memory_space_constraint(a, pltpu.VMEM) for i, a in enumerate(args)]
        return run(*near)

    return on_chip


def body(residual, obs_weight, time_frac, src_partials, att_dir, src_prior, att_prior, obs_source, obs_interval, obs_count):
    devices = lax.axis_size("src") * lax.axis_size("seg")
    square = lambda a: a.reshape(128, 128)
    res, weight, frac, src, interval = map(square, (residual, obs_weight, time_frac, obs_source, obs_interval))
    sums, live = call(
        source_sums_kernel,
        [(4, 320, 128), (128, 128)],
        5,
        (0,),
        [
            pltpu.VMEM((2, 320, 128), jnp.float32),
            pltpu.VMEM((SUMS_UNROLL, 40, 128), jnp.float32),
            pltpu.VMEM((SUMS_UNROLL, 320, 128), jnp.float32),
        ],
        range(1, 5),
    )(obs_count, res, weight, src_partials, src)
    gathered = lax.all_to_all(sums, "seg", split_axis=0, concat_axis=0, tiled=True)
    src_update, packed, base, scale = call(
        source_solve_kernel,
        [(5, 2048), (640, 128), (128, 128), (128, 128)],
        9,
        (),
        [
            pltpu.VMEM((5, 2048), jnp.float32),
            pltpu.VMEM((128, 128), jnp.float32),
            pltpu.VMEM((128, 128), jnp.float32),
            pltpu.SemaphoreType.DMA,
        ],
        (),
        (0,),
    )(gathered, src_prior, res, live, src_partials, src, frac, interval, att_dir)
    arrived = lax.all_to_all(packed.reshape(128, 1, 640), "src", split_axis=0, concat_axis=0, tiled=True).reshape(640, 128)
    (frame,) = call(
        band_sums_kernel,
        [(40, 128)],
        2,
        (),
        [
            pltpu.VMEM((BAND_UNROLL, 576, 128), jnp.float32),
            pltpu.VMEM((BAND_UNROLL, 8, 144, 128), jnp.bfloat16),
            pltpu.VMEM((144, 128), jnp.float32),
            pltpu.VMEM((8, 128), jnp.float32),
        ],
    )(arrived, att_prior)
    both = ("src", "seg")
    swaps = {}
    for start in (1, 0):
        pairs = [(i, i + 1) for i in range(start, devices - 1, 2)]
        swaps[start] = lax.ppermute(frame, both, pairs + [(b, a) for a, b in pairs])
    att_update, correction = call(
        functools.partial(attitude_kernel, knots_total=devices * 64),
        [(3, 64), (128, 128)],
        4,
        (),
        [pltpu.VMEM((3, 64), jnp.float32), pltpu.SemaphoreType.DMA],
        (),
        (0,),
    )(frame, swaps[0], swaps[1], arrived)
    returned = lax.all_to_all(correction.reshape(128, 1, 128), "src", split_axis=0, concat_axis=0, tiled=True)
    residual_out = base - scale * returned.reshape(128, 128)
    return src_update, att_update, residual_out.reshape(-1)


def solution(mesh):
    pair = ("src", "seg")
    in_specs = (
        P(pair), P(pair), P(pair), P(None, pair), P(None, pair), P(None, "src"), P(None, pair), P(pair), P(pair), P(pair, None),
    )
    out_specs = (P(None, "src"), P(None, pair), P(pair))
    return jax.shard_map(body, mesh=mesh, in_specs=in_specs, out_specs=out_specs, check_vma=False)
```
